32 devices in a mesh: groups: 2 (over y), ctx: 4 (over z), head: 2 (over x), rep: 2 (over core).
Axes of the slice: x: 2, y: 2, z: 4, core: 2. Of those that a mesh axis runs over, the one named last changes fastest.
Arguments:
- queries: bfloat16 [1024, 5120], P(('groups', 'ctx'), 'head'), parts along dimension 0, may hold values from -50 to 50
- key_vectors: bfloat16 [1024, 5120], P(('groups', 'ctx'), 'head'), parts along dimension 0, may hold values from -5 to 5
- values: bfloat16 [1024, 5120], P(('groups', 'ctx'), 'head'), parts along dimension 0, may hold values from -6 to 6
- learn_rates: float32 [8, 1024], P('head', ('groups', 'ctx')), parts along dimension 1, may hold values from 0.02 to 0.2
- fast_weights: float32 [16, 3, 640, 640], P(('groups', 'head'), None, ('ctx', 'rep')), parts along dimension 0, may hold values from -0.25 to 0.25
- momentum: float32 [16, 3, 640, 640], P(('groups', 'head'), None, ('ctx', 'rep')), parts along dimension 0, may hold values from -0.25 to 0.25
Outputs:
- layer_output: bfloat16 [1024, 5120], P(('groups', 'ctx'), ('head', 'rep')), parts along dimension 0
- fast_updated: float32 [16, 3, 640, 640], P(('groups', 'head'), None, ('ctx', 'rep')), parts along dimension 0
The draws below stay inside these ranges and needn't reach their ends.
There are 2 independent parts, one for each index of `groups`. The reference program is written for one: setup_inputs(seed, part) draws one part's arguments, and reference() takes and returns one part's arrays. A program takes and returns all parts, laid end to end along the dimension named above; each array names one. Nothing has to cross between parts.
All inputs are finite; a program needn't handle non-finite values.
Results may differ from the reference program's by a relative error of at most 0.038.
Values may be sent and summed in bfloat16 or wider, within the bound.
No kernel may reach another device: no remote copies, remote signals or barrier semaphores. Data moves between devices by JAX's collectives and lax.ppermute only.
A program may use at most 64 MiB of HBM per device.

```python
import math
import jax
import jax.numpy as jnp
from jax import lax

HEADS = 8
DH = 640
TOK_DEV = 128
TOKENS = 512
N_CTX = 4


def drawn_pair(key):
    key_keys = jax.random.fold_in(key, 101)
    key_queries = jax.random.fold_in(key, 202)
    base_keys = jnp.clip(jax.random.normal(key_keys, (TOKENS, HEADS * DH), jnp.float32), -5.0, 5.0)
    base_queries = jnp.clip(jax.random.normal(key_queries, (TOKENS, HEADS * DH), jnp.float32), -5.0, 5.0)
    return (base_queries, base_keys)


def draw_queries(key, part):
    return drawn_pair(key)[0].astype(jnp.bfloat16)


def draw_key_vectors(key, part):
    return drawn_pair(key)[1].astype(jnp.bfloat16)


def level_of(rng, dims, pieces, smallest, high):
    factor_of, own = 1.0, jax.random.fold_in(rng, 6)
    for axis_at, blocks in pieces:
        heights = jnp.exp(jax.random.uniform(jax.random.fold_in(own, axis_at), (blocks,), jnp.float32, smallest / len(pieces), high / len(pieces)))
        factor_of = factor_of * jnp.repeat(heights, dims[axis_at] // blocks).reshape([-1 if axis == axis_at else 1 for axis in range(len(dims))])
    return factor_of


def noise(rng, shape, spread, most, cuts=(), kind=jnp.bfloat16):
    result = jax.random.normal(rng, shape, jnp.float32) * spread
    if len(cuts) > 0:
        result = level_of(rng, shape, cuts, -0.22, 0.18) * result
    return jnp.clip(result, min=-most, max=most).astype(kind)


def setup_inputs(seed: int = 0, part: int = 0) -> dict:
    key_list = jax.random.split(jax.random.key(seed), 7)
    own_keys = jax.random.split(jax.random.fold_in(key_list[6], part), 7)
    return {
        "queries": draw_queries(jax.random.fold_in(jax.random.fold_in(key_list[6], part), 71), part),
        "key_vectors": draw_key_vectors(jax.random.fold_in(jax.random.fold_in(key_list[6], part), 71), part),
        "values": noise(own_keys[2], (TOKENS, HEADS * DH), 1.0, 6.0, ((0, 4), (1, 2))),
        "learn_rates": jnp.clip(jnp.exp(math.log(0.2) - 2.3025851 * jax.random.uniform(own_keys[3], (HEADS, TOKENS), jnp.float32) ** level_of(own_keys[3], (HEADS, TOKENS), ((0, 2), (1, 4)), -0.2, 0.2)), 0.02, 0.2),
        "fast_weights": noise(own_keys[4], (HEADS, 3, DH, DH), DH ** -0.5, 0.25, ((0, 2), (2, 8)), jnp.float32),
        "momentum": noise(own_keys[5], (HEADS, 3, DH, DH), DH ** -0.5, 0.25, ((0, 2), (2, 8)), jnp.float32),
    }


epsilon = 1e-06
momentum_decay = 0.9

def unit_rows(tensor):
    widened = tensor.astype(jnp.float32)
    factor = lax.rsqrt(lax.optimization_barrier(jnp.mean(widened * widened, axis=-1, keepdims=True)) + epsilon)
    return (widened * factor).astype(jnp.bfloat16)

def block_sum(left, right):
    left_blocks = left.reshape(N_CTX, TOK_DEV, -1).astype(jnp.float32)
    right_blocks = right.reshape(N_CTX, TOK_DEV, -1).astype(jnp.float32)
    partial_sums = jnp.einsum('btr,btd->brd', left_blocks, right_blocks)
    rounded = lax.optimization_barrier(partial_sums.astype(jnp.bfloat16))
    return lax.optimization_barrier(jnp.sum(rounded.astype(jnp.float32), axis=0))

def head_gradient(operands):
    key_head, cot_head, weights = operands
    gate = jnp.dot(key_head, weights[0].T, preferred_element_type=jnp.float32)
    upward = jnp.dot(key_head, weights[1].T, preferred_element_type=jnp.float32)
    back = jnp.dot(cot_head, weights[2].T, preferred_element_type=jnp.float32)
    sigma = jax.nn.sigmoid(gate)
    activated = jax.nn.silu(gate)
    hidden = (activated * upward).astype(jnp.bfloat16)
    gate_back = (back * upward * sigma * (1.0 + gate * (1.0 - sigma))).astype(jnp.bfloat16)
    up_back = (back * activated).astype(jnp.bfloat16)
    return jnp.stack([block_sum(gate_back, key_head), block_sum(up_back, key_head), block_sum(hidden, cot_head)])

def head_apply(operands):
    query_head, weights = operands
    gate = jnp.dot(query_head, weights[0].T, preferred_element_type=jnp.float32)
    upward = jnp.dot(query_head, weights[1].T, preferred_element_type=jnp.float32)
    hidden = (jax.nn.silu(gate) * upward).astype(jnp.bfloat16)
    return jnp.dot(hidden, weights[2], preferred_element_type=jnp.float32)

def head_attention(operands):
    query_head, key_head, value_head = operands
    query_blocks = query_head.reshape(N_CTX, TOK_DEV, DH).astype(jnp.float32)
    key_blocks = key_head.reshape(N_CTX, TOK_DEV, DH).astype(jnp.float32)
    value_blocks = value_head.reshape(N_CTX, TOK_DEV, DH).astype(jnp.float32)
    zero_block = jnp.zeros((1, TOK_DEV, DH), jnp.float32)
    key_window = jnp.concatenate([jnp.concatenate([zero_block, key_blocks[:-1]], axis=0), key_blocks], axis=1)
    value_window = jnp.concatenate([jnp.concatenate([zero_block, value_blocks[:-1]], axis=0), value_blocks], axis=1)
    scores = jnp.einsum('btd,bsd->bts', query_blocks, key_window) * DH ** (-0.5)
    block_index = jnp.arange(N_CTX)[:, None, None]
    position = jnp.arange(2 * TOK_DEV)[None, None, :]
    valid = jnp.logical_or(block_index > 0, position >= TOK_DEV)
    scores = jnp.where(valid, scores, -jnp.inf)
    peak = lax.optimization_barrier(jnp.max(scores, axis=-1, keepdims=True))
    weights = jnp.exp(scores - peak)
    probs = (weights / lax.optimization_barrier(jnp.sum(weights, axis=-1, keepdims=True))).astype(jnp.bfloat16)
    attended = jnp.einsum('bts,bsd->btd', probs.astype(jnp.float32), value_window)
    return attended.reshape(TOKENS, DH)

def reference(queries, key_vectors, values, learn_rates, fast_weights, momentum):
    query_heads = queries.reshape(TOKENS, HEADS, DH)
    key_heads = key_vectors.reshape(TOKENS, HEADS, DH)
    value_heads = values.reshape(TOKENS, HEADS, DH)
    query_unit = unit_rows(query_heads)
    key_unit = unit_rows(key_heads)
    token_scale = float(TOKENS) ** (-0.5)
    cotangent = (-(learn_rates.T[:, :, None] * token_scale) * value_heads.astype(jnp.float32)).astype(jnp.bfloat16)
    weights_low = fast_weights.astype(jnp.bfloat16)
    gradient = lax.map(head_gradient, (jnp.transpose(key_unit, (1, 0, 2)), jnp.transpose(cotangent, (1, 0, 2)), weights_low))
    fast_updated = fast_weights - (momentum_decay * momentum + gradient)
    new_low = fast_updated.astype(jnp.bfloat16)
    fast_out = lax.map(head_apply, (jnp.transpose(query_unit, (1, 0, 2)), new_low))
    attended = lax.map(head_attention, (jnp.transpose(query_heads, (1, 0, 2)), jnp.transpose(key_heads, (1, 0, 2)), jnp.transpose(value_heads, (1, 0, 2))))
    combined = jnp.transpose(attended + fast_out, (1, 0, 2))
    layer_output = combined.astype(jnp.bfloat16).reshape(TOKENS, HEADS * DH)
    return (layer_output, fast_updated)
```

```python
import functools

import jax
import jax.numpy as jnp
from jax import lax
from jax.experimental import pallas as pl
from jax.experimental.pallas import tpu as pltpu
from jax.sharding import PartitionSpec as P

epsilon = 1e-06
momentum_decay = 0.9
NT = (((1,), (1,)), ((), ()))


def passed_along(value, axis, steps):
    count = lax.axis_size(axis)
    initial, last = (max(0, -steps), min(count, count - steps))
    return lax.ppermute(value, axis, [(source, source + steps) for source in range(initial, last)])


def ring(value, axis, steps=1):
    count = lax.axis_size(axis)
    return lax.ppermute(value, axis, [(source, (source + steps) % count) for source in range(count)])


def unit_rows(tensor):
    widened = tensor.astype(jnp.float32)
    factor = lax.rsqrt(jnp.mean(widened * widened, axis=-1, keepdims=True) + epsilon)
    return (widened * factor).astype(jnp.bfloat16)


def swiglu_apply(inputs, weights):
    gate = jnp.einsum("thd,hrd->htr", inputs, weights[:, 0], preferred_element_type=jnp.float32)
    upward = jnp.einsum("thd,hrd->htr", inputs, weights[:, 1], preferred_element_type=jnp.float32)
    hidden = (jax.nn.silu(gate) * upward).astype(jnp.bfloat16)
    return jnp.einsum("htr,hrd->htd", hidden, weights[:, 2], preferred_element_type=jnp.float32)


def window_attention(query_own, key_own, value_own, key_prior, value_prior, first_block):
    tok_rows = query_own.shape[0]
    per_rep = query_own.shape[1]
    width = query_own.shape[2]
    block_rows = min(tok_rows, 512)
    block_count = tok_rows // block_rows
    key_window = jnp.concatenate([key_prior, key_own], axis=0)
    value_window = jnp.concatenate([value_prior, value_own], axis=0)
    score_scale = width ** (-0.5)
    position = jnp.arange(2 * tok_rows)
    valid = jnp.logical_or(position >= tok_rows, jnp.logical_not(first_block))
    query_blocks = query_own.reshape(block_count, block_rows, per_rep, width)

    def one_block(query_block):
        scores = (
            jnp.einsum("tad,sad->ats", query_block, key_window, preferred_element_type=jnp.float32)
            * score_scale
        )
        scores = jnp.where(valid[None, None, :], scores, -jnp.inf)
        peak = jnp.max(scores, axis=-1, keepdims=True)
        weights = jnp.exp(scores - peak)
        probs = (weights / jnp.sum(weights, axis=-1, keepdims=True)).astype(jnp.bfloat16)
        return jnp.einsum("ats,sad->tad", probs, value_window, preferred_element_type=jnp.float32)

    return lax.map(one_block, query_blocks).reshape(tok_rows, per_rep, width)


def weights_travel(queries, key_vectors, values, learn_rates, fast_weights, momentum):
    tok_rows = queries.shape[0]
    head_count = fast_weights.shape[0]
    width = fast_weights.shape[3]
    rep_count = lax.axis_size("rep")
    per_rep = head_count // rep_count
    rep_index = lax.axis_index("rep")
    ctx_index = lax.axis_index("ctx")
    total_tokens = tok_rows * lax.axis_size("ctx")
    query_heads = queries.reshape(tok_rows, head_count, width)
    key_heads = key_vectors.reshape(tok_rows, head_count, width)
    value_heads = values.reshape(tok_rows, head_count, width)
    query_unit = unit_rows(query_heads)
    key_unit = unit_rows(key_heads)
    token_scale = float(total_tokens) ** (-0.5)
    cotangent = (
        -(learn_rates.T[:, :, None] * token_scale) * value_heads.astype(jnp.float32)
    ).astype(jnp.bfloat16)
    weight_rows = lax.all_gather(fast_weights.astype(jnp.bfloat16), "ctx", axis=2, tiled=True)
    gate = jnp.einsum(
        "thd,hrd->htr", key_unit, weight_rows[:, 0], preferred_element_type=jnp.float32
    )
    upward = jnp.einsum(
        "thd,hrd->htr", key_unit, weight_rows[:, 1], preferred_element_type=jnp.float32
    )
    back = jnp.einsum(
        "thd,hrd->htr", cotangent, weight_rows[:, 2], preferred_element_type=jnp.float32
    )
    sigma = jax.nn.sigmoid(gate)
    activated = jax.nn.silu(gate)
    hidden = (activated * upward).astype(jnp.bfloat16)
    gate_back = (back * upward * sigma * (1.0 + gate * (1.0 - sigma))).astype(jnp.bfloat16)
    up_back = (back * activated).astype(jnp.bfloat16)
    grad_gate = jnp.einsum("htr,thd->hrd", gate_back, key_unit, preferred_element_type=jnp.float32)
    grad_up = jnp.einsum("htr,thd->hrd", up_back, key_unit, preferred_element_type=jnp.float32)
    grad_down = jnp.einsum("htr,thd->hrd", hidden, cotangent, preferred_element_type=jnp.float32)
    gradient = jnp.stack([grad_gate, grad_up, grad_down], axis=1)
    share = lax.psum_scatter(
        gradient.astype(jnp.bfloat16), "ctx", scatter_dimension=2, tiled=True
    ).astype(jnp.float32)
    fast_updated = fast_weights - (momentum_decay * momentum + share)
    new_rows = lax.all_gather(fast_updated.astype(jnp.bfloat16), "ctx", axis=2, tiled=True)
    own_start = rep_index * per_rep
    partial_out = swiglu_apply(query_unit, new_rows)
    traded = lax.all_to_all(
        partial_out.astype(jnp.bfloat16), "rep", split_axis=0, concat_axis=0, tiled=True
    ).astype(partial_out.dtype)
    fast_out = jnp.sum(traded.reshape(rep_count, per_rep, tok_rows, width), axis=0)
    attend_query = lax.dynamic_slice_in_dim(query_heads, own_start, per_rep, 1)
    attend_key = lax.dynamic_slice_in_dim(key_heads, own_start, per_rep, 1)
    attend_value = lax.dynamic_slice_in_dim(value_heads, own_start, per_rep, 1)
    key_prior, value_prior = passed_along((attend_key, attend_value), "ctx", 1)
    attended = window_attention(
        attend_query, attend_key, attend_value, key_prior, value_prior, ctx_index == 0
    )
    combined = attended + jnp.transpose(fast_out, (1, 0, 2))
    layer_output = combined.astype(jnp.bfloat16).reshape(tok_rows, per_rep * width)
    return (layer_output, fast_updated)


def gradient_body(slots, token_scale, *refs):
    keys, vals, rates = refs[:slots], refs[slots : 2 * slots], refs[2 * slots : 3 * slots]
    low_own, low_par, base_own, base_par, new_own, new_par, new_low, unit, value, low = refs[3 * slots :]
    rows = keys[0].shape[0]
    hid = low_own.shape[2]
    for s in range(slots):
        here = pl.ds(s * rows, rows)
        unit[here, :] = unit_rows(keys[s][...])
        value[here, :] = vals[s][...]
    for m in range(3):
        low[pl.ds(2 * m * hid, hid), :] = low_own[0, m]
        low[pl.ds((2 * m + 1) * hid, hid), :] = low_par[0, m]
    rate = -(jnp.concatenate([r[0] for r in rates], axis=-1) * token_scale)
    fed = lax.dot_general(low[: 4 * hid, :], unit[...], NT, preferred_element_type=jnp.float32)
    gate, upward = fed[: 2 * hid], fed[2 * hid :]
    back = lax.dot_general(low[4 * hid :, :], value[...], NT, preferred_element_type=jnp.float32) * rate
    sigma = jax.nn.sigmoid(gate)
    activated = gate * sigma
    hidden = (activated * upward * rate).astype(jnp.bfloat16)
    gate_back = (back * upward * sigma * (1.0 + gate * (1.0 - sigma))).astype(jnp.bfloat16)
    up_back = (back * activated).astype(jnp.bfloat16)
    for m, (left, right) in enumerate(((gate_back, unit), (up_back, unit), (hidden, value))):
        grad = jnp.dot(left, right[...], preferred_element_type=jnp.float32)
        fresh_own = base_own[0, m] - grad[:hid]
        fresh_par = base_par[0, m] - grad[hid:]
        new_own[0, m] = fresh_own
        new_par[0, m] = fresh_par
        new_low[0, pl.ds(2 * m * hid, hid), :] = fresh_own.astype(jnp.bfloat16)
        new_low[0, pl.ds((2 * m + 1) * hid, hid), :] = fresh_par.astype(jnp.bfloat16)


def gradient_step(keys, vals, rates, low_own, low_par, base_own, base_par):
    slots = len(keys)
    rows = keys[0].shape[0]
    heads, _, hid, width = low_own.shape
    token_scale = float(slots * rows) ** (-0.5)
    token_spec = pl.BlockSpec((rows, width), lambda h: (0, h))
    rate_spec = pl.BlockSpec((1, 1, rows), lambda h: (h, 0, 0))
    weight_spec = pl.BlockSpec((1, 3, hid, width), lambda h: (h, 0, 0, 0))
    low_spec = pl.BlockSpec((1, 6 * hid, width), lambda h: (h, 0, 0))
    whole = jax.ShapeDtypeStruct(low_own.shape, jnp.float32)
    work = heads * slots * rows * hid * width
    return pl.pallas_call(
        functools.partial(gradient_body, slots, token_scale),
        out_shape=(whole, whole, jax.ShapeDtypeStruct((heads, 6 * hid, width), jnp.bfloat16)),
        grid=(heads,),
        in_specs=[token_spec] * (2 * slots) + [rate_spec] * slots + [weight_spec] * 4,
        out_specs=(weight_spec, weight_spec, low_spec),
        scratch_shapes=[
            pltpu.VMEM((slots * rows, width), jnp.bfloat16),
            pltpu.VMEM((slots * rows, width), jnp.bfloat16),
            pltpu.VMEM((6 * hid, width), jnp.bfloat16),
        ],
        cost_estimate=pl.CostEstimate(
            flops=24 * work, bytes_accessed=36 * heads * hid * width, transcendentals=0
        ),
        name="gradient_step",
    )(*keys, *vals, *rates, low_own, low_par, base_own, base_par)


def apply_body(query, low, *refs):
    out = refs[-1]
    width = low.shape[2]
    hid = low.shape[1] // 6
    for h in range(low.shape[0]):
        columns = slice(h * width, (h + 1) * width)
        unit = unit_rows(query[:, columns])
        gate = lax.dot_general(unit, low[h, : 2 * hid, :], NT, preferred_element_type=jnp.float32)
        upward = lax.dot_general(
            unit, low[h, 2 * hid : 4 * hid, :], NT, preferred_element_type=jnp.float32
        )
        hidden = (gate * jax.nn.sigmoid(gate) * upward).astype(jnp.bfloat16)
        made = jnp.dot(hidden, low[h, 4 * hid :, :], preferred_element_type=jnp.float32)
        if len(refs) > 1:
            made = made + refs[0][:, columns]
        out[:, columns] = made.astype(out.dtype)


def apply_step(query, low, dtype, *more):
    heads, total, width = low.shape
    return pl.pallas_call(
        apply_body,
        out_shape=jax.ShapeDtypeStruct(query.shape, dtype),
        cost_estimate=pl.CostEstimate(
            flops=2 * query.shape[0] * heads * total * width,
            bytes_accessed=2 * heads * total * width,
            transcendentals=0,
        ),
        name="apply_step",
    )(query, low, *more)


def attend_body(width, first, query, key_own, key_prior, value_own, value_prior, out):
    rows = query.shape[0]
    heads = query.shape[1] // width
    allowed = jnp.where(first[0] != 0, -jnp.inf, 0.0).astype(jnp.float32)
    for h in range(heads):
        columns = slice(h * width, (h + 1) * width)
        part = query[:, columns]
        near = lax.dot_general(part, key_own[:, columns], NT, preferred_element_type=jnp.float32)
        far = lax.dot_general(part, key_prior[:, columns], NT, preferred_element_type=jnp.float32)
        near = near * width ** (-0.5)
        far = far * width ** (-0.5) + allowed
        peak = jnp.maximum(
            jnp.max(near, axis=-1, keepdims=True), jnp.max(far, axis=-1, keepdims=True)
        )
        near = jnp.exp(near - peak)
        far = jnp.exp(far - peak)
        total = jnp.sum(near, axis=-1, keepdims=True) + jnp.sum(far, axis=-1, keepdims=True)
        near = (near / total).astype(jnp.bfloat16)
        far = (far / total).astype(jnp.bfloat16)
        out[:, columns] = jnp.dot(
            near, value_own[:, columns], preferred_element_type=jnp.float32
        ) + jnp.dot(far, value_prior[:, columns], preferred_element_type=jnp.float32)


def attend_step(width, first, query, key_own, key_prior, value_own, value_prior):
    in_vmem = pl.BlockSpec(memory_space=pltpu.VMEM)
    rows, columns = query.shape
    return pl.pallas_call(
        functools.partial(attend_body, width),
        out_shape=jax.ShapeDtypeStruct(query.shape, jnp.float32),
        in_specs=[pl.BlockSpec(memory_space=pltpu.SMEM)] + [in_vmem] * 5,
        out_specs=in_vmem,
        cost_estimate=pl.CostEstimate(
            flops=8 * rows * rows * columns, bytes_accessed=14 * rows * columns, transcendentals=0
        ),
        name="attend_step",
    )(first, query, key_own, key_prior, value_own, value_prior)


def tokens_travel(queries, key_vectors, values, learn_rates, fast_weights, momentum):
    head_count = fast_weights.shape[0]
    width = fast_weights.shape[3]
    slots = lax.axis_size("ctx")
    per_rep = head_count // 2
    rep_index = lax.axis_index("rep")
    start = rep_index * per_rep
    away = per_rep - start

    def own_columns(tensor):
        return lax.dynamic_slice_in_dim(tensor, start * width, per_rep * width, 1)

    def own(tensor):
        return lax.dynamic_slice_in_dim(tensor, start, per_rep, 0)

    def other(tensor):
        return lax.dynamic_slice_in_dim(tensor, away, per_rep, 0)

    keys, vals, asked = [own_columns(key_vectors)], [own_columns(values)], [own_columns(queries)]
    rates = [own(learn_rates)[:, None, :]]
    for step in range(1, slots):
        keys.append(ring(keys[-1], "ctx"))
        vals.append(ring(vals[-1], "ctx"))
        rates.append(ring(rates[0], "ctx", step))
    base = fast_weights - momentum_decay * momentum
    low = fast_weights.astype(jnp.bfloat16)
    low_par = ring(other(low), "rep")
    base_par = ring(other(base), "rep")
    for step in range(1, slots):
        asked.append(ring(asked[-1], "ctx"))
    first = (lax.axis_index("ctx") == 0).astype(jnp.int32).reshape(1)
    attended = attend_step(width, first, asked[0], keys[0], keys[1], vals[0], vals[1])
    new_own, new_par, new_low = gradient_step(
        keys, vals, rates, own(low), low_par, own(base), base_par
    )
    moving = None
    for step in range(1, slots):
        if moving is None:
            made = apply_step(asked[step], new_low, jnp.bfloat16)
        else:
            made = apply_step(asked[step], new_low, jnp.float32)
            made = (made + moving.astype(jnp.float32)).astype(jnp.bfloat16)
        moving = ring(made, "ctx")
    kept = apply_step(asked[0], new_low, jnp.float32, attended)
    layer_output = (kept + moving.astype(jnp.float32)).astype(jnp.bfloat16)
    returned = ring(new_par, "rep")
    fast_updated = jnp.where(
        rep_index == 0,
        jnp.concatenate([new_own, returned], axis=0),
        jnp.concatenate([returned, new_own], axis=0),
    )
    return (layer_output, fast_updated)


def on_device(queries, key_vectors, values, learn_rates, fast_weights, momentum):
    slots = lax.axis_size("ctx")
    fits = (
        lax.axis_size("rep") == 2
        and 2 <= slots <= 8
        and fast_weights.shape[0] % 2 == 0
        and fast_weights.shape[2] % 16 == 0
        and queries.shape[0] == 128
    )
    program = tokens_travel if fits else weights_travel
    return program(queries, key_vectors, values, learn_rates, fast_weights, momentum)


def solution(mesh):
    return jax.shard_map(
        on_device,
        mesh=mesh,
        in_specs=(
            P(("groups", "ctx"), "head"),
            P(("groups", "ctx"), "head"),
            P(("groups", "ctx"), "head"),
            P("head", ("groups", "ctx")),
            P(("groups", "head"), None, ("ctx", "rep"), None),
            P(("groups", "head"), None, ("ctx", "rep"), None),
        ),
        out_specs=(
            P(("groups", "ctx"), ("head", "rep")),
            P(("groups", "head"), None, ("ctx", "rep"), None),
        ),
        check_vma=False,
    )
```

```python
import functools

import jax
import jax.numpy as jnp
from jax import lax
from jax.experimental import pallas as pl
from jax.experimental.pallas import tpu as pltpu
from jax.sharding import PartitionSpec as P


epsilon = 1e-06
momentum_decay = 0.9
NT = (((1,), (1,)), ((), ()))


def passed_along(value, axis, steps):
    count = lax.axis_size(axis)
    initial, last = (max(0, -steps), min(count, count - steps))
    return lax.ppermute(value, axis, [(source, source + steps) for source in range(initial, last)])


def ring(value, axis, steps=1):
    count = lax.axis_size(axis)
    return lax.ppermute(value, axis, [(source, (source + steps) % count) for source in range(count)])


def unit_rows(tensor):
    widened = tensor.astype(jnp.float32)
    factor = lax.rsqrt(jnp.mean(widened * widened, axis=-1, keepdims=True) + epsilon)
    return (widened * factor).astype(jnp.bfloat16)


def swiglu_apply(inputs, weights):
    gate = jnp.einsum("thd,hrd->htr", inputs, weights[:, 0], preferred_element_type=jnp.float32)
    upward = jnp.einsum("thd,hrd->htr", inputs, weights[:, 1], preferred_element_type=jnp.float32)
    hidden = (jax.nn.silu(gate) * upward).astype(jnp.bfloat16)
    return jnp.einsum("htr,hrd->htd", hidden, weights[:, 2], preferred_element_type=jnp.float32)


def window_attention(query_own, key_own, value_own, key_prior, value_prior, first_block):
    tok_rows = query_own.shape[0]
    per_rep = query_own.shape[1]
    width = query_own.shape[2]
    block_rows = min(tok_rows, 512)
    block_count = tok_rows // block_rows
    key_window = jnp.concatenate([key_prior, key_own], axis=0)
    value_window = jnp.concatenate([value_prior, value_own], axis=0)
    score_scale = width ** (-0.5)
    position = jnp.arange(2 * tok_rows)
    valid = jnp.logical_or(position >= tok_rows, jnp.logical_not(first_block))
    query_blocks = query_own.reshape(block_count, block_rows, per_rep, width)

    def one_block(query_block):
        scores = (
            jnp.einsum("tad,sad->ats", query_block, key_window, preferred_element_type=jnp.float32)
            * score_scale
        )
        scores = jnp.where(valid[None, None, :], scores, -jnp.inf)
        peak = jnp.max(scores, axis=-1, keepdims=True)
        weights = jnp.exp(scores - peak)
        probs = (weights / jnp.sum(weights, axis=-1, keepdims=True)).astype(jnp.bfloat16)
        return jnp.einsum("ats,sad->tad", probs, value_window, preferred_element_type=jnp.float32)

    return lax.map(one_block, query_blocks).reshape(tok_rows, per_rep, width)


def weights_travel(queries, key_vectors, values, learn_rates, fast_weights, momentum):
    tok_rows = queries.shape[0]
    head_count = fast_weights.shape[0]
    width = fast_weights.shape[3]
    rep_count = lax.axis_size("rep")
    per_rep = head_count // rep_count
    rep_index = lax.axis_index("rep")
    ctx_index = lax.axis_index("ctx")
    total_tokens = tok_rows * lax.axis_size("ctx")
    query_heads = queries.reshape(tok_rows, head_count, width)
    key_heads = key_vectors.reshape(tok_rows, head_count, width)
    value_heads = values.reshape(tok_rows, head_count, width)
    query_unit = unit_rows(query_heads)
    key_unit = unit_rows(key_heads)
    token_scale = float(total_tokens) ** (-0.5)
    cotangent = (
        -(learn_rates.T[:, :, None] * token_scale) * value_heads.astype(jnp.float32)
    ).astype(jnp.bfloat16)
    weight_rows = lax.all_gather(fast_weights.astype(jnp.bfloat16), "ctx", axis=2, tiled=True)
    gate = jnp.einsum(
        "thd,hrd->htr", key_unit, weight_rows[:, 0], preferred_element_type=jnp.float32
    )
    upward = jnp.einsum(
        "thd,hrd->htr", key_unit, weight_rows[:, 1], preferred_element_type=jnp.float32
    )
    back = jnp.einsum(
        "thd,hrd->htr", cotangent, weight_rows[:, 2], preferred_element_type=jnp.float32
    )
    sigma = jax.nn.sigmoid(gate)
    activated = jax.nn.silu(gate)
    hidden = (activated * upward).astype(jnp.bfloat16)
    gate_back = (back * upward * sigma * (1.0 + gate * (1.0 - sigma))).astype(jnp.bfloat16)
    up_back = (back * activated).astype(jnp.bfloat16)
    grad_gate = jnp.einsum("htr,thd->hrd", gate_back, key_unit, preferred_element_type=jnp.float32)
    grad_up = jnp.einsum("htr,thd->hrd", up_back, key_unit, preferred_element_type=jnp.float32)
    grad_down = jnp.einsum("htr,thd->hrd", hidden, cotangent, preferred_element_type=jnp.float32)
    gradient = jnp.stack([grad_gate, grad_up, grad_down], axis=1)
    share = lax.psum_scatter(
        gradient.astype(jnp.bfloat16), "ctx", scatter_dimension=2, tiled=True
    ).astype(jnp.float32)
    fast_updated = fast_weights - (momentum_decay * momentum + share)
    new_rows = lax.all_gather(fast_updated.astype(jnp.bfloat16), "ctx", axis=2, tiled=True)
    own_start = rep_index * per_rep
    partial_out = swiglu_apply(query_unit, new_rows)
    traded = lax.all_to_all(
        partial_out.astype(jnp.bfloat16), "rep", split_axis=0, concat_axis=0, tiled=True
    ).astype(partial_out.dtype)
    fast_out = jnp.sum(traded.reshape(rep_count, per_rep, tok_rows, width), axis=0)
    attend_query = lax.dynamic_slice_in_dim(query_heads, own_start, per_rep, 1)
    attend_key = lax.dynamic_slice_in_dim(key_heads, own_start, per_rep, 1)
    attend_value = lax.dynamic_slice_in_dim(value_heads, own_start, per_rep, 1)
    key_prior, value_prior = passed_along((attend_key, attend_value), "ctx", 1)
    attended = window_attention(
        attend_query, attend_key, attend_value, key_prior, value_prior, ctx_index == 0
    )
    combined = attended + jnp.transpose(fast_out, (1, 0, 2))
    layer_output = combined.astype(jnp.bfloat16).reshape(tok_rows, per_rep * width)
    return (layer_output, fast_updated)


def cotangent_body(token_scale, rep, values, rates, out_raw, out):
    heads = rates.shape[0] // 2
    rows, columns = out.shape
    width = columns // heads
    for h in range(heads):
        rate = -(rates[pl.ds(rep[0] * heads + h, 1), :] * token_scale)
        rate = jnp.transpose(jnp.broadcast_to(rate, (rows, rows)))[:, :1]
        part = values[:, h * width : (h + 1) * width]
        out_raw[:, h * width : (h + 1) * width] = part
        out[:, h * width : (h + 1) * width] = (rate * part.astype(jnp.float32)).astype(jnp.bfloat16)


def cotangent_step(token_scale, rep, values, rates):
    rows, columns = values.shape[0], values.shape[1] // 2
    made = jax.ShapeDtypeStruct((rows, columns), jnp.bfloat16)
    whole = pl.BlockSpec((rows, columns), lambda i, rep: (0, 0))
    return pl.pallas_call(
        functools.partial(cotangent_body, token_scale),
        out_shape=(made, made),
        grid_spec=pltpu.PrefetchScalarGridSpec(
            num_scalar_prefetch=1,
            grid=(1,),
            in_specs=[
                pl.BlockSpec((rows, columns), lambda i, rep: (0, rep[0])),
                pl.BlockSpec(rates.shape, lambda i, rep: (0, 0)),
            ],
            out_specs=(whole, whole),
        ),
        compiler_params=pltpu.CompilerParams(vmem_limit_bytes=8 << 20),
        cost_estimate=pl.CostEstimate(
            flops=2 * rows * columns, bytes_accessed=6 * rows * columns, transcendentals=0
        ),
        name="cotangent_step",
    )(rep, values, rates)


def gradient_body(slots, *refs):
    keys, cots = refs[:slots], refs[slots : 2 * slots]
    low_own, low_par, base_own, base_par, new_own, new_par, new_low, unit, cot, low = refs[2 * slots :]
    rows = keys[0].shape[0]
    hid = low_own.shape[2]
    for s in range(slots):
        here = pl.ds(s * rows, rows)
        unit[here, :] = unit_rows(keys[s][...])
        cot[here, :] = cots[s][...]
    for m in range(3):
        low[pl.ds(2 * m * hid, hid), :] = low_own[0, m]
        low[pl.ds((2 * m + 1) * hid, hid), :] = low_par[0, m]
    fed = lax.dot_general(low[: 4 * hid, :], unit[...], NT, preferred_element_type=jnp.float32)
    gate, upward = fed[: 2 * hid], fed[2 * hid :]
    back = lax.dot_general(low[4 * hid :, :], cot[...], NT, preferred_element_type=jnp.float32)
    sigma = jax.nn.sigmoid(gate)
    activated = gate * sigma
    hidden = (activated * upward).astype(jnp.bfloat16)
    gate_back = (back * upward * sigma * (1.0 + gate * (1.0 - sigma))).astype(jnp.bfloat16)
    up_back = (back * activated).astype(jnp.bfloat16)
    for m, (left, right) in enumerate(((gate_back, unit), (up_back, unit), (hidden, cot))):
        grad = jnp.dot(left, right[...], preferred_element_type=jnp.float32)
        fresh_own = base_own[0, m] - grad[:hid]
        fresh_par = base_par[0, m] - grad[hid:]
        new_own[0, m] = fresh_own
        new_par[0, m] = fresh_par
        new_low[0, pl.ds(2 * m * hid, hid), :] = fresh_own.astype(jnp.bfloat16)
        new_low[0, pl.ds((2 * m + 1) * hid, hid), :] = fresh_par.astype(jnp.bfloat16)


def gradient_step(keys, cots, low_own, low_par, base_own, base_par):
    slots = len(keys)
    rows = keys[0].shape[0]
    heads, _, hid, width = low_own.shape
    token_spec = pl.BlockSpec((rows, width), lambda h: (0, h))
    weight_spec = pl.BlockSpec((1, 3, hid, width), lambda h: (h, 0, 0, 0))
    low_spec = pl.BlockSpec((1, 6 * hid, width), lambda h: (h, 0, 0))
    fresh = pltpu.HBM(low_own.shape, jnp.float32)
    return pl.pallas_call(
        functools.partial(gradient_body, slots),
        out_shape=(fresh, fresh, jax.ShapeDtypeStruct((heads, 6 * hid, width), jnp.bfloat16)),
        grid=(heads,),
        in_specs=[token_spec] * (2 * slots) + [weight_spec] * 4,
        out_specs=(weight_spec, weight_spec, low_spec),
        scratch_shapes=[
            pltpu.VMEM((slots * rows, width), jnp.bfloat16),
            pltpu.VMEM((slots * rows, width), jnp.bfloat16),
            pltpu.VMEM((6 * hid, width), jnp.bfloat16),
        ],
        compiler_params=pltpu.CompilerParams(vmem_limit_bytes=24 << 20),
        cost_estimate=pl.CostEstimate(
            flops=24 * heads * slots * rows * hid * width,
            bytes_accessed=48 * heads * hid * width,
            transcendentals=0,
        ),
        name="gradient_step",
    )(*keys, *cots, low_own, low_par, base_own, base_par)


def apply_body(query, low, *refs):
    heads, total, width = low.shape
    more, outs = refs[:-heads], refs[-heads:]
    hid = total // 6
    for h in range(heads):
        columns = slice(h * width, (h + 1) * width)
        unit = unit_rows(query[:, columns])
        gate = lax.dot_general(unit, low[h, : 2 * hid, :], NT, preferred_element_type=jnp.float32)
        upward = lax.dot_general(
            unit, low[h, 2 * hid : 4 * hid, :], NT, preferred_element_type=jnp.float32
        )
        hidden = (gate * jax.nn.sigmoid(gate) * upward).astype(jnp.bfloat16)
        made = jnp.dot(hidden, low[h, 4 * hid :, :], preferred_element_type=jnp.float32)
        if more:
            made = made + more[0][:, columns]
        outs[h][...] = made.astype(outs[h].dtype)


def apply_step(query, low, dtype, *more):
    heads, total, width = low.shape
    rows = query.shape[0]
    return pl.pallas_call(
        apply_body,
        out_shape=tuple(jax.ShapeDtypeStruct((rows, width), dtype) for _ in range(heads)),
        compiler_params=pltpu.CompilerParams(vmem_limit_bytes=8 << 20),
        cost_estimate=pl.CostEstimate(
            flops=2 * rows * heads * total * width,
            bytes_accessed=2 * heads * total * width,
            transcendentals=0,
        ),
        name="apply_step",
    )(query, low, *more)


def attend_body(heads, token_scale, first, query, key_own, key_prior, value_own, cot_prior, rate_prior, out):
    width = query.shape[1] // heads
    allowed = jnp.where(first[0] != 0, -jnp.inf, 0.0).astype(jnp.float32)
    for h in range(heads):
        columns = slice(h * width, (h + 1) * width)
        part = query[:, columns]
        near = lax.dot_general(part, key_own[:, columns], NT, preferred_element_type=jnp.float32)
        far = lax.dot_general(part, key_prior[:, columns], NT, preferred_element_type=jnp.float32)
        near = near * width ** (-0.5)
        far = far * width ** (-0.5) + allowed
        peak = jnp.maximum(
            jnp.max(near, axis=-1, keepdims=True), jnp.max(far, axis=-1, keepdims=True)
        )
        near = jnp.exp(near - peak)
        far = jnp.exp(far - peak)
        total = jnp.sum(near, axis=-1, keepdims=True) + jnp.sum(far, axis=-1, keepdims=True)
        rate = -(rate_prior[h] * token_scale)
        near = (near / total).astype(jnp.bfloat16)
        far = (far / total / rate).astype(jnp.bfloat16)
        out[:, columns] = jnp.dot(
            near, value_own[:, columns], preferred_element_type=jnp.float32
        ) + jnp.dot(far, cot_prior[:, columns], preferred_element_type=jnp.float32)


def attend_step(token_scale, first, query, key_own, key_prior, value_own, cot_prior, rate_prior):
    rows, columns = query.shape
    return pl.pallas_call(
        functools.partial(attend_body, rate_prior.shape[0], token_scale),
        out_shape=jax.ShapeDtypeStruct(query.shape, jnp.float32),
        in_specs=[pl.BlockSpec(memory_space=pltpu.SMEM)] + [pl.BlockSpec()] * 6,
        out_specs=pl.BlockSpec(),
        compiler_params=pltpu.CompilerParams(vmem_limit_bytes=8 << 20),
        cost_estimate=pl.CostEstimate(
            flops=8 * rows * rows * columns, bytes_accessed=14 * rows * columns, transcendentals=0
        ),
        name="attend_step",
    )(first, query, key_own, key_prior, value_own, cot_prior, rate_prior)


def tokens_travel(queries, key_vectors, values, learn_rates, fast_weights, momentum):
    width = fast_weights.shape[3]
    slots = lax.axis_size("ctx")
    per_rep = fast_weights.shape[0] // 2
    rep_index = lax.axis_index("rep")
    start = rep_index * per_rep
    away = per_rep - start
    token_scale = float(slots * queries.shape[0]) ** (-0.5)

    def own_columns(tensor):
        return lax.dynamic_slice_in_dim(tensor, start * width, per_rep * width, 1)

    def own(tensor):
        return lax.dynamic_slice_in_dim(tensor, start, per_rep, 0)

    def other(tensor):
        return lax.dynamic_slice_in_dim(tensor, away, per_rep, 0)

    def hop(value, axis="ctx"):
        return ring(value, axis)

    value_own, cot = cotangent_step(token_scale, rep_index.reshape(1), values, learn_rates)
    keys, cots, asked = [own_columns(key_vectors)], [cot], [own_columns(queries)]
    for _ in range(1, slots):
        keys.append(hop(keys[-1]))
        cots.append(hop(cots[-1]))
    rate_prior = hop(own(learn_rates)[:, None, :])
    base = fast_weights - momentum_decay * momentum
    low = fast_weights.astype(jnp.bfloat16)
    low_par = hop(other(low), "rep")
    base_par = hop(other(base), "rep")
    for _ in range(1, slots):
        asked.append(hop(asked[-1]))
    first = (lax.axis_index("ctx") == 0).astype(jnp.int32).reshape(1)
    attended = attend_step(
        token_scale, first, asked[0], keys[0], keys[1], value_own, cots[1], rate_prior
    )
    own_low, own_base = own(low), own(base)
    new_own, new_par, new_low = gradient_step(
        keys, cots, own_low, low_par, own_base, base_par
    )
    heads = range(per_rep)
    moving = []
    for step in range(1, slots):
        if step == 1:
            sent = apply_step(asked[step], new_low, jnp.bfloat16)
        else:
            made = apply_step(asked[step], new_low, jnp.float32)
            sent = [
                (made[h] + moving[h].astype(jnp.float32)).astype(jnp.bfloat16) for h in heads
            ]
        moving = [hop(sent[h]) for h in heads]
    kept = apply_step(asked[0], new_low, jnp.float32, attended)
    layer_output = jnp.concatenate(
        [(kept[h] + moving[h].astype(jnp.float32)).astype(jnp.bfloat16) for h in heads], axis=1
    )
    returned = hop(new_par, "rep")
    fast_updated = jnp.where(
        rep_index == 0,
        jnp.concatenate([new_own, returned], axis=0),
        jnp.concatenate([returned, new_own], axis=0),
    )
    return (layer_output, fast_updated)


def on_device(queries, key_vectors, values, learn_rates, fast_weights, momentum):
    slots = lax.axis_size("ctx")
    fits = (
        lax.axis_size("rep") == 2
        and 2 <= slots <= 8
        and fast_weights.shape[0] % 2 == 0
        and fast_weights.shape[2] % 16 == 0
        and queries.shape[0] == 128
    )
    program = tokens_travel if fits else weights_travel
    return program(queries, key_vectors, values, learn_rates, fast_weights, momentum)


def solution(mesh):
    return jax.shard_map(
        on_device,
        mesh=mesh,
        in_specs=(
            P(("groups", "ctx"), "head"),
            P(("groups", "ctx"), "head"),
            P(("groups", "ctx"), "head"),
            P("head", ("groups", "ctx")),
            P(("groups", "head"), None, ("ctx", "rep"), None),
            P(("groups", "head"), None, ("ctx", "rep"), None),
        ),
        out_specs=(
            P(("groups", "ctx"), ("head", "rep")),
            P(("groups", "head"), None, ("ctx", "rep"), None),
        ),
        check_vma=False,
    )
```

```python
import functools

import jax
import jax.numpy as jnp
from jax import lax
from jax.experimental import pallas as pl
from jax.experimental.pallas import tpu as pltpu
from jax.sharding import PartitionSpec as P


epsilon = 1e-06
momentum_decay = 0.9
NT = (((1,), (1,)), ((), ()))


def passed_along(value, axis, steps):
    count = lax.axis_size(axis)
    initial, last = (max(0, -steps), min(count, count - steps))
    return lax.ppermute(value, axis, [(source, source + steps) for source in range(initial, last)])


def ring(value, axis, steps=1):
    count = lax.axis_size(axis)
    return lax.ppermute(value, axis, [(source, (source + steps) % count) for source in range(count)])


def unit_rows(tensor):
    widened = tensor.astype(jnp.float32)
    factor = lax.rsqrt(jnp.mean(widened * widened, axis=-1, keepdims=True) + epsilon)
    return (widened * factor).astype(jnp.bfloat16)


def swiglu_apply(inputs, weights):
    gate = jnp.einsum("thd,hrd->htr", inputs, weights[:, 0], preferred_element_type=jnp.float32)
    upward = jnp.einsum("thd,hrd->htr", inputs, weights[:, 1], preferred_element_type=jnp.float32)
    hidden = (jax.nn.silu(gate) * upward).astype(jnp.bfloat16)
    return jnp.einsum("htr,hrd->htd", hidden, weights[:, 2], preferred_element_type=jnp.float32)


def window_attention(query_own, key_own, value_own, key_prior, value_prior, first_block):
    tok_rows = query_own.shape[0]
    per_rep = query_own.shape[1]
    width = query_own.shape[2]
    block_rows = min(tok_rows, 512)
    block_count = tok_rows // block_rows
    key_window = jnp.concatenate([key_prior, key_own], axis=0)
    value_window = jnp.concatenate([value_prior, value_own], axis=0)
    score_scale = width ** (-0.5)
    position = jnp.arange(2 * tok_rows)
    valid = jnp.logical_or(position >= tok_rows, jnp.logical_not(first_block))
    query_blocks = query_own.reshape(block_count, block_rows, per_rep, width)

    def one_block(query_block):
        scores = (
            jnp.einsum("tad,sad->ats", query_block, key_window, preferred_element_type=jnp.float32)
            * score_scale
        )
        scores = jnp.where(valid[None, None, :], scores, -jnp.inf)
        peak = jnp.max(scores, axis=-1, keepdims=True)
        weights = jnp.exp(scores - peak)
        probs = (weights / jnp.sum(weights, axis=-1, keepdims=True)).astype(jnp.bfloat16)
        return jnp.einsum("ats,sad->tad", probs, value_window, preferred_element_type=jnp.float32)

    return lax.map(one_block, query_blocks).reshape(tok_rows, per_rep, width)


def weights_travel(queries, key_vectors, values, learn_rates, fast_weights, momentum):
    tok_rows = queries.shape[0]
    head_count = fast_weights.shape[0]
    width = fast_weights.shape[3]
    rep_count = lax.axis_size("rep")
    per_rep = head_count // rep_count
    rep_index = lax.axis_index("rep")
    ctx_index = lax.axis_index("ctx")
    total_tokens = tok_rows * lax.axis_size("ctx")
    query_heads = queries.reshape(tok_rows, head_count, width)
    key_heads = key_vectors.reshape(tok_rows, head_count, width)
    value_heads = values.reshape(tok_rows, head_count, width)
    query_unit = unit_rows(query_heads)
    key_unit = unit_rows(key_heads)
    token_scale = float(total_tokens) ** (-0.5)
    cotangent = (
        -(learn_rates.T[:, :, None] * token_scale) * value_heads.astype(jnp.float32)
    ).astype(jnp.bfloat16)
    weight_rows = lax.all_gather(fast_weights.astype(jnp.bfloat16), "ctx", axis=2, tiled=True)
    gate = jnp.einsum(
        "thd,hrd->htr", key_unit, weight_rows[:, 0], preferred_element_type=jnp.float32
    )
    upward = jnp.einsum(
        "thd,hrd->htr", key_unit, weight_rows[:, 1], preferred_element_type=jnp.float32
    )
    back = jnp.einsum(
        "thd,hrd->htr", cotangent, weight_rows[:, 2], preferred_element_type=jnp.float32
    )
    sigma = jax.nn.sigmoid(gate)
    activated = jax.nn.silu(gate)
    hidden = (activated * upward).astype(jnp.bfloat16)
    gate_back = (back * upward * sigma * (1.0 + gate * (1.0 - sigma))).astype(jnp.bfloat16)
    up_back = (back * activated).astype(jnp.bfloat16)
    grad_gate = jnp.einsum("htr,thd->hrd", gate_back, key_unit, preferred_element_type=jnp.float32)
    grad_up = jnp.einsum("htr,thd->hrd", up_back, key_unit, preferred_element_type=jnp.float32)
    grad_down = jnp.einsum("htr,thd->hrd", hidden, cotangent, preferred_element_type=jnp.float32)
    gradient = jnp.stack([grad_gate, grad_up, grad_down], axis=1)
    share = lax.psum_scatter(
        gradient.astype(jnp.bfloat16), "ctx", scatter_dimension=2, tiled=True
    ).astype(jnp.float32)
    fast_updated = fast_weights - (momentum_decay * momentum + share)
    new_rows = lax.all_gather(fast_updated.astype(jnp.bfloat16), "ctx", axis=2, tiled=True)
    own_start = rep_index * per_rep
    partial_out = swiglu_apply(query_unit, new_rows)
    traded = lax.all_to_all(
        partial_out.astype(jnp.bfloat16), "rep", split_axis=0, concat_axis=0, tiled=True
    ).astype(partial_out.dtype)
    fast_out = jnp.sum(traded.reshape(rep_count, per_rep, tok_rows, width), axis=0)
    attend_query = lax.dynamic_slice_in_dim(query_heads, own_start, per_rep, 1)
    attend_key = lax.dynamic_slice_in_dim(key_heads, own_start, per_rep, 1)
    attend_value = lax.dynamic_slice_in_dim(value_heads, own_start, per_rep, 1)
    key_prior, value_prior = passed_along((attend_key, attend_value), "ctx", 1)
    attended = window_attention(
        attend_query, attend_key, attend_value, key_prior, value_prior, ctx_index == 0
    )
    combined = attended + jnp.transpose(fast_out, (1, 0, 2))
    layer_output = combined.astype(jnp.bfloat16).reshape(tok_rows, per_rep * width)
    return (layer_output, fast_updated)


def in_hbm(value):
    return pltpu.with_memory_space_constraint(value, pltpu.HBM)


def cotangent_body(token_scale, rep, values, rates, out_raw, out):
    heads = rates.shape[0] // 2
    rows, columns = out.shape
    width = columns // heads
    for h in range(heads):
        rate = -(rates[pl.ds(rep[0] * heads + h, 1), :] * token_scale)
        rate = jnp.transpose(jnp.broadcast_to(rate, (rows, rows)))[:, :1]
        part = values[:, h * width : (h + 1) * width]
        out_raw[:, h * width : (h + 1) * width] = part
        out[:, h * width : (h + 1) * width] = (rate * part.astype(jnp.float32)).astype(jnp.bfloat16)


def cotangent_step(token_scale, rep, values, rates):
    rows, columns = values.shape[0], values.shape[1] // 2
    made = jax.ShapeDtypeStruct((rows, columns), jnp.bfloat16)
    whole = pl.BlockSpec((rows, columns), lambda i, rep: (0, 0))
    return pl.pallas_call(
        functools.partial(cotangent_body, token_scale),
        out_shape=(made, made),
        grid_spec=pltpu.PrefetchScalarGridSpec(
            num_scalar_prefetch=1,
            grid=(1,),
            in_specs=[
                pl.BlockSpec((rows, columns), lambda i, rep: (0, rep[0])),
                pl.BlockSpec(rates.shape, lambda i, rep: (0, 0)),
            ],
            out_specs=(whole, whole),
        ),
        compiler_params=pltpu.CompilerParams(vmem_limit_bytes=8 << 20),
        cost_estimate=pl.CostEstimate(
            flops=2 * rows * columns, bytes_accessed=6 * rows * columns, transcendentals=0
        ),
        name="cotangent_step",
    )(rep, in_hbm(values), in_hbm(rates))


def other_body(rep, weights, momentum, low, base):
    current = weights[...]
    low[...] = current.astype(jnp.bfloat16)
    base[...] = current - momentum_decay * momentum[...]


def other_step(rep, weights, momentum):
    heads = weights.shape[0] // 2
    block = (1,) + weights.shape[1:]
    made = (heads,) + weights.shape[1:]
    taken = pl.BlockSpec(block, lambda h, rep: ((1 - rep[0]) * heads + h, 0, 0, 0))
    given = pl.BlockSpec(block, lambda h, rep: (h, 0, 0, 0))
    return pl.pallas_call(
        other_body,
        out_shape=(pltpu.HBM(made, jnp.bfloat16), pltpu.HBM(made, jnp.float32)),
        grid_spec=pltpu.PrefetchScalarGridSpec(
            num_scalar_prefetch=1,
            grid=(heads,),
            in_specs=[taken, taken],
            out_specs=(given, given),
        ),
        compiler_params=pltpu.CompilerParams(vmem_limit_bytes=12 << 20),
        cost_estimate=pl.CostEstimate(
            flops=weights.size, bytes_accessed=7 * weights.size, transcendentals=0
        ),
        name="other_step",
    )(rep, in_hbm(weights), in_hbm(momentum))


def gradient_body(slots, rep, *refs):
    keys, cots = refs[:slots], refs[slots : 2 * slots]
    weights, momentum, low_par, base_par, new_own, new_par, new_low, unit, cot, low = refs[2 * slots :]
    rows = keys[0].shape[0]
    hid = weights.shape[2]
    for s in range(slots):
        here = pl.ds(s * rows, rows)
        unit[here, :] = unit_rows(keys[s][...])
        cot[here, :] = cots[s][...]
    for m in range(3):
        low[pl.ds(2 * m * hid, hid), :] = weights[0, m].astype(jnp.bfloat16)
        low[pl.ds((2 * m + 1) * hid, hid), :] = low_par[0, m]
    fed = lax.dot_general(low[: 4 * hid, :], unit[...], NT, preferred_element_type=jnp.float32)
    gate, upward = fed[: 2 * hid], fed[2 * hid :]
    back = lax.dot_general(low[4 * hid :, :], cot[...], NT, preferred_element_type=jnp.float32)
    sigma = jax.nn.sigmoid(gate)
    activated = gate * sigma
    hidden = (activated * upward).astype(jnp.bfloat16)
    gate_back = (back * upward * sigma * (1.0 + gate * (1.0 - sigma))).astype(jnp.bfloat16)
    up_back = (back * activated).astype(jnp.bfloat16)
    for m, (left, right) in enumerate(((gate_back, unit), (up_back, unit), (hidden, cot))):
        grad = jnp.dot(left, right[...], preferred_element_type=jnp.float32)
        fresh_own = weights[0, m] - (momentum_decay * momentum[0, m] + grad[:hid])
        fresh_par = base_par[0, m] - grad[hid:]
        new_own[0, m] = fresh_own
        new_par[0, m] = fresh_par
        new_low[0, pl.ds(2 * m * hid, hid), :] = fresh_own.astype(jnp.bfloat16)
        new_low[0, pl.ds((2 * m + 1) * hid, hid), :] = fresh_par.astype(jnp.bfloat16)


def gradient_step(rep, keys, cots, weights, momentum, low_par, base_par):
    slots = len(keys)
    rows = keys[0].shape[0]
    heads, _, hid, width = low_par.shape
    token_spec = pl.BlockSpec((rows, width), lambda h, rep: (0, h))
    own_spec = pl.BlockSpec((1, 3, hid, width), lambda h, rep: (rep[0] * heads + h, 0, 0, 0))
    weight_spec = pl.BlockSpec((1, 3, hid, width), lambda h, rep: (h, 0, 0, 0))
    low_spec = pl.BlockSpec((1, 6 * hid, width), lambda h, rep: (h, 0, 0))
    fresh = pltpu.HBM(low_par.shape, jnp.float32)
    return pl.pallas_call(
        functools.partial(gradient_body, slots),
        out_shape=(fresh, fresh, jax.ShapeDtypeStruct((heads, 6 * hid, width), jnp.bfloat16)),
        grid_spec=pltpu.PrefetchScalarGridSpec(
            num_scalar_prefetch=1,
            grid=(heads,),
            in_specs=[token_spec] * (2 * slots) + [own_spec] * 2 + [weight_spec] * 2,
            out_specs=(weight_spec, weight_spec, low_spec),
            scratch_shapes=[
                pltpu.VMEM((slots * rows, width), jnp.bfloat16),
                pltpu.VMEM((slots * rows, width), jnp.bfloat16),
                pltpu.VMEM((6 * hid, width), jnp.bfloat16),
            ],
        ),
        compiler_params=pltpu.CompilerParams(vmem_limit_bytes=24 << 20),
        cost_estimate=pl.CostEstimate(
            flops=24 * heads * slots * rows * hid * width,
            bytes_accessed=48 * heads * hid * width,
            transcendentals=0,
        ),
        name="gradient_step",
    )(rep, *map(in_hbm, (*keys, *cots, weights, momentum, low_par, base_par)))


def apply_body(query, low, *refs):
    hid = low.shape[1] // 6
    unit = unit_rows(query[...])
    gate = lax.dot_general(unit, low[0, : 2 * hid, :], NT, preferred_element_type=jnp.float32)
    upward = lax.dot_general(
        unit, low[0, 2 * hid : 4 * hid, :], NT, preferred_element_type=jnp.float32
    )
    hidden = (gate * jax.nn.sigmoid(gate) * upward).astype(jnp.bfloat16)
    made = jnp.dot(hidden, low[0, 4 * hid :, :], preferred_element_type=jnp.float32)
    if len(refs) > 1:
        made = made + refs[0][...]
    refs[-1][...] = made.astype(refs[-1].dtype)


def apply_step(head, query, low, dtype, *more):
    rows, width = query.shape
    total = low.shape[1]
    whole = pl.BlockSpec((rows, width), lambda i: (0, 0))
    return pl.pallas_call(
        apply_body,
        out_shape=jax.ShapeDtypeStruct((rows, width), dtype),
        grid=(1,),
        in_specs=[whole, pl.BlockSpec((1, total, width), lambda i: (head, 0, 0))]
        + [whole] * len(more),
        out_specs=whole,
        compiler_params=pltpu.CompilerParams(vmem_limit_bytes=8 << 20),
        cost_estimate=pl.CostEstimate(
            flops=2 * rows * total * width, bytes_accessed=2 * total * width, transcendentals=0
        ),
        name="apply_step",
    )(query, low, *more)


def attend_body(token_scale, first, key_own, key_prior, value_own, cot_prior, rate_prior, *refs):
    heads = len(refs) // 2
    asked, outs = refs[:heads], refs[heads:]
    width = asked[0].shape[1]
    allowed = jnp.where(first[0] != 0, -jnp.inf, 0.0).astype(jnp.float32)
    for h in range(heads):
        columns = slice(h * width, (h + 1) * width)
        part = asked[h][...]
        near = lax.dot_general(part, key_own[:, columns], NT, preferred_element_type=jnp.float32)
        far = lax.dot_general(part, key_prior[:, columns], NT, preferred_element_type=jnp.float32)
        near = near * width ** (-0.5)
        far = far * width ** (-0.5) + allowed
        peak = jnp.maximum(
            jnp.max(near, axis=-1, keepdims=True), jnp.max(far, axis=-1, keepdims=True)
        )
        near = jnp.exp(near - peak)
        far = jnp.exp(far - peak)
        total = jnp.sum(near, axis=-1, keepdims=True) + jnp.sum(far, axis=-1, keepdims=True)
        rate = -(rate_prior[h] * token_scale)
        near = (near / total).astype(jnp.bfloat16)
        far = (far / total / rate).astype(jnp.bfloat16)
        outs[h][...] = jnp.dot(
            near, value_own[:, columns], preferred_element_type=jnp.float32
        ) + jnp.dot(far, cot_prior[:, columns], preferred_element_type=jnp.float32)


def attend_step(token_scale, first, key_own, key_prior, value_own, cot_prior, rate_prior, asked):
    rows, columns = key_own.shape
    made = tuple(jax.ShapeDtypeStruct(query.shape, jnp.float32) for query in asked)
    return pl.pallas_call(
        functools.partial(attend_body, token_scale),
        out_shape=made,
        in_specs=[pl.BlockSpec(memory_space=pltpu.SMEM)] + [pl.BlockSpec()] * (5 + len(asked)),
        compiler_params=pltpu.CompilerParams(vmem_limit_bytes=8 << 20),
        cost_estimate=pl.CostEstimate(
            flops=8 * rows * rows * columns, bytes_accessed=14 * rows * columns, transcendentals=0
        ),
        name="attend_step",
    )(first, *map(in_hbm, (key_own, key_prior, value_own, cot_prior)), rate_prior, *asked)


def tokens_travel(queries, key_vectors, values, learn_rates, fast_weights, momentum):
    width = fast_weights.shape[3]
    slots = lax.axis_size("ctx")
    per_rep = fast_weights.shape[0] // 2
    rep_index = lax.axis_index("rep")
    start = rep_index * per_rep
    token_scale = float(slots * queries.shape[0]) ** (-0.5)

    def own_columns(tensor):
        return lax.dynamic_slice_in_dim(tensor, start * width, per_rep * width, 1)

    def hop(value, axis="ctx"):
        return ring(value, axis)

    rep = rep_index.reshape(1)
    value_own, cot = cotangent_step(token_scale, rep, values, learn_rates)
    heads = range(per_rep)
    keys, cots = [own_columns(key_vectors)], [cot]
    asked = [[lax.dynamic_slice_in_dim(queries, (start + h) * width, width, 1) for h in heads]]
    for _ in range(1, slots):
        keys.append(hop(keys[-1]))
        cots.append(hop(cots[-1]))
    rate_prior = hop(lax.dynamic_slice_in_dim(learn_rates, start, per_rep, 0)[:, None, :])
    low_other, base_other = other_step(rep, fast_weights, momentum)
    low_par = hop(low_other, "rep")
    base_par = hop(base_other, "rep")
    for _ in range(1, slots):
        asked.append([hop(asked[-1][h]) for h in heads])
    first = (lax.axis_index("ctx") == 0).astype(jnp.int32).reshape(1)
    attended = attend_step(
        token_scale, first, keys[0], keys[1], value_own, cots[1], rate_prior, asked[0]
    )
    new_own, new_par, new_low = gradient_step(
        rep, keys, cots, fast_weights, momentum, low_par, base_par
    )
    moving = []
    for step in range(1, slots):
        if step == 1:
            sent = [apply_step(h, asked[step][h], new_low, jnp.bfloat16) for h in heads]
        else:
            made = [apply_step(h, asked[step][h], new_low, jnp.float32) for h in heads]
            sent = [
                (made[h] + moving[h].astype(jnp.float32)).astype(jnp.bfloat16) for h in heads
            ]
        moving = [hop(sent[h]) for h in heads]
    kept = []
    for h in heads:
        kept.append(apply_step(h, asked[0][h], new_low, jnp.float32, attended[h]))
    layer_output = jnp.concatenate(
        [(kept[h] + moving[h].astype(jnp.float32)).astype(jnp.bfloat16) for h in heads], axis=1
    )
    returned = hop(new_par, "rep")
    fast_updated = jnp.where(
        rep_index == 0,
        jnp.concatenate([new_own, returned], axis=0),
        jnp.concatenate([returned, new_own], axis=0),
    )
    return (layer_output, fast_updated)


def on_device(queries, key_vectors, values, learn_rates, fast_weights, momentum):
    slots = lax.axis_size("ctx")
    fits = (
        lax.axis_size("rep") == 2
        and 2 <= slots <= 8
        and fast_weights.shape[0] % 2 == 0
        and fast_weights.shape[2] % 16 == 0
        and queries.shape[0] == 128
    )
    program = tokens_travel if fits else weights_travel
    return program(queries, key_vectors, values, learn_rates, fast_weights, momentum)


def solution(mesh):
    return jax.shard_map(
        on_device,
        mesh=mesh,
        in_specs=(
            P(("groups", "ctx"), "head"),
            P(("groups", "ctx"), "head"),
            P(("groups", "ctx"), "head"),
            P("head", ("groups", "ctx")),
            P(("groups", "head"), None, ("ctx", "rep"), None),
            P(("groups", "head"), None, ("ctx", "rep"), None),
        ),
        out_specs=(
            P(("groups", "ctx"), ("head", "rep")),
            P(("groups", "head"), None, ("ctx", "rep"), None),
        ),
        check_vma=False,
    )
```

```python
import functools

import jax
import jax.numpy as jnp
from jax import lax
from jax.experimental import pallas as pl
from jax.experimental.pallas import tpu as pltpu
from jax.sharding import PartitionSpec as P


epsilon = 1e-06
momentum_decay = 0.9
NT = (((1,), (1,)), ((), ()))


def passed_along(value, axis, steps):
    count = lax.axis_size(axis)
    initial, last = (max(0, -steps), min(count, count - steps))
    return lax.ppermute(value, axis, [(source, source + steps) for source in range(initial, last)])


def ring(value, axis, steps=1):
    count = lax.axis_size(axis)
    return lax.ppermute(value, axis, [(source, (source + steps) % count) for source in range(count)])


def unit_rows(tensor):
    widened = tensor.astype(jnp.float32)
    factor = lax.rsqrt(jnp.mean(widened * widened, axis=-1, keepdims=True) + epsilon)
    return (widened * factor).astype(jnp.bfloat16)


def swiglu_apply(inputs, weights):
    gate = jnp.einsum("thd,hrd->htr", inputs, weights[:, 0], preferred_element_type=jnp.float32)
    upward = jnp.einsum("thd,hrd->htr", inputs, weights[:, 1], preferred_element_type=jnp.float32)
    hidden = (jax.nn.silu(gate) * upward).astype(jnp.bfloat16)
    return jnp.einsum("htr,hrd->htd", hidden, weights[:, 2], preferred_element_type=jnp.float32)


def window_attention(query_own, key_own, value_own, key_prior, value_prior, first_block):
    tok_rows = query_own.shape[0]
    per_rep = query_own.shape[1]
    width = query_own.shape[2]
    block_rows = min(tok_rows, 512)
    block_count = tok_rows // block_rows
    key_window = jnp.concatenate([key_prior, key_own], axis=0)
    value_window = jnp.concatenate([value_prior, value_own], axis=0)
    score_scale = width ** (-0.5)
    position = jnp.arange(2 * tok_rows)
    valid = jnp.logical_or(position >= tok_rows, jnp.logical_not(first_block))
    query_blocks = query_own.reshape(block_count, block_rows, per_rep, width)

    def one_block(query_block):
        scores = (
            jnp.einsum("tad,sad->ats", query_block, key_window, preferred_element_type=jnp.float32)
            * score_scale
        )
        scores = jnp.where(valid[None, None, :], scores, -jnp.inf)
        peak = jnp.max(scores, axis=-1, keepdims=True)
        weights = jnp.exp(scores - peak)
        probs = (weights / jnp.sum(weights, axis=-1, keepdims=True)).astype(jnp.bfloat16)
        return jnp.einsum("ats,sad->tad", probs, value_window, preferred_element_type=jnp.float32)

    return lax.map(one_block, query_blocks).reshape(tok_rows, per_rep, width)


def weights_travel(queries, key_vectors, values, learn_rates, fast_weights, momentum):
    tok_rows = queries.shape[0]
    head_count = fast_weights.shape[0]
    width = fast_weights.shape[3]
    rep_count = lax.axis_size("rep")
    per_rep = head_count // rep_count
    rep_index = lax.axis_index("rep")
    ctx_index = lax.axis_index("ctx")
    total_tokens = tok_rows * lax.axis_size("ctx")
    query_heads = queries.reshape(tok_rows, head_count, width)
    key_heads = key_vectors.reshape(tok_rows, head_count, width)
    value_heads = values.reshape(tok_rows, head_count, width)
    query_unit = unit_rows(query_heads)
    key_unit = unit_rows(key_heads)
    token_scale = float(total_tokens) ** (-0.5)
    cotangent = (
        -(learn_rates.T[:, :, None] * token_scale) * value_heads.astype(jnp.float32)
    ).astype(jnp.bfloat16)
    weight_rows = lax.all_gather(fast_weights.astype(jnp.bfloat16), "ctx", axis=2, tiled=True)
    gate = jnp.einsum(
        "thd,hrd->htr", key_unit, weight_rows[:, 0], preferred_element_type=jnp.float32
    )
    upward = jnp.einsum(
        "thd,hrd->htr", key_unit, weight_rows[:, 1], preferred_element_type=jnp.float32
    )
    back = jnp.einsum(
        "thd,hrd->htr", cotangent, weight_rows[:, 2], preferred_element_type=jnp.float32
    )
    sigma = jax.nn.sigmoid(gate)
    activated = jax.nn.silu(gate)
    hidden = (activated * upward).astype(jnp.bfloat16)
    gate_back = (back * upward * sigma * (1.0 + gate * (1.0 - sigma))).astype(jnp.bfloat16)
    up_back = (back * activated).astype(jnp.bfloat16)
    grad_gate = jnp.einsum("htr,thd->hrd", gate_back, key_unit, preferred_element_type=jnp.float32)
    grad_up = jnp.einsum("htr,thd->hrd", up_back, key_unit, preferred_element_type=jnp.float32)
    grad_down = jnp.einsum("htr,thd->hrd", hidden, cotangent, preferred_element_type=jnp.float32)
    gradient = jnp.stack([grad_gate, grad_up, grad_down], axis=1)
    share = lax.psum_scatter(
        gradient.astype(jnp.bfloat16), "ctx", scatter_dimension=2, tiled=True
    ).astype(jnp.float32)
    fast_updated = fast_weights - (momentum_decay * momentum + share)
    new_rows = lax.all_gather(fast_updated.astype(jnp.bfloat16), "ctx", axis=2, tiled=True)
    own_start = rep_index * per_rep
    partial_out = swiglu_apply(query_unit, new_rows)
    traded = lax.all_to_all(
        partial_out.astype(jnp.bfloat16), "rep", split_axis=0, concat_axis=0, tiled=True
    ).astype(partial_out.dtype)
    fast_out = jnp.sum(traded.reshape(rep_count, per_rep, tok_rows, width), axis=0)
    attend_query = lax.dynamic_slice_in_dim(query_heads, own_start, per_rep, 1)
    attend_key = lax.dynamic_slice_in_dim(key_heads, own_start, per_rep, 1)
    attend_value = lax.dynamic_slice_in_dim(value_heads, own_start, per_rep, 1)
    key_prior, value_prior = passed_along((attend_key, attend_value), "ctx", 1)
    attended = window_attention(
        attend_query, attend_key, attend_value, key_prior, value_prior, ctx_index == 0
    )
    combined = attended + jnp.transpose(fast_out, (1, 0, 2))
    layer_output = combined.astype(jnp.bfloat16).reshape(tok_rows, per_rep * width)
    return (layer_output, fast_updated)


def in_hbm(value):
    return pltpu.with_memory_space_constraint(value, pltpu.HBM)


def columns_body(rep, whole, out, semaphore):
    columns = out.shape[1]
    taken = whole.at[:, pl.ds(pl.multiple_of(rep[0] * columns, columns), columns)]
    copy = pltpu.make_async_copy(taken, out, semaphore)
    copy.start()
    copy.wait()


def columns_step(rep, whole):
    rows, columns = whole.shape[0], whole.shape[1] // 2
    return pl.pallas_call(
        columns_body,
        out_shape=jax.ShapeDtypeStruct((rows, columns), whole.dtype),
        in_specs=[pl.BlockSpec(memory_space=pltpu.SMEM), pl.BlockSpec(memory_space=pl.ANY)],
        out_specs=pl.BlockSpec(memory_space=pltpu.VMEM),
        scratch_shapes=[pltpu.SemaphoreType.DMA],
        compiler_params=pltpu.CompilerParams(vmem_limit_bytes=4 << 20),
        cost_estimate=pl.CostEstimate(
            flops=0, bytes_accessed=4 * rows * columns, transcendentals=0
        ),
        name="columns_step",
    )(rep, in_hbm(whole))


def cotangent_body(token_scale, rep, values, rates, out_raw, out):
    heads = rates.shape[0] // 2
    rows, columns = out.shape
    width = columns // heads
    for h in range(heads):
        rate = -(rates[pl.ds(rep[0] * heads + h, 1), :] * token_scale)
        rate = jnp.transpose(jnp.broadcast_to(rate, (rows, rows)))[:, :1]
        part = values[:, h * width : (h + 1) * width]
        out_raw[:, h * width : (h + 1) * width] = part
        out[:, h * width : (h + 1) * width] = (rate * part.astype(jnp.float32)).astype(jnp.bfloat16)


def cotangent_step(token_scale, rep, values, rates):
    rows, columns = values.shape[0], values.shape[1] // 2
    made = jax.ShapeDtypeStruct((rows, columns), jnp.bfloat16)
    whole = pl.BlockSpec((rows, columns), lambda i, rep: (0, 0))
    return pl.pallas_call(
        functools.partial(cotangent_body, token_scale),
        out_shape=(made, made),
        grid_spec=pltpu.PrefetchScalarGridSpec(
            num_scalar_prefetch=1,
            grid=(1,),
            in_specs=[
                pl.BlockSpec((rows, columns), lambda i, rep: (0, rep[0])),
                pl.BlockSpec(rates.shape, lambda i, rep: (0, 0)),
            ],
            out_specs=(whole, whole),
        ),
        compiler_params=pltpu.CompilerParams(vmem_limit_bytes=8 << 20),
        cost_estimate=pl.CostEstimate(
            flops=2 * rows * columns, bytes_accessed=6 * rows * columns, transcendentals=0
        ),
        name="cotangent_step",
    )(rep, in_hbm(values), in_hbm(rates))


def other_body(rep, weights, momentum, low, base):
    current = weights[...]
    low[...] = current.astype(jnp.bfloat16)
    base[...] = current - momentum_decay * momentum[...]


def other_step(rep, weights, momentum):
    heads = weights.shape[0] // 2
    block = (1,) + weights.shape[1:]
    made = (heads,) + weights.shape[1:]
    taken = pl.BlockSpec(block, lambda h, rep: ((1 - rep[0]) * heads + h, 0, 0, 0))
    given = pl.BlockSpec(block, lambda h, rep: (h, 0, 0, 0))
    return pl.pallas_call(
        other_body,
        out_shape=(pltpu.HBM(made, jnp.bfloat16), pltpu.HBM(made, jnp.float32)),
        grid_spec=pltpu.PrefetchScalarGridSpec(
            num_scalar_prefetch=1,
            grid=(heads,),
            in_specs=[taken, taken],
            out_specs=(given, given),
        ),
        compiler_params=pltpu.CompilerParams(vmem_limit_bytes=12 << 20),
        cost_estimate=pl.CostEstimate(
            flops=weights.size, bytes_accessed=7 * weights.size, transcendentals=0
        ),
        name="other_step",
    )(rep, in_hbm(weights), in_hbm(momentum))


def gradient_body(slots, rep, *refs):
    keys, cots = refs[:slots], refs[slots : 2 * slots]
    weights, momentum, low_par, base_par, new_own, new_par, new_low, unit, cot, low = refs[2 * slots :]
    rows = keys[0].shape[0]
    hid = weights.shape[2]
    for s in range(slots):
        here = pl.ds(s * rows, rows)
        unit[here, :] = unit_rows(keys[s][...])
        cot[here, :] = cots[s][...]
    for m in range(3):
        low[pl.ds(2 * m * hid, hid), :] = weights[0, m].astype(jnp.bfloat16)
        low[pl.ds((2 * m + 1) * hid, hid), :] = low_par[0, m]
    fed = lax.dot_general(low[: 4 * hid, :], unit[...], NT, preferred_element_type=jnp.float32)
    gate, upward = fed[: 2 * hid], fed[2 * hid :]
    back = lax.dot_general(low[4 * hid :, :], cot[...], NT, preferred_element_type=jnp.float32)
    sigma = jax.nn.sigmoid(gate)
    activated = gate * sigma
    hidden = (activated * upward).astype(jnp.bfloat16)
    gate_back = (back * upward * sigma * (1.0 + gate * (1.0 - sigma))).astype(jnp.bfloat16)
    up_back = (back * activated).astype(jnp.bfloat16)
    for m, (left, right) in enumerate(((gate_back, unit), (up_back, unit), (hidden, cot))):
        grad = jnp.dot(left, right[...], preferred_element_type=jnp.float32)
        fresh_own = weights[0, m] - (momentum_decay * momentum[0, m] + grad[:hid])
        fresh_par = base_par[0, m] - grad[hid:]
        new_own[0, m] = fresh_own
        new_par[0, m] = fresh_par
        new_low[0, pl.ds(2 * m * hid, hid), :] = fresh_own.astype(jnp.bfloat16)
        new_low[0, pl.ds((2 * m + 1) * hid, hid), :] = fresh_par.astype(jnp.bfloat16)


def gradient_step(head, rep, keys, cots, weights, momentum, low_par, base_par):
    slots = len(keys)
    rows = keys[0].shape[0]
    heads, _, hid, width = low_par.shape
    block = (1, 3, hid, width)
    token_spec = pl.BlockSpec((rows, width), lambda i, rep: (0, head))
    own_spec = pl.BlockSpec(block, lambda i, rep: (rep[0] * heads + head, 0, 0, 0))
    par_spec = pl.BlockSpec(block, lambda i, rep: (head, 0, 0, 0))
    new_spec = pl.BlockSpec(block, lambda i, rep: (0, 0, 0, 0))
    low_spec = pl.BlockSpec((1, 6 * hid, width), lambda i, rep: (0, 0, 0))
    fresh = pltpu.HBM(block, jnp.float32)
    return pl.pallas_call(
        functools.partial(gradient_body, slots),
        out_shape=(fresh, fresh, jax.ShapeDtypeStruct((1, 6 * hid, width), jnp.bfloat16)),
        grid_spec=pltpu.PrefetchScalarGridSpec(
            num_scalar_prefetch=1,
            grid=(1,),
            in_specs=[token_spec] * (2 * slots) + [own_spec] * 2 + [par_spec] * 2,
            out_specs=(new_spec, new_spec, low_spec),
            scratch_shapes=[
                pltpu.VMEM((slots * rows, width), jnp.bfloat16),
                pltpu.VMEM((slots * rows, width), jnp.bfloat16),
                pltpu.VMEM((6 * hid, width), jnp.bfloat16),
            ],
        ),
        compiler_params=pltpu.CompilerParams(vmem_limit_bytes=24 << 20),
        cost_estimate=pl.CostEstimate(
            flops=24 * slots * rows * hid * width,
            bytes_accessed=48 * hid * width,
            transcendentals=0,
        ),
        name="gradient_step",
    )(rep, *map(in_hbm, (*keys, *cots, weights, momentum)), low_par, base_par)


def apply_body(query, low, *refs):
    hid = low.shape[1] // 6
    unit = unit_rows(query[...])
    gate = lax.dot_general(unit, low[0, : 2 * hid, :], NT, preferred_element_type=jnp.float32)
    upward = lax.dot_general(
        unit, low[0, 2 * hid : 4 * hid, :], NT, preferred_element_type=jnp.float32
    )
    hidden = (gate * jax.nn.sigmoid(gate) * upward).astype(jnp.bfloat16)
    made = jnp.dot(hidden, low[0, 4 * hid :, :], preferred_element_type=jnp.float32)
    if len(refs) > 1:
        made = made + refs[0][...]
    refs[-1][...] = made.astype(refs[-1].dtype)


def apply_step(query, low, dtype, *more):
    rows, width = query.shape
    total = low.shape[1]
    whole = pl.BlockSpec((rows, width), lambda i: (0, 0))
    return pl.pallas_call(
        apply_body,
        out_shape=jax.ShapeDtypeStruct((rows, width), dtype),
        grid=(1,),
        in_specs=[whole, pl.BlockSpec((1, total, width), lambda i: (0, 0, 0))]
        + [whole] * len(more),
        out_specs=whole,
        compiler_params=pltpu.CompilerParams(vmem_limit_bytes=8 << 20),
        cost_estimate=pl.CostEstimate(
            flops=2 * rows * total * width, bytes_accessed=2 * total * width, transcendentals=0
        ),
        name="apply_step",
    )(query, low, *more)


def output_body(kept, moved, *refs):
    refs[-1][...] = (kept[...] + moved[...].astype(jnp.float32)).astype(jnp.bfloat16)


def output_step(head, heads, kept, moved, before):
    rows, width = kept.shape
    whole = pl.BlockSpec((rows, width), lambda i: (0, 0))
    more = () if before is None else (before,)
    return pl.pallas_call(
        output_body,
        out_shape=pltpu.HBM((rows, heads * width), jnp.bfloat16),
        grid=(1,),
        in_specs=[whole, whole] + [pl.BlockSpec(memory_space=pl.ANY)] * len(more),
        out_specs=pl.BlockSpec((rows, width), lambda i: (0, head)),
        input_output_aliases={2: 0} if more else {},
        compiler_params=pltpu.CompilerParams(vmem_limit_bytes=4 << 20),
        cost_estimate=pl.CostEstimate(
            flops=rows * width, bytes_accessed=8 * rows * width, transcendentals=0
        ),
        name="output_step",
    )(kept, moved, *more)


def attend_body(token_scale, first, key_own, key_prior, value_own, cot_prior, rate_prior, *refs):
    heads = len(refs) // 2
    asked, outs = refs[:heads], refs[heads:]
    width = asked[0].shape[1]
    allowed = jnp.where(first[0] != 0, -jnp.inf, 0.0).astype(jnp.float32)
    for h in range(heads):
        columns = slice(h * width, (h + 1) * width)
        part = asked[h][...]
        near = lax.dot_general(part, key_own[:, columns], NT, preferred_element_type=jnp.float32)
        far = lax.dot_general(part, key_prior[:, columns], NT, preferred_element_type=jnp.float32)
        near = near * width ** (-0.5)
        far = far * width ** (-0.5) + allowed
        peak = jnp.maximum(
            jnp.max(near, axis=-1, keepdims=True), jnp.max(far, axis=-1, keepdims=True)
        )
        near = jnp.exp(near - peak)
        far = jnp.exp(far - peak)
        total = jnp.sum(near, axis=-1, keepdims=True) + jnp.sum(far, axis=-1, keepdims=True)
        rate = -(rate_prior[h] * token_scale)
        near = (near / total).astype(jnp.bfloat16)
        far = (far / total / rate).astype(jnp.bfloat16)
        outs[h][...] = jnp.dot(
            near, value_own[:, columns], preferred_element_type=jnp.float32
        ) + jnp.dot(far, cot_prior[:, columns], preferred_element_type=jnp.float32)


def attend_step(token_scale, first, key_own, key_prior, value_own, cot_prior, rate_prior, asked):
    rows, columns = key_own.shape
    made = tuple(jax.ShapeDtypeStruct(query.shape, jnp.float32) for query in asked)
    return pl.pallas_call(
        functools.partial(attend_body, token_scale),
        out_shape=made,
        in_specs=[pl.BlockSpec(memory_space=pltpu.SMEM)] + [pl.BlockSpec()] * (5 + len(asked)),
        compiler_params=pltpu.CompilerParams(vmem_limit_bytes=8 << 20),
        cost_estimate=pl.CostEstimate(
            flops=8 * rows * rows * columns, bytes_accessed=14 * rows * columns, transcendentals=0
        ),
        name="attend_step",
    )(first, *map(in_hbm, (key_own, key_prior, value_own, cot_prior)), rate_prior, *asked)


def tokens_travel(queries, key_vectors, values, learn_rates, fast_weights, momentum):
    width = fast_weights.shape[3]
    slots = lax.axis_size("ctx")
    per_rep = fast_weights.shape[0] // 2
    rep_index = lax.axis_index("rep")
    start = rep_index * per_rep
    token_scale = float(slots * queries.shape[0]) ** (-0.5)

    def hop(value, axis="ctx"):
        return ring(value, axis)

    rep = rep_index.reshape(1)
    value_own, cot = cotangent_step(token_scale, rep, values, learn_rates)
    heads = range(per_rep)
    keys, cots = [columns_step(rep, key_vectors)], [cot]
    asked = [[lax.dynamic_slice_in_dim(queries, (start + h) * width, width, 1) for h in heads]]
    for _ in range(1, slots):
        keys.append(hop(keys[-1]))
        cots.append(hop(cots[-1]))
    rate_prior = hop(lax.dynamic_slice_in_dim(learn_rates, start, per_rep, 0)[:, None, :])
    low_other, base_other = other_step(rep, fast_weights, momentum)
    low_par = hop(low_other, "rep")
    base_par = hop(base_other, "rep")
    for _ in range(1, slots):
        asked.append([hop(asked[-1][h]) for h in heads])
    first = (lax.axis_index("ctx") == 0).astype(jnp.int32).reshape(1)
    attended = attend_step(
        token_scale, first, keys[0], keys[1], value_own, cots[1], rate_prior, asked[0]
    )
    fresh = []
    for h in heads:
        fresh.append(gradient_step(h, rep, keys, cots, fast_weights, momentum, low_par, base_par))
    lows = [new[2] for new in fresh]
    moving = []
    for step in range(1, slots):
        if step == 1:
            sent = [apply_step(asked[step][h], lows[h], jnp.bfloat16) for h in heads]
        else:
            made = [apply_step(asked[step][h], lows[h], jnp.float32) for h in heads]
            sent = [
                (made[h] + moving[h].astype(jnp.float32)).astype(jnp.bfloat16) for h in heads
            ]
        moving = [hop(sent[h]) for h in heads]
    layer_output = None
    for h in heads:
        kept = apply_step(asked[0][h], lows[h], jnp.float32, attended[h])
        layer_output = output_step(h, per_rep, kept, moving[h], layer_output)
    returned = [hop(fresh[h][1], "rep") for h in heads]
    owned = [new[0] for new in fresh]
    fast_updated = jnp.where(
        rep_index == 0,
        jnp.concatenate([*owned, *returned], axis=0),
        jnp.concatenate([*returned, *owned], axis=0),
    )
    return (layer_output, fast_updated)


def on_device(queries, key_vectors, values, learn_rates, fast_weights, momentum):
    slots = lax.axis_size("ctx")
    fits = (
        lax.axis_size("rep") == 2
        and 2 <= slots <= 8
        and fast_weights.shape[0] % 2 == 0
        and fast_weights.shape[2] % 16 == 0
        and queries.shape[0] == 128
    )
    program = tokens_travel if fits else weights_travel
    return program(queries, key_vectors, values, learn_rates, fast_weights, momentum)


def solution(mesh):
    return jax.shard_map(
        on_device,
        mesh=mesh,
        in_specs=(
            P(("groups", "ctx"), "head"),
            P(("groups", "ctx"), "head"),
            P(("groups", "ctx"), "head"),
            P("head", ("groups", "ctx")),
            P(("groups", "head"), None, ("ctx", "rep"), None),
            P(("groups", "head"), None, ("ctx", "rep"), None),
        ),
        out_specs=(
            P(("groups", "ctx"), ("head", "rep")),
            P(("groups", "head"), None, ("ctx", "rep"), None),
        ),
        check_vma=False,
    )
```

```python
import functools

import jax
import jax.numpy as jnp
from jax import lax
from jax.experimental import pallas as pl
from jax.experimental.pallas import tpu as pltpu
from jax.sharding import PartitionSpec as P


epsilon = 1e-06
momentum_decay = 0.9
NT = (((1,), (1,)), ((), ()))


def passed_along(value, axis, steps):
    count = lax.axis_size(axis)
    initial, last = (max(0, -steps), min(count, count - steps))
    return lax.ppermute(value, axis, [(source, source + steps) for source in range(initial, last)])


def ring(value, axis, steps=1):
    count = lax.axis_size(axis)
    return lax.ppermute(value, axis, [(source, (source + steps) % count) for source in range(count)])


def unit_rows(tensor):
    widened = tensor.astype(jnp.float32)
    factor = lax.rsqrt(jnp.mean(widened * widened, axis=-1, keepdims=True) + epsilon)
    return (widened * factor).astype(jnp.bfloat16)


def swiglu_apply(inputs, weights):
    gate = jnp.einsum("thd,hrd->htr", inputs, weights[:, 0], preferred_element_type=jnp.float32)
    upward = jnp.einsum("thd,hrd->htr", inputs, weights[:, 1], preferred_element_type=jnp.float32)
    hidden = (jax.nn.silu(gate) * upward).astype(jnp.bfloat16)
    return jnp.einsum("htr,hrd->htd", hidden, weights[:, 2], preferred_element_type=jnp.float32)


def window_attention(query_own, key_own, value_own, key_prior, value_prior, first_block):
    tok_rows = query_own.shape[0]
    per_rep = query_own.shape[1]
    width = query_own.shape[2]
    block_rows = min(tok_rows, 512)
    block_count = tok_rows // block_rows
    key_window = jnp.concatenate([key_prior, key_own], axis=0)
    value_window = jnp.concatenate([value_prior, value_own], axis=0)
    score_scale = width ** (-0.5)
    position = jnp.arange(2 * tok_rows)
    valid = jnp.logical_or(position >= tok_rows, jnp.logical_not(first_block))
    query_blocks = query_own.reshape(block_count, block_rows, per_rep, width)

    def one_block(query_block):
        scores = (
            jnp.einsum("tad,sad->ats", query_block, key_window, preferred_element_type=jnp.float32)
            * score_scale
        )
        scores = jnp.where(valid[None, None, :], scores, -jnp.inf)
        peak = jnp.max(scores, axis=-1, keepdims=True)
        weights = jnp.exp(scores - peak)
        probs = (weights / jnp.sum(weights, axis=-1, keepdims=True)).astype(jnp.bfloat16)
        return jnp.einsum("ats,sad->tad", probs, value_window, preferred_element_type=jnp.float32)

    return lax.map(one_block, query_blocks).reshape(tok_rows, per_rep, width)


def weights_travel(queries, key_vectors, values, learn_rates, fast_weights, momentum):
    tok_rows = queries.shape[0]
    head_count = fast_weights.shape[0]
    width = fast_weights.shape[3]
    rep_count = lax.axis_size("rep")
    per_rep = head_count // rep_count
    rep_index = lax.axis_index("rep")
    ctx_index = lax.axis_index("ctx")
    total_tokens = tok_rows * lax.axis_size("ctx")
    query_heads = queries.reshape(tok_rows, head_count, width)
    key_heads = key_vectors.reshape(tok_rows, head_count, width)
    value_heads = values.reshape(tok_rows, head_count, width)
    query_unit = unit_rows(query_heads)
    key_unit = unit_rows(key_heads)
    token_scale = float(total_tokens) ** (-0.5)
    cotangent = (
        -(learn_rates.T[:, :, None] * token_scale) * value_heads.astype(jnp.float32)
    ).astype(jnp.bfloat16)
    weight_rows = lax.all_gather(fast_weights.astype(jnp.bfloat16), "ctx", axis=2, tiled=True)
    gate = jnp.einsum(
        "thd,hrd->htr", key_unit, weight_rows[:, 0], preferred_element_type=jnp.float32
    )
    upward = jnp.einsum(
        "thd,hrd->htr", key_unit, weight_rows[:, 1], preferred_element_type=jnp.float32
    )
    back = jnp.einsum(
        "thd,hrd->htr", cotangent, weight_rows[:, 2], preferred_element_type=jnp.float32
    )
    sigma = jax.nn.sigmoid(gate)
    activated = jax.nn.silu(gate)
    hidden = (activated * upward).astype(jnp.bfloat16)
    gate_back = (back * upward * sigma * (1.0 + gate * (1.0 - sigma))).astype(jnp.bfloat16)
    up_back = (back * activated).astype(jnp.bfloat16)
    grad_gate = jnp.einsum("htr,thd->hrd", gate_back, key_unit, preferred_element_type=jnp.float32)
    grad_up = jnp.einsum("htr,thd->hrd", up_back, key_unit, preferred_element_type=jnp.float32)
    grad_down = jnp.einsum("htr,thd->hrd", hidden, cotangent, preferred_element_type=jnp.float32)
    gradient = jnp.stack([grad_gate, grad_up, grad_down], axis=1)
    share = lax.psum_scatter(
        gradient.astype(jnp.bfloat16), "ctx", scatter_dimension=2, tiled=True
    ).astype(jnp.float32)
    fast_updated = fast_weights - (momentum_decay * momentum + share)
    new_rows = lax.all_gather(fast_updated.astype(jnp.bfloat16), "ctx", axis=2, tiled=True)
    own_start = rep_index * per_rep
    partial_out = swiglu_apply(query_unit, new_rows)
    traded = lax.all_to_all(
        partial_out.astype(jnp.bfloat16), "rep", split_axis=0, concat_axis=0, tiled=True
    ).astype(partial_out.dtype)
    fast_out = jnp.sum(traded.reshape(rep_count, per_rep, tok_rows, width), axis=0)
    attend_query = lax.dynamic_slice_in_dim(query_heads, own_start, per_rep, 1)
    attend_key = lax.dynamic_slice_in_dim(key_heads, own_start, per_rep, 1)
    attend_value = lax.dynamic_slice_in_dim(value_heads, own_start, per_rep, 1)
    key_prior, value_prior = passed_along((attend_key, attend_value), "ctx", 1)
    attended = window_attention(
        attend_query, attend_key, attend_value, key_prior, value_prior, ctx_index == 0
    )
    combined = attended + jnp.transpose(fast_out, (1, 0, 2))
    layer_output = combined.astype(jnp.bfloat16).reshape(tok_rows, per_rep * width)
    return (layer_output, fast_updated)


def in_hbm(value):
    return pltpu.with_memory_space_constraint(value, pltpu.HBM)


def columns_body(rep, whole, out, semaphore):
    columns = out.shape[1]
    taken = whole.at[:, pl.ds(pl.multiple_of(rep[0] * columns, columns), columns)]
    copy = pltpu.make_async_copy(taken, out, semaphore)
    copy.start()
    copy.wait()


def columns_step(rep, whole):
    rows, columns = whole.shape[0], whole.shape[1] // 2
    return pl.pallas_call(
        columns_body,
        out_shape=jax.ShapeDtypeStruct((rows, columns), whole.dtype),
        in_specs=[pl.BlockSpec(memory_space=pltpu.SMEM), pl.BlockSpec(memory_space=pl.ANY)],
        out_specs=pl.BlockSpec(memory_space=pltpu.VMEM),
        scratch_shapes=[pltpu.SemaphoreType.DMA],
        compiler_params=pltpu.CompilerParams(vmem_limit_bytes=4 << 20),
        cost_estimate=pl.CostEstimate(
            flops=0, bytes_accessed=4 * rows * columns, transcendentals=0
        ),
        name="columns_step",
    )(rep, in_hbm(whole))


def cotangent_body(token_scale, rep, values, rates, out_raw, out):
    heads = rates.shape[0] // 2
    rows, columns = out.shape
    width = columns // heads
    for h in range(heads):
        rate = -(rates[pl.ds(rep[0] * heads + h, 1), :] * token_scale)
        rate = jnp.transpose(jnp.broadcast_to(rate, (rows, rows)))[:, :1]
        part = values[:, h * width : (h + 1) * width]
        out_raw[:, h * width : (h + 1) * width] = part
        out[:, h * width : (h + 1) * width] = (rate * part.astype(jnp.float32)).astype(jnp.bfloat16)


def cotangent_step(token_scale, rep, values, rates):
    rows, columns = values.shape[0], values.shape[1] // 2
    made = jax.ShapeDtypeStruct((rows, columns), jnp.bfloat16)
    whole = pl.BlockSpec((rows, columns), lambda i, rep: (0, 0))
    return pl.pallas_call(
        functools.partial(cotangent_body, token_scale),
        out_shape=(made, made),
        grid_spec=pltpu.PrefetchScalarGridSpec(
            num_scalar_prefetch=1,
            grid=(1,),
            in_specs=[
                pl.BlockSpec((rows, columns), lambda i, rep: (0, rep[0])),
                pl.BlockSpec(rates.shape, lambda i, rep: (0, 0)),
            ],
            out_specs=(whole, whole),
        ),
        compiler_params=pltpu.CompilerParams(vmem_limit_bytes=8 << 20),
        cost_estimate=pl.CostEstimate(
            flops=2 * rows * columns, bytes_accessed=6 * rows * columns, transcendentals=0
        ),
        name="cotangent_step",
    )(rep, in_hbm(values), in_hbm(rates))


def other_body(rep, weights, momentum, low, base):
    current = weights[...]
    low[...] = current.astype(jnp.bfloat16)
    base[...] = current - momentum_decay * momentum[...]


def other_step(rep, weights, momentum):
    heads = weights.shape[0] // 2
    block = (1,) + weights.shape[1:]
    made = (heads,) + weights.shape[1:]
    taken = pl.BlockSpec(block, lambda h, rep: ((1 - rep[0]) * heads + h, 0, 0, 0))
    given = pl.BlockSpec(block, lambda h, rep: (h, 0, 0, 0))
    return pl.pallas_call(
        other_body,
        out_shape=(pltpu.HBM(made, jnp.bfloat16), pltpu.HBM(made, jnp.float32)),
        grid_spec=pltpu.PrefetchScalarGridSpec(
            num_scalar_prefetch=1,
            grid=(heads,),
            in_specs=[taken, taken],
            out_specs=(given, given),
        ),
        compiler_params=pltpu.CompilerParams(vmem_limit_bytes=12 << 20),
        cost_estimate=pl.CostEstimate(
            flops=weights.size, bytes_accessed=7 * weights.size, transcendentals=0
        ),
        name="other_step",
    )(rep, in_hbm(weights), in_hbm(momentum))


def gradient_products(unit, cot, low, hid):
    fed = lax.dot_general(low[: 4 * hid, :], unit[...], NT, preferred_element_type=jnp.float32)
    gate, upward = fed[: 2 * hid], fed[2 * hid :]
    back = lax.dot_general(low[4 * hid :, :], cot[...], NT, preferred_element_type=jnp.float32)
    sigma = jax.nn.sigmoid(gate)
    activated = gate * sigma
    hidden = (activated * upward).astype(jnp.bfloat16)
    gate_back = (back * upward * sigma * (1.0 + gate * (1.0 - sigma))).astype(jnp.bfloat16)
    up_back = (back * activated).astype(jnp.bfloat16)
    pairs = ((gate_back, unit), (up_back, unit), (hidden, cot))
    return [jnp.dot(left, right[...], preferred_element_type=jnp.float32) for left, right in pairs]


def early_body(slots, rep, *refs):
    keys, cots = refs[:slots], refs[slots : 2 * slots]
    weights, momentum, low_par, base_par, so_far, low, unit, cot = refs[2 * slots :]
    rows = keys[0].shape[0]
    hid = weights.shape[2]
    for s in range(slots):
        here = pl.ds(s * rows, rows)
        unit[here, :] = unit_rows(keys[s][...])
        cot[here, :] = cots[s][...]
    for m in range(3):
        low[pl.ds(2 * m * hid, hid), :] = weights[0, m].astype(jnp.bfloat16)
        low[pl.ds((2 * m + 1) * hid, hid), :] = low_par[0, m]
    for m, grad in enumerate(gradient_products(unit, cot, low, hid)):
        own, par = pl.ds(2 * m * hid, hid), pl.ds((2 * m + 1) * hid, hid)
        so_far[own, :] = weights[0, m] - (momentum_decay * momentum[0, m] + grad[:hid])
        so_far[par, :] = base_par[0, m] - grad[hid:]


def early_step(head, rep, keys, cots, weights, momentum, low_par, base_par):
    slots = len(keys)
    rows = keys[0].shape[0]
    heads, _, hid, width = low_par.shape
    block = (1, 3, hid, width)
    token_spec = pl.BlockSpec((rows, width), lambda i, rep: (0, head))
    own_spec = pl.BlockSpec(block, lambda i, rep: (rep[0] * heads + head, 0, 0, 0))
    par_spec = pl.BlockSpec(block, lambda i, rep: (head, 0, 0, 0))
    made_spec = pl.BlockSpec((6 * hid, width), lambda i, rep: (0, 0))
    return pl.pallas_call(
        functools.partial(early_body, slots),
        out_shape=(
            jax.ShapeDtypeStruct((6 * hid, width), jnp.float32),
            jax.ShapeDtypeStruct((6 * hid, width), jnp.bfloat16),
        ),
        grid_spec=pltpu.PrefetchScalarGridSpec(
            num_scalar_prefetch=1,
            grid=(1,),
            in_specs=[token_spec] * (2 * slots) + [own_spec] * 2 + [par_spec] * 2,
            out_specs=(made_spec, made_spec),
            scratch_shapes=[
                pltpu.VMEM((slots * rows, width), jnp.bfloat16),
                pltpu.VMEM((slots * rows, width), jnp.bfloat16),
            ],
        ),
        compiler_params=pltpu.CompilerParams(vmem_limit_bytes=20 << 20),
        cost_estimate=pl.CostEstimate(
            flops=24 * slots * rows * hid * width,
            bytes_accessed=60 * hid * width,
            transcendentals=0,
        ),
        name="early_step",
    )(rep, *map(in_hbm, (*keys, *cots, weights, momentum)), low_par, base_par)


def last_body(key, cotangent, so_far, low, new_own, new_par, new_low, unit):
    hid = so_far.shape[0] // 6
    unit[...] = unit_rows(key[...])
    for m, grad in enumerate(gradient_products(unit, cotangent, low, hid)):
        fresh_own = so_far[pl.ds(2 * m * hid, hid), :] - grad[:hid]
        fresh_par = so_far[pl.ds((2 * m + 1) * hid, hid), :] - grad[hid:]
        new_own[0, m] = fresh_own
        new_par[0, m] = fresh_par
        new_low[pl.ds(2 * m * hid, hid), :] = fresh_own.astype(jnp.bfloat16)
        new_low[pl.ds((2 * m + 1) * hid, hid), :] = fresh_par.astype(jnp.bfloat16)


def last_step(head, key, cotangent, so_far, low):
    rows = key.shape[0]
    total, width = low.shape
    hid = total // 6
    token_spec = pl.BlockSpec((rows, width), lambda i: (0, head))
    made_spec = pl.BlockSpec((total, width), lambda i: (0, 0))
    block = (1, 3, hid, width)
    new_spec = pl.BlockSpec(block, lambda i: (0, 0, 0, 0))
    fresh = pltpu.HBM(block, jnp.float32)
    return pl.pallas_call(
        last_body,
        out_shape=(fresh, fresh, jax.ShapeDtypeStruct((total, width), jnp.bfloat16)),
        grid=(1,),
        in_specs=[token_spec, token_spec, made_spec, made_spec],
        out_specs=(new_spec, new_spec, made_spec),
        scratch_shapes=[pltpu.VMEM((rows, width), jnp.bfloat16)],
        compiler_params=pltpu.CompilerParams(vmem_limit_bytes=16 << 20),
        cost_estimate=pl.CostEstimate(
            flops=4 * rows * total * width, bytes_accessed=12 * total * width, transcendentals=0
        ),
        name="last_step",
    )(key, cotangent, so_far, low)


def apply_body(query, low, *refs):
    hid = low.shape[0] // 6
    unit = unit_rows(query[...])
    gate = lax.dot_general(unit, low[: 2 * hid, :], NT, preferred_element_type=jnp.float32)
    upward = lax.dot_general(
        unit, low[2 * hid : 4 * hid, :], NT, preferred_element_type=jnp.float32
    )
    hidden = (gate * jax.nn.sigmoid(gate) * upward).astype(jnp.bfloat16)
    made = jnp.dot(hidden, low[4 * hid :, :], preferred_element_type=jnp.float32)
    if len(refs) > 1:
        made = made + refs[0][...]
    refs[-1][...] = made.astype(refs[-1].dtype)


def apply_step(query, low, dtype, *more):
    rows, width = query.shape
    total = low.shape[0]
    whole = pl.BlockSpec((rows, width), lambda i: (0, 0))
    return pl.pallas_call(
        apply_body,
        out_shape=jax.ShapeDtypeStruct((rows, width), dtype),
        grid=(1,),
        in_specs=[whole, pl.BlockSpec((total, width), lambda i: (0, 0))]
        + [whole] * len(more),
        out_specs=whole,
        compiler_params=pltpu.CompilerParams(vmem_limit_bytes=8 << 20),
        cost_estimate=pl.CostEstimate(
            flops=2 * rows * total * width, bytes_accessed=2 * total * width, transcendentals=0
        ),
        name="apply_step",
    )(query, low, *more)


def output_body(kept, moved, *refs):
    refs[-1][...] = (kept[...] + moved[...].astype(jnp.float32)).astype(jnp.bfloat16)


def output_step(head, heads, kept, moved, before):
    rows, width = kept.shape
    whole = pl.BlockSpec((rows, width), lambda i: (0, 0))
    more = () if before is None else (before,)
    return pl.pallas_call(
        output_body,
        out_shape=pltpu.HBM((rows, heads * width), jnp.bfloat16),
        grid=(1,),
        in_specs=[whole, whole] + [pl.BlockSpec(memory_space=pl.ANY)] * len(more),
        out_specs=pl.BlockSpec((rows, width), lambda i: (0, head)),
        input_output_aliases={2: 0} if more else {},
        compiler_params=pltpu.CompilerParams(vmem_limit_bytes=4 << 20),
        cost_estimate=pl.CostEstimate(
            flops=rows * width, bytes_accessed=8 * rows * width, transcendentals=0
        ),
        name="output_step",
    )(kept, moved, *more)


def attend_body(token_scale, first, key_own, key_prior, value_own, cot_prior, rate_prior, *refs):
    heads = len(refs) // 2
    asked, outs = refs[:heads], refs[heads:]
    width = asked[0].shape[1]
    allowed = jnp.where(first[0] != 0, -jnp.inf, 0.0).astype(jnp.float32)
    for h in range(heads):
        columns = slice(h * width, (h + 1) * width)
        part = asked[h][...]
        near = lax.dot_general(part, key_own[:, columns], NT, preferred_element_type=jnp.float32)
        far = lax.dot_general(part, key_prior[:, columns], NT, preferred_element_type=jnp.float32)
        near = near * width ** (-0.5)
        far = far * width ** (-0.5) + allowed
        peak = jnp.maximum(
            jnp.max(near, axis=-1, keepdims=True), jnp.max(far, axis=-1, keepdims=True)
        )
        near = jnp.exp(near - peak)
        far = jnp.exp(far - peak)
        total = jnp.sum(near, axis=-1, keepdims=True) + jnp.sum(far, axis=-1, keepdims=True)
        rate = -(rate_prior[h] * token_scale)
        near = (near / total).astype(jnp.bfloat16)
        far = (far / total / rate).astype(jnp.bfloat16)
        outs[h][...] = jnp.dot(
            near, value_own[:, columns], preferred_element_type=jnp.float32
        ) + jnp.dot(far, cot_prior[:, columns], preferred_element_type=jnp.float32)


def attend_step(token_scale, first, key_own, key_prior, value_own, cot_prior, rate_prior, asked):
    rows, columns = key_own.shape
    made = tuple(jax.ShapeDtypeStruct(query.shape, jnp.float32) for query in asked)
    return pl.pallas_call(
        functools.partial(attend_body, token_scale),
        out_shape=made,
        in_specs=[pl.BlockSpec(memory_space=pltpu.SMEM)] + [pl.BlockSpec()] * (5 + len(asked)),
        compiler_params=pltpu.CompilerParams(vmem_limit_bytes=8 << 20),
        cost_estimate=pl.CostEstimate(
            flops=8 * rows * rows * columns, bytes_accessed=14 * rows * columns, transcendentals=0
        ),
        name="attend_step",
    )(first, *map(in_hbm, (key_own, key_prior, value_own, cot_prior)), rate_prior, *asked)


def tokens_travel(queries, key_vectors, values, learn_rates, fast_weights, momentum):
    width = fast_weights.shape[3]
    slots = lax.axis_size("ctx")
    per_rep = fast_weights.shape[0] // 2
    rep_index = lax.axis_index("rep")
    start = rep_index * per_rep
    token_scale = float(slots * queries.shape[0]) ** (-0.5)

    def hop(value, axis="ctx"):
        return ring(value, axis)

    rep = rep_index.reshape(1)
    value_own, cot = cotangent_step(token_scale, rep, values, learn_rates)
    heads = range(per_rep)
    keys, cots = [columns_step(rep, key_vectors)], [cot]
    asked = [[lax.dynamic_slice_in_dim(queries, (start + h) * width, width, 1) for h in heads]]
    for _ in range(1, slots):
        keys.append(hop(keys[-1]))
        cots.append(hop(cots[-1]))
    rate_prior = hop(lax.dynamic_slice_in_dim(learn_rates, start, per_rep, 0)[:, None, :])
    low_other, base_other = other_step(rep, fast_weights, momentum)
    low_par = hop(low_other, "rep")
    base_par = hop(base_other, "rep")
    for _ in range(1, slots):
        asked.append([hop(asked[-1][h]) for h in heads])
    first = (lax.axis_index("ctx") == 0).astype(jnp.int32).reshape(1)
    attended = attend_step(
        token_scale, first, keys[0], keys[1], value_own, cots[1], rate_prior, asked[0]
    )
    early = []
    for h in heads:
        early.append(
            early_step(
                h, rep, keys[:-1], cots[:-1], fast_weights, momentum, low_par, base_par
            )
        )
    fresh = []
    for h in heads:
        fresh.append(last_step(h, keys[-1], cots[-1], *early[h]))
    lows = [new[2] for new in fresh]
    moving = []
    for step in range(1, slots):
        if step == 1:
            sent = [apply_step(asked[step][h], lows[h], jnp.bfloat16) for h in heads]
        else:
            made = [apply_step(asked[step][h], lows[h], jnp.float32) for h in heads]
            sent = [
                (made[h] + moving[h].astype(jnp.float32)).astype(jnp.bfloat16) for h in heads
            ]
        moving = [hop(sent[h]) for h in heads]
    layer_output = None
    for h in heads:
        kept = apply_step(asked[0][h], lows[h], jnp.float32, attended[h])
        layer_output = output_step(h, per_rep, kept, moving[h], layer_output)
    returned = [hop(fresh[h][1], "rep") for h in heads]
    owned = [new[0] for new in fresh]
    fast_updated = jnp.where(
        rep_index == 0,
        jnp.concatenate([*owned, *returned], axis=0),
        jnp.concatenate([*returned, *owned], axis=0),
    )
    return (layer_output, fast_updated)


def on_device(queries, key_vectors, values, learn_rates, fast_weights, momentum):
    slots = lax.axis_size("ctx")
    fits = (
        lax.axis_size("rep") == 2
        and 2 <= slots <= 8
        and fast_weights.shape[0] % 2 == 0
        and fast_weights.shape[2] % 16 == 0
        and queries.shape[0] == 128
    )
    program = tokens_travel if fits else weights_travel
    return program(queries, key_vectors, values, learn_rates, fast_weights, momentum)


def solution(mesh):
    return jax.shard_map(
        on_device,
        mesh=mesh,
        in_specs=(
            P(("groups", "ctx"), "head"),
            P(("groups", "ctx"), "head"),
            P(("groups", "ctx"), "head"),
            P("head", ("groups", "ctx")),
            P(("groups", "head"), None, ("ctx", "rep"), None),
            P(("groups", "head"), None, ("ctx", "rep"), None),
        ),
        out_specs=(
            P(("groups", "ctx"), ("head", "rep")),
            P(("groups", "head"), None, ("ctx", "rep"), None),
        ),
        check_vma=False,
    )
```

```python
import functools

import jax
import jax.numpy as jnp
from jax import lax
from jax.experimental import pallas as pl
from jax.experimental.pallas import tpu as pltpu
from jax.sharding import PartitionSpec as P


epsilon = 1e-06
momentum_decay = 0.9
NT = (((1,), (1,)), ((), ()))


def passed_along(value, axis, steps):
    count = lax.axis_size(axis)
    initial, last = (max(0, -steps), min(count, count - steps))
    return lax.ppermute(value, axis, [(source, source + steps) for source in range(initial, last)])


def ring(value, axis, steps=1):
    count = lax.axis_size(axis)
    return lax.ppermute(value, axis, [(source, (source + steps) % count) for source in range(count)])


def unit_rows(tensor):
    widened = tensor.astype(jnp.float32)
    factor = lax.rsqrt(jnp.mean(widened * widened, axis=-1, keepdims=True) + epsilon)
    return (widened * factor).astype(jnp.bfloat16)


def swiglu_apply(inputs, weights):
    gate = jnp.einsum("thd,hrd->htr", inputs, weights[:, 0], preferred_element_type=jnp.float32)
    upward = jnp.einsum("thd,hrd->htr", inputs, weights[:, 1], preferred_element_type=jnp.float32)
    hidden = (jax.nn.silu(gate) * upward).astype(jnp.bfloat16)
    return jnp.einsum("htr,hrd->htd", hidden, weights[:, 2], preferred_element_type=jnp.float32)


def window_attention(query_own, key_own, value_own, key_prior, value_prior, first_block):
    tok_rows = query_own.shape[0]
    per_rep = query_own.shape[1]
    width = query_own.shape[2]
    block_rows = min(tok_rows, 512)
    block_count = tok_rows // block_rows
    key_window = jnp.concatenate([key_prior, key_own], axis=0)
    value_window = jnp.concatenate([value_prior, value_own], axis=0)
    score_scale = width ** (-0.5)
    position = jnp.arange(2 * tok_rows)
    valid = jnp.logical_or(position >= tok_rows, jnp.logical_not(first_block))
    query_blocks = query_own.reshape(block_count, block_rows, per_rep, width)

    def one_block(query_block):
        scores = (
            jnp.einsum("tad,sad->ats", query_block, key_window, preferred_element_type=jnp.float32)
            * score_scale
        )
        scores = jnp.where(valid[None, None, :], scores, -jnp.inf)
        peak = jnp.max(scores, axis=-1, keepdims=True)
        weights = jnp.exp(scores - peak)
        probs = (weights / jnp.sum(weights, axis=-1, keepdims=True)).astype(jnp.bfloat16)
        return jnp.einsum("ats,sad->tad", probs, value_window, preferred_element_type=jnp.float32)

    return lax.map(one_block, query_blocks).reshape(tok_rows, per_rep, width)


def weights_travel(queries, key_vectors, values, learn_rates, fast_weights, momentum):
    tok_rows = queries.shape[0]
    head_count = fast_weights.shape[0]
    width = fast_weights.shape[3]
    rep_count = lax.axis_size("rep")
    per_rep = head_count // rep_count
    rep_index = lax.axis_index("rep")
    ctx_index = lax.axis_index("ctx")
    total_tokens = tok_rows * lax.axis_size("ctx")
    query_heads = queries.reshape(tok_rows, head_count, width)
    key_heads = key_vectors.reshape(tok_rows, head_count, width)
    value_heads = values.reshape(tok_rows, head_count, width)
    query_unit = unit_rows(query_heads)
    key_unit = unit_rows(key_heads)
    token_scale = float(total_tokens) ** (-0.5)
    cotangent = (
        -(learn_rates.T[:, :, None] * token_scale) * value_heads.astype(jnp.float32)
    ).astype(jnp.bfloat16)
    weight_rows = lax.all_gather(fast_weights.astype(jnp.bfloat16), "ctx", axis=2, tiled=True)
    gate = jnp.einsum(
        "thd,hrd->htr", key_unit, weight_rows[:, 0], preferred_element_type=jnp.float32
    )
    upward = jnp.einsum(
        "thd,hrd->htr", key_unit, weight_rows[:, 1], preferred_element_type=jnp.float32
    )
    back = jnp.einsum(
        "thd,hrd->htr", cotangent, weight_rows[:, 2], preferred_element_type=jnp.float32
    )
    sigma = jax.nn.sigmoid(gate)
    activated = jax.nn.silu(gate)
    hidden = (activated * upward).astype(jnp.bfloat16)
    gate_back = (back * upward * sigma * (1.0 + gate * (1.0 - sigma))).astype(jnp.bfloat16)
    up_back = (back * activated).astype(jnp.bfloat16)
    grad_gate = jnp.einsum("htr,thd->hrd", gate_back, key_unit, preferred_element_type=jnp.float32)
    grad_up = jnp.einsum("htr,thd->hrd", up_back, key_unit, preferred_element_type=jnp.float32)
    grad_down = jnp.einsum("htr,thd->hrd", hidden, cotangent, preferred_element_type=jnp.float32)
    gradient = jnp.stack([grad_gate, grad_up, grad_down], axis=1)
    share = lax.psum_scatter(
        gradient.astype(jnp.bfloat16), "ctx", scatter_dimension=2, tiled=True
    ).astype(jnp.float32)
    fast_updated = fast_weights - (momentum_decay * momentum + share)
    new_rows = lax.all_gather(fast_updated.astype(jnp.bfloat16), "ctx", axis=2, tiled=True)
    own_start = rep_index * per_rep
    partial_out = swiglu_apply(query_unit, new_rows)
    traded = lax.all_to_all(
        partial_out.astype(jnp.bfloat16), "rep", split_axis=0, concat_axis=0, tiled=True
    ).astype(partial_out.dtype)
    fast_out = jnp.sum(traded.reshape(rep_count, per_rep, tok_rows, width), axis=0)
    attend_query = lax.dynamic_slice_in_dim(query_heads, own_start, per_rep, 1)
    attend_key = lax.dynamic_slice_in_dim(key_heads, own_start, per_rep, 1)
    attend_value = lax.dynamic_slice_in_dim(value_heads, own_start, per_rep, 1)
    key_prior, value_prior = passed_along((attend_key, attend_value), "ctx", 1)
    attended = window_attention(
        attend_query, attend_key, attend_value, key_prior, value_prior, ctx_index == 0
    )
    combined = attended + jnp.transpose(fast_out, (1, 0, 2))
    layer_output = combined.astype(jnp.bfloat16).reshape(tok_rows, per_rep * width)
    return (layer_output, fast_updated)


def in_hbm(value):
    return pltpu.with_memory_space_constraint(value, pltpu.HBM)


def columns_body(rep, whole, out, semaphore):
    columns = out.shape[1]
    taken = whole.at[:, pl.ds(pl.multiple_of(rep[0] * columns, columns), columns)]
    copy = pltpu.make_async_copy(taken, out, semaphore)
    copy.start()
    copy.wait()


def columns_step(rep, whole):
    rows, columns = whole.shape[0], whole.shape[1] // 2
    return pl.pallas_call(
        columns_body,
        out_shape=jax.ShapeDtypeStruct((rows, columns), whole.dtype),
        in_specs=[pl.BlockSpec(memory_space=pltpu.SMEM), pl.BlockSpec(memory_space=pl.ANY)],
        out_specs=pl.BlockSpec(memory_space=pltpu.VMEM),
        scratch_shapes=[pltpu.SemaphoreType.DMA],
        compiler_params=pltpu.CompilerParams(vmem_limit_bytes=4 << 20),
        cost_estimate=pl.CostEstimate(
            flops=0, bytes_accessed=4 * rows * columns, transcendentals=0
        ),
        name="columns_step",
    )(rep, in_hbm(whole))


def cotangent_body(token_scale, rep, values, rates, out_raw, out):
    heads = rates.shape[0] // 2
    rows, columns = out.shape
    width = columns // heads
    for h in range(heads):
        rate = -(rates[pl.ds(rep[0] * heads + h, 1), :] * token_scale)
        rate = jnp.transpose(jnp.broadcast_to(rate, (rows, rows)))[:, :1]
        part = values[:, h * width : (h + 1) * width]
        out_raw[:, h * width : (h + 1) * width] = part
        out[:, h * width : (h + 1) * width] = (rate * part.astype(jnp.float32)).astype(jnp.bfloat16)


def cotangent_step(token_scale, rep, values, rates):
    rows, columns = values.shape[0], values.shape[1] // 2
    made = jax.ShapeDtypeStruct((rows, columns), jnp.bfloat16)
    whole = pl.BlockSpec((rows, columns), lambda i, rep: (0, 0))
    return pl.pallas_call(
        functools.partial(cotangent_body, token_scale),
        out_shape=(made, made),
        grid_spec=pltpu.PrefetchScalarGridSpec(
            num_scalar_prefetch=1,
            grid=(1,),
            in_specs=[
                pl.BlockSpec((rows, columns), lambda i, rep: (0, rep[0])),
                pl.BlockSpec(rates.shape, lambda i, rep: (0, 0)),
            ],
            out_specs=(whole, whole),
        ),
        compiler_params=pltpu.CompilerParams(vmem_limit_bytes=8 << 20),
        cost_estimate=pl.CostEstimate(
            flops=2 * rows * columns, bytes_accessed=6 * rows * columns, transcendentals=0
        ),
        name="cotangent_step",
    )(rep, in_hbm(values), in_hbm(rates))


def other_body(rep, weights, momentum, low, base):
    current = weights[...]
    low[...] = current.astype(jnp.bfloat16)
    base[...] = current - momentum_decay * momentum[...]


def other_step(rep, weights, momentum):
    heads = weights.shape[0] // 2
    block = (1,) + weights.shape[1:]
    made = (heads,) + weights.shape[1:]
    taken = pl.BlockSpec(block, lambda h, rep: ((1 - rep[0]) * heads + h, 0, 0, 0))
    given = pl.BlockSpec(block, lambda h, rep: (h, 0, 0, 0))
    return pl.pallas_call(
        other_body,
        out_shape=(pltpu.HBM(made, jnp.bfloat16), pltpu.HBM(made, jnp.float32)),
        grid_spec=pltpu.PrefetchScalarGridSpec(
            num_scalar_prefetch=1,
            grid=(heads,),
            in_specs=[taken, taken],
            out_specs=(given, given),
        ),
        compiler_params=pltpu.CompilerParams(vmem_limit_bytes=12 << 20),
        cost_estimate=pl.CostEstimate(
            flops=weights.size, bytes_accessed=7 * weights.size, transcendentals=0
        ),
        name="other_step",
    )(rep, in_hbm(weights), in_hbm(momentum))


def gradient_products(unit, cot, low, hid):
    fed = lax.dot_general(low[: 4 * hid, :], unit[...], NT, preferred_element_type=jnp.float32)
    gate, upward = fed[: 2 * hid], fed[2 * hid :]
    back = lax.dot_general(low[4 * hid :, :], cot[...], NT, preferred_element_type=jnp.float32)
    sigma = jax.nn.sigmoid(gate)
    activated = gate * sigma
    hidden = (activated * upward).astype(jnp.bfloat16)
    gate_back = (back * upward * sigma * (1.0 + gate * (1.0 - sigma))).astype(jnp.bfloat16)
    up_back = (back * activated).astype(jnp.bfloat16)
    pairs = ((gate_back, unit), (up_back, unit), (hidden, cot))
    return [jnp.dot(left, right[...], preferred_element_type=jnp.float32) for left, right in pairs]


def early_body(slots, rep, *refs):
    keys, cots = refs[:slots], refs[slots : 2 * slots]
    weights, momentum, low_par, base_par, so_far, low, unit, cot = refs[2 * slots :]
    rows = keys[0].shape[0]
    hid = weights.shape[2]
    for s in range(slots):
        here = pl.ds(s * rows, rows)
        unit[here, :] = unit_rows(keys[s][...])
        cot[here, :] = cots[s][...]
    for m in range(3):
        low[pl.ds(2 * m * hid, hid), :] = weights[0, m].astype(jnp.bfloat16)
        low[pl.ds((2 * m + 1) * hid, hid), :] = low_par[0, m]
    for m, grad in enumerate(gradient_products(unit, cot, low, hid)):
        own, par = pl.ds(2 * m * hid, hid), pl.ds((2 * m + 1) * hid, hid)
        so_far[own, :] = weights[0, m] - (momentum_decay * momentum[0, m] + grad[:hid])
        so_far[par, :] = base_par[0, m] - grad[hid:]


def early_step(head, rep, keys, cots, weights, momentum, low_par, base_par):
    slots = len(keys)
    rows = keys[0].shape[0]
    heads, _, hid, width = low_par.shape
    block = (1, 3, hid, width)
    token_spec = pl.BlockSpec((rows, width), lambda i, rep: (0, head))
    own_spec = pl.BlockSpec(block, lambda i, rep: (rep[0] * heads + head, 0, 0, 0))
    par_spec = pl.BlockSpec(block, lambda i, rep: (head, 0, 0, 0))
    made_spec = pl.BlockSpec((6 * hid, width), lambda i, rep: (0, 0))
    return pl.pallas_call(
        functools.partial(early_body, slots),
        out_shape=(
            jax.ShapeDtypeStruct((6 * hid, width), jnp.float32),
            jax.ShapeDtypeStruct((6 * hid, width), jnp.bfloat16),
        ),
        grid_spec=pltpu.PrefetchScalarGridSpec(
            num_scalar_prefetch=1,
            grid=(1,),
            in_specs=[token_spec] * (2 * slots) + [own_spec] * 2 + [par_spec] * 2,
            out_specs=(made_spec, made_spec),
            scratch_shapes=[
                pltpu.VMEM((slots * rows, width), jnp.bfloat16),
                pltpu.VMEM((slots * rows, width), jnp.bfloat16),
            ],
        ),
        compiler_params=pltpu.CompilerParams(vmem_limit_bytes=20 << 20),
        cost_estimate=pl.CostEstimate(
            flops=24 * slots * rows * hid * width,
            bytes_accessed=60 * hid * width,
            transcendentals=0,
        ),
        name="early_step",
    )(rep, *map(in_hbm, (*keys, *cots, weights, momentum)), low_par, base_par)


def last_body(key, cotangent, so_far, low, new_own, new_par, new_low, unit):
    hid = so_far.shape[0] // 6
    unit[...] = unit_rows(key[...])
    for m, grad in enumerate(gradient_products(unit, cotangent, low, hid)):
        fresh_own = so_far[pl.ds(2 * m * hid, hid), :] - grad[:hid]
        fresh_par = so_far[pl.ds((2 * m + 1) * hid, hid), :] - grad[hid:]
        new_own[0, m] = fresh_own
        new_par[0, m] = fresh_par
        new_low[pl.ds(2 * m * hid, hid), :] = fresh_own.astype(jnp.bfloat16)
        new_low[pl.ds((2 * m + 1) * hid, hid), :] = fresh_par.astype(jnp.bfloat16)


def last_step(head, key, cotangent, so_far, low):
    rows = key.shape[0]
    total, width = low.shape
    hid = total // 6
    token_spec = pl.BlockSpec((rows, width), lambda i: (0, head))
    made_spec = pl.BlockSpec((total, width), lambda i: (0, 0))
    block = (1, 3, hid, width)
    new_spec = pl.BlockSpec(block, lambda i: (0, 0, 0, 0))
    fresh = pltpu.HBM(block, jnp.float32)
    return pl.pallas_call(
        last_body,
        out_shape=(fresh, fresh, jax.ShapeDtypeStruct((total, width), jnp.bfloat16)),
        grid=(1,),
        in_specs=[token_spec, token_spec, made_spec, made_spec],
        out_specs=(new_spec, new_spec, made_spec),
        scratch_shapes=[pltpu.VMEM((rows, width), jnp.bfloat16)],
        compiler_params=pltpu.CompilerParams(vmem_limit_bytes=16 << 20),
        cost_estimate=pl.CostEstimate(
            flops=4 * rows * total * width, bytes_accessed=12 * total * width, transcendentals=0
        ),
        name="last_step",
    )(key, cotangent, so_far, low)


def apply_body(query, low, *refs):
    hid = low.shape[0] // 6
    unit = unit_rows(query[...])
    gate = lax.dot_general(unit, low[: 2 * hid, :], NT, preferred_element_type=jnp.float32)
    upward = lax.dot_general(
        unit, low[2 * hid : 4 * hid, :], NT, preferred_element_type=jnp.float32
    )
    hidden = (gate * jax.nn.sigmoid(gate) * upward).astype(jnp.bfloat16)
    made = jnp.dot(hidden, low[4 * hid :, :], preferred_element_type=jnp.float32)
    if len(refs) > 1:
        made = made + refs[0][...]
    refs[-1][...] = made.astype(refs[-1].dtype)


def apply_step(query, low, dtype, *more):
    rows, width = query.shape
    total = low.shape[0]
    whole = pl.BlockSpec((rows, width), lambda i: (0, 0))
    return pl.pallas_call(
        apply_body,
        out_shape=jax.ShapeDtypeStruct((rows, width), dtype),
        grid=(1,),
        in_specs=[whole, pl.BlockSpec((total, width), lambda i: (0, 0))]
        + [whole] * len(more),
        out_specs=whole,
        compiler_params=pltpu.CompilerParams(vmem_limit_bytes=8 << 20),
        cost_estimate=pl.CostEstimate(
            flops=2 * rows * total * width, bytes_accessed=2 * total * width, transcendentals=0
        ),
        name="apply_step",
    )(query, low, *more)


def output_body(kept, moved, *refs):
    refs[-1][...] = (kept[...] + moved[...].astype(jnp.float32)).astype(jnp.bfloat16)


def output_step(head, heads, kept, moved, before):
    rows, width = kept.shape
    more = () if before is None else (before,)
    return pl.pallas_call(
        output_body,
        out_shape=pltpu.HBM((rows, heads * width), jnp.bfloat16),
        grid=(1,),
        in_specs=[pl.BlockSpec(memory_space=pltpu.VMEM)] * 2
        + [pl.BlockSpec(memory_space=pl.ANY)] * len(more),
        out_specs=pl.BlockSpec((rows, width), lambda i: (0, head)),
        input_output_aliases={2: 0} if more else {},
        compiler_params=pltpu.CompilerParams(vmem_limit_bytes=4 << 20),
        cost_estimate=pl.CostEstimate(
            flops=rows * width, bytes_accessed=8 * rows * width, transcendentals=0
        ),
        name="output_step",
    )(kept, moved, *more)


def attend_body(token_scale, first, key_own, key_prior, value_own, cot_prior, rate_prior, *refs):
    heads = len(refs) // 2
    asked, outs = refs[:heads], refs[heads:]
    width = asked[0].shape[1]
    allowed = jnp.where(first[0] != 0, -jnp.inf, 0.0).astype(jnp.float32)
    for h in range(heads):
        columns = slice(h * width, (h + 1) * width)
        part = asked[h][...]
        near = lax.dot_general(part, key_own[:, columns], NT, preferred_element_type=jnp.float32)
        far = lax.dot_general(part, key_prior[:, columns], NT, preferred_element_type=jnp.float32)
        near = near * width ** (-0.5)
        far = far * width ** (-0.5) + allowed
        peak = jnp.maximum(
            jnp.max(near, axis=-1, keepdims=True), jnp.max(far, axis=-1, keepdims=True)
        )
        near = jnp.exp(near - peak)
        far = jnp.exp(far - peak)
        total = jnp.sum(near, axis=-1, keepdims=True) + jnp.sum(far, axis=-1, keepdims=True)
        rate = -(rate_prior[h] * token_scale)
        near = (near / total).astype(jnp.bfloat16)
        far = (far / total / rate).astype(jnp.bfloat16)
        outs[h][...] = jnp.dot(
            near, value_own[:, columns], preferred_element_type=jnp.float32
        ) + jnp.dot(far, cot_prior[:, columns], preferred_element_type=jnp.float32)


def attend_step(token_scale, first, key_own, key_prior, value_own, cot_prior, rate_prior, asked):
    rows, columns = key_own.shape
    made = tuple(jax.ShapeDtypeStruct(query.shape, jnp.float32) for query in asked)
    return pl.pallas_call(
        functools.partial(attend_body, token_scale),
        out_shape=made,
        in_specs=[pl.BlockSpec(memory_space=pltpu.SMEM)] + [pl.BlockSpec()] * (5 + len(asked)),
        compiler_params=pltpu.CompilerParams(vmem_limit_bytes=8 << 20),
        cost_estimate=pl.CostEstimate(
            flops=8 * rows * rows * columns, bytes_accessed=14 * rows * columns, transcendentals=0
        ),
        name="attend_step",
    )(first, *map(in_hbm, (key_own, key_prior, value_own, cot_prior)), rate_prior, *asked)


def tokens_travel(queries, key_vectors, values, learn_rates, fast_weights, momentum):
    width = fast_weights.shape[3]
    slots = lax.axis_size("ctx")
    per_rep = fast_weights.shape[0] // 2
    rep_index = lax.axis_index("rep")
    start = rep_index * per_rep
    token_scale = float(slots * queries.shape[0]) ** (-0.5)

    def hop(value, axis="ctx", steps=-1):
        return ring(value, axis, steps)

    rep = rep_index.reshape(1)
    value_own, cot = cotangent_step(token_scale, rep, values, learn_rates)
    heads = range(per_rep)
    keys, cots = [columns_step(rep, key_vectors)], [cot]
    asked = [[lax.dynamic_slice_in_dim(queries, (start + h) * width, width, 1) for h in heads]]
    for _ in range(1, slots):
        keys.append(hop(keys[-1]))
        cots.append(hop(cots[-1]))
    rate_prior = hop(lax.dynamic_slice_in_dim(learn_rates, start, per_rep, 0)[:, None, :], steps=1)
    low_other, base_other = other_step(rep, fast_weights, momentum)
    low_par = hop(low_other, "rep")
    base_par = hop(base_other, "rep")
    for _ in range(1, slots):
        asked.append([hop(asked[-1][h]) for h in heads])
    first = (lax.axis_index("ctx") == 0).astype(jnp.int32).reshape(1)
    attended = attend_step(
        token_scale, first, keys[0], keys[-1], value_own, cots[-1], rate_prior, asked[0]
    )
    early = []
    for h in heads:
        early.append(
            early_step(
                h, rep, keys[:-1], cots[:-1], fast_weights, momentum, low_par, base_par
            )
        )
    fresh = []
    for h in heads:
        fresh.append(last_step(h, keys[-1], cots[-1], *early[h]))
    lows = [new[2] for new in fresh]
    moving = []
    for step in range(1, slots):
        made = []
        for h in heads:
            kind = jnp.bfloat16 if step == 1 else jnp.float32
            made.append(apply_step(asked[step][h], lows[h], kind))
        if step > 1:
            made = [
                (made[h] + moving[h].astype(jnp.float32)).astype(jnp.bfloat16) for h in heads
            ]
        moving = [hop(made[h]) for h in heads]
    layer_output = None
    for h in heads:
        kept = apply_step(asked[0][h], lows[h], jnp.float32, attended[h])
        layer_output = output_step(h, per_rep, kept, moving[h], layer_output)
    returned = [hop(fresh[h][1], "rep") for h in heads]
    owned = [new[0] for new in fresh]
    fast_updated = jnp.where(
        rep_index == 0,
        jnp.concatenate([*owned, *returned], axis=0),
        jnp.concatenate([*returned, *owned], axis=0),
    )
    return (layer_output, fast_updated)


def on_device(queries, key_vectors, values, learn_rates, fast_weights, momentum):
    slots = lax.axis_size("ctx")
    fits = (
        lax.axis_size("rep") == 2
        and 2 <= slots <= 8
        and fast_weights.shape[0] % 2 == 0
        and fast_weights.shape[2] % 16 == 0
        and queries.shape[0] == 128
    )
    program = tokens_travel if fits else weights_travel
    return program(queries, key_vectors, values, learn_rates, fast_weights, momentum)


def solution(mesh):
    return jax.shard_map(
        on_device,
        mesh=mesh,
        in_specs=(
            P(("groups", "ctx"), "head"),
            P(("groups", "ctx"), "head"),
            P(("groups", "ctx"), "head"),
            P("head", ("groups", "ctx")),
            P(("groups", "head"), None, ("ctx", "rep"), None),
            P(("groups", "head"), None, ("ctx", "rep"), None),
        ),
        out_specs=(
            P(("groups", "ctx"), ("head", "rep")),
            P(("groups", "head"), None, ("ctx", "rep"), None),
        ),
        check_vma=False,
    )
```

```python
import functools

import jax
import jax.numpy as jnp
from jax import lax
from jax.experimental import pallas as pl
from jax.experimental.pallas import tpu as pltpu
from jax.sharding import PartitionSpec as P


epsilon = 1e-06
momentum_decay = 0.9
NT = (((1,), (1,)), ((), ()))


def passed_along(value, axis, steps):
    count = lax.axis_size(axis)
    initial, last = (max(0, -steps), min(count, count - steps))
    return lax.ppermute(value, axis, [(source, source + steps) for source in range(initial, last)])


def ring(value, axis, order=None):
    order = order or range(lax.axis_size(axis))
    return lax.ppermute(value, axis, list(zip(order, (*order[1:], order[0]))))


def unit_rows(tensor):
    widened = tensor.astype(jnp.float32)
    factor = lax.rsqrt(jnp.mean(widened * widened, axis=-1, keepdims=True) + epsilon)
    return (widened * factor).astype(jnp.bfloat16)


def swiglu_apply(inputs, weights):
    gate = jnp.einsum("thd,hrd->htr", inputs, weights[:, 0], preferred_element_type=jnp.float32)
    upward = jnp.einsum("thd,hrd->htr", inputs, weights[:, 1], preferred_element_type=jnp.float32)
    hidden = (jax.nn.silu(gate) * upward).astype(jnp.bfloat16)
    return jnp.einsum("htr,hrd->htd", hidden, weights[:, 2], preferred_element_type=jnp.float32)


def window_attention(query_own, key_own, value_own, key_prior, value_prior, first_block):
    tok_rows = query_own.shape[0]
    per_rep = query_own.shape[1]
    width = query_own.shape[2]
    block_rows = min(tok_rows, 512)
    block_count = tok_rows // block_rows
    key_window = jnp.concatenate([key_prior, key_own], axis=0)
    value_window = jnp.concatenate([value_prior, value_own], axis=0)
    score_scale = width ** (-0.5)
    position = jnp.arange(2 * tok_rows)
    valid = jnp.logical_or(position >= tok_rows, jnp.logical_not(first_block))
    query_blocks = query_own.reshape(block_count, block_rows, per_rep, width)

    def one_block(query_block):
        scores = (
            jnp.einsum("tad,sad->ats", query_block, key_window, preferred_element_type=jnp.float32)
            * score_scale
        )
        scores = jnp.where(valid[None, None, :], scores, -jnp.inf)
        peak = jnp.max(scores, axis=-1, keepdims=True)
        weights = jnp.exp(scores - peak)
        probs = (weights / jnp.sum(weights, axis=-1, keepdims=True)).astype(jnp.bfloat16)
        return jnp.einsum("ats,sad->tad", probs, value_window, preferred_element_type=jnp.float32)

    return lax.map(one_block, query_blocks).reshape(tok_rows, per_rep, width)


def weights_travel(queries, key_vectors, values, learn_rates, fast_weights, momentum):
    tok_rows = queries.shape[0]
    head_count = fast_weights.shape[0]
    width = fast_weights.shape[3]
    rep_count = lax.axis_size("rep")
    per_rep = head_count // rep_count
    rep_index = lax.axis_index("rep")
    ctx_index = lax.axis_index("ctx")
    total_tokens = tok_rows * lax.axis_size("ctx")
    query_heads = queries.reshape(tok_rows, head_count, width)
    key_heads = key_vectors.reshape(tok_rows, head_count, width)
    value_heads = values.reshape(tok_rows, head_count, width)
    query_unit = unit_rows(query_heads)
    key_unit = unit_rows(key_heads)
    token_scale = float(total_tokens) ** (-0.5)
    cotangent = (
        -(learn_rates.T[:, :, None] * token_scale) * value_heads.astype(jnp.float32)
    ).astype(jnp.bfloat16)
    weight_rows = lax.all_gather(fast_weights.astype(jnp.bfloat16), "ctx", axis=2, tiled=True)
    gate = jnp.einsum(
        "thd,hrd->htr", key_unit, weight_rows[:, 0], preferred_element_type=jnp.float32
    )
    upward = jnp.einsum(
        "thd,hrd->htr", key_unit, weight_rows[:, 1], preferred_element_type=jnp.float32
    )
    back = jnp.einsum(
        "thd,hrd->htr", cotangent, weight_rows[:, 2], preferred_element_type=jnp.float32
    )
    sigma = jax.nn.sigmoid(gate)
    activated = jax.nn.silu(gate)
    hidden = (activated * upward).astype(jnp.bfloat16)
    gate_back = (back * upward * sigma * (1.0 + gate * (1.0 - sigma))).astype(jnp.bfloat16)
    up_back = (back * activated).astype(jnp.bfloat16)
    grad_gate = jnp.einsum("htr,thd->hrd", gate_back, key_unit, preferred_element_type=jnp.float32)
    grad_up = jnp.einsum("htr,thd->hrd", up_back, key_unit, preferred_element_type=jnp.float32)
    grad_down = jnp.einsum("htr,thd->hrd", hidden, cotangent, preferred_element_type=jnp.float32)
    gradient = jnp.stack([grad_gate, grad_up, grad_down], axis=1)
    share = lax.psum_scatter(
        gradient.astype(jnp.bfloat16), "ctx", scatter_dimension=2, tiled=True
    ).astype(jnp.float32)
    fast_updated = fast_weights - (momentum_decay * momentum + share)
    new_rows = lax.all_gather(fast_updated.astype(jnp.bfloat16), "ctx", axis=2, tiled=True)
    own_start = rep_index * per_rep
    partial_out = swiglu_apply(query_unit, new_rows)
    traded = lax.all_to_all(
        partial_out.astype(jnp.bfloat16), "rep", split_axis=0, concat_axis=0, tiled=True
    ).astype(partial_out.dtype)
    fast_out = jnp.sum(traded.reshape(rep_count, per_rep, tok_rows, width), axis=0)
    attend_query = lax.dynamic_slice_in_dim(query_heads, own_start, per_rep, 1)
    attend_key = lax.dynamic_slice_in_dim(key_heads, own_start, per_rep, 1)
    attend_value = lax.dynamic_slice_in_dim(value_heads, own_start, per_rep, 1)
    key_prior, value_prior = passed_along((attend_key, attend_value), "ctx", 1)
    attended = window_attention(
        attend_query, attend_key, attend_value, key_prior, value_prior, ctx_index == 0
    )
    combined = attended + jnp.transpose(fast_out, (1, 0, 2))
    layer_output = combined.astype(jnp.bfloat16).reshape(tok_rows, per_rep * width)
    return (layer_output, fast_updated)


def in_hbm(value):
    return pltpu.with_memory_space_constraint(value, pltpu.HBM)


def columns_body(rep, whole, out, semaphore):
    columns = out.shape[1]
    taken = whole.at[:, pl.ds(pl.multiple_of(rep[0] * columns, columns), columns)]
    copy = pltpu.make_async_copy(taken, out, semaphore)
    copy.start()
    copy.wait()


def columns_step(rep, whole):
    rows, columns = whole.shape[0], whole.shape[1] // 2
    return pl.pallas_call(
        columns_body,
        out_shape=jax.ShapeDtypeStruct((rows, columns), whole.dtype),
        in_specs=[pl.BlockSpec(memory_space=pltpu.SMEM), pl.BlockSpec(memory_space=pl.ANY)],
        out_specs=pl.BlockSpec(memory_space=pltpu.VMEM),
        scratch_shapes=[pltpu.SemaphoreType.DMA],
        compiler_params=pltpu.CompilerParams(vmem_limit_bytes=4 << 20),
        cost_estimate=pl.CostEstimate(
            flops=0, bytes_accessed=4 * rows * columns, transcendentals=0
        ),
        name="columns_step",
    )(rep, in_hbm(whole))


def cotangent_body(token_scale, rep, values, rates, out_raw, out):
    heads = rates.shape[0] // 2
    rows, columns = out.shape
    width = columns // heads
    for h in range(heads):
        rate = -(rates[pl.ds(rep[0] * heads + h, 1), :] * token_scale)
        rate = jnp.transpose(jnp.broadcast_to(rate, (rows, rows)))[:, :1]
        part = values[:, h * width : (h + 1) * width]
        out_raw[:, h * width : (h + 1) * width] = part
        out[:, h * width : (h + 1) * width] = (rate * part.astype(jnp.float32)).astype(jnp.bfloat16)


def cotangent_step(token_scale, rep, values, rates):
    rows, columns = values.shape[0], values.shape[1] // 2
    made = jax.ShapeDtypeStruct((rows, columns), jnp.bfloat16)
    whole = pl.BlockSpec((rows, columns), lambda i, rep: (0, 0))
    return pl.pallas_call(
        functools.partial(cotangent_body, token_scale),
        out_shape=(made, made),
        grid_spec=pltpu.PrefetchScalarGridSpec(
            num_scalar_prefetch=1,
            grid=(1,),
            in_specs=[
                pl.BlockSpec((rows, columns), lambda i, rep: (0, rep[0])),
                pl.BlockSpec(rates.shape, lambda i, rep: (0, 0)),
            ],
            out_specs=(whole, whole),
        ),
        compiler_params=pltpu.CompilerParams(vmem_limit_bytes=8 << 20),
        cost_estimate=pl.CostEstimate(
            flops=2 * rows * columns, bytes_accessed=6 * rows * columns, transcendentals=0
        ),
        name="cotangent_step",
    )(rep, in_hbm(values), in_hbm(rates))


def other_body(rep, weights, momentum, low, base):
    current = weights[...]
    low[...] = current.astype(jnp.bfloat16)
    base[...] = current - momentum_decay * momentum[...]


def other_step(rep, weights, momentum):
    heads = weights.shape[0] // 2
    block = (1,) + weights.shape[1:]
    made = (heads,) + weights.shape[1:]
    taken = pl.BlockSpec(block, lambda h, rep: ((1 - rep[0]) * heads + h, 0, 0, 0))
    given = pl.BlockSpec(block, lambda h, rep: (h, 0, 0, 0))
    return pl.pallas_call(
        other_body,
        out_shape=(pltpu.HBM(made, jnp.bfloat16), pltpu.HBM(made, jnp.float32)),
        grid_spec=pltpu.PrefetchScalarGridSpec(
            num_scalar_prefetch=1,
            grid=(heads,),
            in_specs=[taken, taken],
            out_specs=(given, given),
        ),
        compiler_params=pltpu.CompilerParams(vmem_limit_bytes=12 << 20),
        cost_estimate=pl.CostEstimate(
            flops=weights.size, bytes_accessed=7 * weights.size, transcendentals=0
        ),
        name="other_step",
    )(rep, in_hbm(weights), in_hbm(momentum))


def gradient_products(unit, cot, low, hid):
    fed = lax.dot_general(low[: 4 * hid, :], unit[...], NT, preferred_element_type=jnp.float32)
    gate, upward = fed[: 2 * hid], fed[2 * hid :]
    back = lax.dot_general(low[4 * hid :, :], cot[...], NT, preferred_element_type=jnp.float32)
    sigma = jax.nn.sigmoid(gate)
    activated = gate * sigma
    hidden = (activated * upward).astype(jnp.bfloat16)
    gate_back = (back * upward * sigma * (1.0 + gate * (1.0 - sigma))).astype(jnp.bfloat16)
    up_back = (back * activated).astype(jnp.bfloat16)
    pairs = ((gate_back, unit), (up_back, unit), (hidden, cot))
    return [jnp.dot(left, right[...], preferred_element_type=jnp.float32) for left, right in pairs]


def early_body(slots, rep, *refs):
    keys, cots = refs[:slots], refs[slots : 2 * slots]
    weights, momentum, low_par, base_par, so_far, low, unit, cot = refs[2 * slots :]
    rows = keys[0].shape[0]
    hid = weights.shape[2]
    for s in range(slots):
        here = pl.ds(s * rows, rows)
        unit[here, :] = unit_rows(keys[s][...])
        cot[here, :] = cots[s][...]
    for m in range(3):
        low[pl.ds(2 * m * hid, hid), :] = weights[0, m].astype(jnp.bfloat16)
        low[pl.ds((2 * m + 1) * hid, hid), :] = low_par[0, m]
    for m, grad in enumerate(gradient_products(unit, cot, low, hid)):
        own, par = pl.ds(2 * m * hid, hid), pl.ds((2 * m + 1) * hid, hid)
        so_far[own, :] = weights[0, m] - (momentum_decay * momentum[0, m] + grad[:hid])
        so_far[par, :] = base_par[0, m] - grad[hid:]


def early_step(head, rep, keys, cots, weights, momentum, low_par, base_par):
    slots = len(keys)
    rows = keys[0].shape[0]
    heads, _, hid, width = low_par.shape
    block = (1, 3, hid, width)
    token_spec = pl.BlockSpec((rows, width), lambda i, rep: (0, head))
    own_spec = pl.BlockSpec(block, lambda i, rep: (rep[0] * heads + head, 0, 0, 0))
    par_spec = pl.BlockSpec(block, lambda i, rep: (head, 0, 0, 0))
    made_spec = pl.BlockSpec((6 * hid, width), lambda i, rep: (0, 0))
    return pl.pallas_call(
        functools.partial(early_body, slots),
        out_shape=(
            (pltpu.HBM if head else jax.ShapeDtypeStruct)((6 * hid, width), jnp.float32),
            jax.ShapeDtypeStruct((6 * hid, width), jnp.bfloat16),
        ),
        grid_spec=pltpu.PrefetchScalarGridSpec(
            num_scalar_prefetch=1,
            grid=(1,),
            in_specs=[token_spec] * (2 * slots) + [own_spec] * 2 + [par_spec] * 2,
            out_specs=(made_spec, made_spec),
            scratch_shapes=[
                pltpu.VMEM((slots * rows, width), jnp.bfloat16),
                pltpu.VMEM((slots * rows, width), jnp.bfloat16),
            ],
        ),
        compiler_params=pltpu.CompilerParams(vmem_limit_bytes=20 << 20),
        cost_estimate=pl.CostEstimate(
            flops=24 * slots * rows * hid * width,
            bytes_accessed=60 * hid * width,
            transcendentals=0,
        ),
        name="early_step",
    )(rep, *map(in_hbm, (*keys, *cots, weights, momentum)), low_par, base_par)


def last_body(key, cotangent, so_far, low, new_own, new_par, new_low, unit):
    hid = so_far.shape[0] // 6
    unit[...] = unit_rows(key[...])
    for m, grad in enumerate(gradient_products(unit, cotangent, low, hid)):
        fresh_own = so_far[pl.ds(2 * m * hid, hid), :] - grad[:hid]
        fresh_par = so_far[pl.ds((2 * m + 1) * hid, hid), :] - grad[hid:]
        new_own[0, m] = fresh_own
        new_par[0, m] = fresh_par
        new_low[pl.ds(2 * m * hid, hid), :] = fresh_own.astype(jnp.bfloat16)
        new_low[pl.ds((2 * m + 1) * hid, hid), :] = fresh_par.astype(jnp.bfloat16)


def last_step(head, key, cotangent, so_far, low):
    rows = key.shape[0]
    total, width = low.shape
    hid = total // 6
    token_spec = pl.BlockSpec((rows, width), lambda i: (0, head))
    made_spec = pl.BlockSpec((total, width), lambda i: (0, 0))
    block = (1, 3, hid, width)
    new_spec = pl.BlockSpec(block, lambda i: (0, 0, 0, 0))
    fresh = pltpu.HBM(block, jnp.float32)
    return pl.pallas_call(
        last_body,
        out_shape=(fresh, fresh, jax.ShapeDtypeStruct((total, width), jnp.bfloat16)),
        grid=(1,),
        in_specs=[token_spec, token_spec, made_spec, made_spec],
        out_specs=(new_spec, new_spec, made_spec),
        scratch_shapes=[pltpu.VMEM((rows, width), jnp.bfloat16)],
        compiler_params=pltpu.CompilerParams(vmem_limit_bytes=16 << 20),
        cost_estimate=pl.CostEstimate(
            flops=4 * rows * total * width, bytes_accessed=12 * total * width, transcendentals=0
        ),
        name="last_step",
    )(key, cotangent, in_hbm(so_far) if head else so_far, low)


def apply_body(query, low, *refs):
    hid = low.shape[0] // 6
    unit = unit_rows(query[...])
    gate = lax.dot_general(unit, low[: 2 * hid, :], NT, preferred_element_type=jnp.float32)
    upward = lax.dot_general(
        unit, low[2 * hid : 4 * hid, :], NT, preferred_element_type=jnp.float32
    )
    hidden = (gate * jax.nn.sigmoid(gate) * upward).astype(jnp.bfloat16)
    made = jnp.dot(hidden, low[4 * hid :, :], preferred_element_type=jnp.float32)
    if len(refs) > 1:
        made = made + refs[0][...]
    refs[-1][...] = made.astype(refs[-1].dtype)


def apply_step(query, low, dtype, *more):
    rows, width = query.shape
    total = low.shape[0]
    whole = pl.BlockSpec((rows, width), lambda i: (0, 0))
    return pl.pallas_call(
        apply_body,
        out_shape=jax.ShapeDtypeStruct((rows, width), dtype),
        grid=(1,),
        in_specs=[whole, pl.BlockSpec((total, width), lambda i: (0, 0))]
        + [whole] * len(more),
        out_specs=whole,
        compiler_params=pltpu.CompilerParams(vmem_limit_bytes=8 << 20),
        cost_estimate=pl.CostEstimate(
            flops=2 * rows * total * width, bytes_accessed=2 * total * width, transcendentals=0
        ),
        name="apply_step",
    )(query, low, *more)


def output_body(kept, moved, *refs):
    refs[-1][...] = (kept[...] + moved[...].astype(jnp.float32)).astype(jnp.bfloat16)


def output_step(head, heads, kept, moved, before):
    rows, width = kept.shape
    more = () if before is None else (before,)
    return pl.pallas_call(
        output_body,
        out_shape=pltpu.HBM((rows, heads * width), jnp.bfloat16),
        grid=(1,),
        in_specs=[pl.BlockSpec(memory_space=pltpu.VMEM)] * 2
        + [pl.BlockSpec(memory_space=pl.ANY)] * len(more),
        out_specs=pl.BlockSpec((rows, width), lambda i: (0, head)),
        input_output_aliases={2: 0} if more else {},
        compiler_params=pltpu.CompilerParams(vmem_limit_bytes=4 << 20),
        cost_estimate=pl.CostEstimate(
            flops=rows * width, bytes_accessed=8 * rows * width, transcendentals=0
        ),
        name="output_step",
    )(kept, moved, *more)


def attend_body(token_scale, block_index, *refs):
    key_own, value_own, rate_prior = refs[:3]
    key_slots, cot_slots = refs[3:6], refs[6:9]
    heads = (len(refs) - 9) // 2
    asked, outs = refs[9 : 9 + heads], refs[9 + heads :]
    width = asked[0].shape[1]
    index = block_index[0]
    allowed = jnp.where(index == 0, -jnp.inf, 0.0).astype(jnp.float32)
    for h in range(heads):
        columns = slice(h * width, (h + 1) * width)
        key_prior, cot_prior = (
            jnp.where(
                index == 3,
                one[:, columns],
                jnp.where(index == 2, two[:, columns], three[:, columns]),
            )
            for one, two, three in (key_slots, cot_slots)
        )
        part = asked[h][...]
        near = lax.dot_general(part, key_own[:, columns], NT, preferred_element_type=jnp.float32)
        far = lax.dot_general(part, key_prior, NT, preferred_element_type=jnp.float32)
        near = near * width ** (-0.5)
        far = far * width ** (-0.5) + allowed
        peak = jnp.maximum(
            jnp.max(near, axis=-1, keepdims=True), jnp.max(far, axis=-1, keepdims=True)
        )
        near = jnp.exp(near - peak)
        far = jnp.exp(far - peak)
        total = jnp.sum(near, axis=-1, keepdims=True) + jnp.sum(far, axis=-1, keepdims=True)
        rate = -(rate_prior[h] * token_scale)
        near = (near / total).astype(jnp.bfloat16)
        far = (far / total / rate).astype(jnp.bfloat16)
        outs[h][...] = jnp.dot(
            near, value_own[:, columns], preferred_element_type=jnp.float32
        ) + jnp.dot(far, cot_prior, preferred_element_type=jnp.float32)


def attend_step(token_scale, block_index, keys, value_own, cots, rate_prior, asked):
    rows, columns = value_own.shape
    made = tuple(jax.ShapeDtypeStruct(query.shape, jnp.float32) for query in asked)
    return pl.pallas_call(
        functools.partial(attend_body, token_scale),
        out_shape=made,
        in_specs=[pl.BlockSpec(memory_space=pltpu.SMEM)] + [pl.BlockSpec()] * (9 + len(asked)),
        compiler_params=pltpu.CompilerParams(vmem_limit_bytes=10 << 20),
        cost_estimate=pl.CostEstimate(
            flops=8 * rows * rows * columns, bytes_accessed=20 * rows * columns, transcendentals=0
        ),
        name="attend_step",
    )(
        block_index,
        in_hbm(keys[0]),
        in_hbm(value_own),
        rate_prior,
        *map(in_hbm, (*keys[1:], *cots)),
        *asked,
    )


def tokens_travel(queries, key_vectors, values, learn_rates, fast_weights, momentum):
    width = fast_weights.shape[3]
    slots = lax.axis_size("ctx")
    per_rep = fast_weights.shape[0] // 2
    rep_index = lax.axis_index("rep")
    start = rep_index * per_rep
    token_scale = float(slots * queries.shape[0]) ** (-0.5)

    cycle = (0, 2, 3, 1)

    def hop(value, axis="ctx", order=cycle):
        return ring(value, axis, order if axis == "ctx" else None)

    rep = rep_index.reshape(1)
    value_own, cot = cotangent_step(token_scale, rep, values, learn_rates)
    heads = range(per_rep)
    keys, cots = [columns_step(rep, key_vectors)], [cot]
    asked = [[lax.dynamic_slice_in_dim(queries, (start + h) * width, width, 1) for h in heads]]
    for _ in range(1, slots):
        keys.append(hop(keys[-1]))
        cots.append(hop(cots[-1]))
    rate_prior = hop(
        lax.dynamic_slice_in_dim(learn_rates, start, per_rep, 0)[:, None, :], order=None
    )
    low_other, base_other = other_step(rep, fast_weights, momentum)
    low_par = hop(low_other, "rep")
    base_par = hop(base_other, "rep")
    for _ in range(1, slots):
        asked.append([hop(asked[-1][h]) for h in heads])
    block_index = lax.axis_index("ctx").reshape(1)
    attended = attend_step(
        token_scale, block_index, keys, value_own, cots[1:], rate_prior, asked[0]
    )
    early = []
    for h in heads:
        early.append(
            early_step(
                h, rep, keys[:-1], cots[:-1], fast_weights, momentum, low_par, base_par
            )
        )
    fresh = []
    for h in heads:
        fresh.append(last_step(h, keys[-1], cots[-1], *early[h]))
    lows = [new[2] for new in fresh]
    moving = []
    for step in range(1, slots):
        made = []
        for h in heads:
            kind = jnp.bfloat16 if step == 1 else jnp.float32
            made.append(apply_step(asked[step][h], lows[h], kind))
        if step > 1:
            made = [
                (made[h] + moving[h].astype(jnp.float32)).astype(jnp.bfloat16) for h in heads
            ]
        moving = [hop(made[h]) for h in heads]
    layer_output = None
    for h in heads:
        kept = apply_step(asked[0][h], lows[h], jnp.float32, attended[h])
        layer_output = output_step(h, per_rep, kept, moving[h], layer_output)
    returned = [hop(fresh[h][1], "rep") for h in heads]
    owned = [new[0] for new in fresh]
    fast_updated = jnp.where(
        rep_index == 0,
        jnp.concatenate([*owned, *returned], axis=0),
        jnp.concatenate([*returned, *owned], axis=0),
    )
    return (layer_output, fast_updated)


def on_device(queries, key_vectors, values, learn_rates, fast_weights, momentum):
    slots = lax.axis_size("ctx")
    fits = (
        lax.axis_size("rep") == 2
        and slots == 4
        and fast_weights.shape[0] == 4
        and fast_weights.shape[2] % 16 == 0
        and queries.shape[0] == 128
    )
    program = tokens_travel if fits else weights_travel
    return program(queries, key_vectors, values, learn_rates, fast_weights, momentum)


def solution(mesh):
    return jax.shard_map(
        on_device,
        mesh=mesh,
        in_specs=(
            P(("groups", "ctx"), "head"),
            P(("groups", "ctx"), "head"),
            P(("groups", "ctx"), "head"),
            P("head", ("groups", "ctx")),
            P(("groups", "head"), None, ("ctx", "rep"), None),
            P(("groups", "head"), None, ("ctx", "rep"), None),
        ),
        out_specs=(
            P(("groups", "ctx"), ("head", "rep")),
            P(("groups", "head"), None, ("ctx", "rep"), None),
        ),
        check_vma=False,
    )
```

```python
import functools

import jax
import jax.numpy as jnp
from jax import lax
from jax.experimental import pallas as pl
from jax.experimental.pallas import tpu as pltpu
from jax.sharding import PartitionSpec as P


epsilon = 1e-06
momentum_decay = 0.9
NT = (((1,), (1,)), ((), ()))


def passed_along(value, axis, steps):
    count = lax.axis_size(axis)
    initial, last = (max(0, -steps), min(count, count - steps))
    return lax.ppermute(value, axis, [(source, source + steps) for source in range(initial, last)])


def ring(value, axis, order=None):
    order = order or range(lax.axis_size(axis))
    return lax.ppermute(value, axis, list(zip(order, (*order[1:], order[0]))))


def unit_rows(tensor):
    widened = tensor.astype(jnp.float32)
    factor = lax.rsqrt(jnp.mean(widened * widened, axis=-1, keepdims=True) + epsilon)
    return (widened * factor).astype(jnp.bfloat16)


def swiglu_apply(inputs, weights):
    gate = jnp.einsum("thd,hrd->htr", inputs, weights[:, 0], preferred_element_type=jnp.float32)
    upward = jnp.einsum("thd,hrd->htr", inputs, weights[:, 1], preferred_element_type=jnp.float32)
    hidden = (jax.nn.silu(gate) * upward).astype(jnp.bfloat16)
    return jnp.einsum("htr,hrd->htd", hidden, weights[:, 2], preferred_element_type=jnp.float32)


def window_attention(query_own, key_own, value_own, key_prior, value_prior, first_block):
    tok_rows = query_own.shape[0]
    per_rep = query_own.shape[1]
    width = query_own.shape[2]
    block_rows = min(tok_rows, 512)
    block_count = tok_rows // block_rows
    key_window = jnp.concatenate([key_prior, key_own], axis=0)
    value_window = jnp.concatenate([value_prior, value_own], axis=0)
    score_scale = width ** (-0.5)
    position = jnp.arange(2 * tok_rows)
    valid = jnp.logical_or(position >= tok_rows, jnp.logical_not(first_block))
    query_blocks = query_own.reshape(block_count, block_rows, per_rep, width)

    def one_block(query_block):
        scores = (
            jnp.einsum("tad,sad->ats", query_block, key_window, preferred_element_type=jnp.float32)
            * score_scale
        )
        scores = jnp.where(valid[None, None, :], scores, -jnp.inf)
        peak = jnp.max(scores, axis=-1, keepdims=True)
        weights = jnp.exp(scores - peak)
        probs = (weights / jnp.sum(weights, axis=-1, keepdims=True)).astype(jnp.bfloat16)
        return jnp.einsum("ats,sad->tad", probs, value_window, preferred_element_type=jnp.float32)

    return lax.map(one_block, query_blocks).reshape(tok_rows, per_rep, width)


def weights_travel(queries, key_vectors, values, learn_rates, fast_weights, momentum):
    tok_rows = queries.shape[0]
    head_count = fast_weights.shape[0]
    width = fast_weights.shape[3]
    rep_count = lax.axis_size("rep")
    per_rep = head_count // rep_count
    rep_index = lax.axis_index("rep")
    ctx_index = lax.axis_index("ctx")
    total_tokens = tok_rows * lax.axis_size("ctx")
    query_heads = queries.reshape(tok_rows, head_count, width)
    key_heads = key_vectors.reshape(tok_rows, head_count, width)
    value_heads = values.reshape(tok_rows, head_count, width)
    query_unit = unit_rows(query_heads)
    key_unit = unit_rows(key_heads)
    token_scale = float(total_tokens) ** (-0.5)
    cotangent = (
        -(learn_rates.T[:, :, None] * token_scale) * value_heads.astype(jnp.float32)
    ).astype(jnp.bfloat16)
    weight_rows = lax.all_gather(fast_weights.astype(jnp.bfloat16), "ctx", axis=2, tiled=True)
    gate = jnp.einsum(
        "thd,hrd->htr", key_unit, weight_rows[:, 0], preferred_element_type=jnp.float32
    )
    upward = jnp.einsum(
        "thd,hrd->htr", key_unit, weight_rows[:, 1], preferred_element_type=jnp.float32
    )
    back = jnp.einsum(
        "thd,hrd->htr", cotangent, weight_rows[:, 2], preferred_element_type=jnp.float32
    )
    sigma = jax.nn.sigmoid(gate)
    activated = jax.nn.silu(gate)
    hidden = (activated * upward).astype(jnp.bfloat16)
    gate_back = (back * upward * sigma * (1.0 + gate * (1.0 - sigma))).astype(jnp.bfloat16)
    up_back = (back * activated).astype(jnp.bfloat16)
    grad_gate = jnp.einsum("htr,thd->hrd", gate_back, key_unit, preferred_element_type=jnp.float32)
    grad_up = jnp.einsum("htr,thd->hrd", up_back, key_unit, preferred_element_type=jnp.float32)
    grad_down = jnp.einsum("htr,thd->hrd", hidden, cotangent, preferred_element_type=jnp.float32)
    gradient = jnp.stack([grad_gate, grad_up, grad_down], axis=1)
    share = lax.psum_scatter(
        gradient.astype(jnp.bfloat16), "ctx", scatter_dimension=2, tiled=True
    ).astype(jnp.float32)
    fast_updated = fast_weights - (momentum_decay * momentum + share)
    new_rows = lax.all_gather(fast_updated.astype(jnp.bfloat16), "ctx", axis=2, tiled=True)
    own_start = rep_index * per_rep
    partial_out = swiglu_apply(query_unit, new_rows)
    traded = lax.all_to_all(
        partial_out.astype(jnp.bfloat16), "rep", split_axis=0, concat_axis=0, tiled=True
    ).astype(partial_out.dtype)
    fast_out = jnp.sum(traded.reshape(rep_count, per_rep, tok_rows, width), axis=0)
    attend_query = lax.dynamic_slice_in_dim(query_heads, own_start, per_rep, 1)
    attend_key = lax.dynamic_slice_in_dim(key_heads, own_start, per_rep, 1)
    attend_value = lax.dynamic_slice_in_dim(value_heads, own_start, per_rep, 1)
    key_prior, value_prior = passed_along((attend_key, attend_value), "ctx", 1)
    attended = window_attention(
        attend_query, attend_key, attend_value, key_prior, value_prior, ctx_index == 0
    )
    combined = attended + jnp.transpose(fast_out, (1, 0, 2))
    layer_output = combined.astype(jnp.bfloat16).reshape(tok_rows, per_rep * width)
    return (layer_output, fast_updated)


def in_hbm(value):
    return pltpu.with_memory_space_constraint(value, pltpu.HBM)


def columns_body(rep, whole, out, semaphore):
    columns = out.shape[1]
    taken = whole.at[:, pl.ds(pl.multiple_of(rep[0] * columns, columns), columns)]
    copy = pltpu.make_async_copy(taken, out, semaphore)
    copy.start()
    copy.wait()


def columns_step(rep, whole):
    rows, columns = whole.shape[0], whole.shape[1] // 2
    return pl.pallas_call(
        columns_body,
        out_shape=jax.ShapeDtypeStruct((rows, columns), whole.dtype),
        in_specs=[pl.BlockSpec(memory_space=pltpu.SMEM), pl.BlockSpec(memory_space=pl.ANY)],
        out_specs=pl.BlockSpec(memory_space=pltpu.VMEM),
        scratch_shapes=[pltpu.SemaphoreType.DMA],
        compiler_params=pltpu.CompilerParams(vmem_limit_bytes=4 << 20),
        cost_estimate=pl.CostEstimate(
            flops=0, bytes_accessed=4 * rows * columns, transcendentals=0
        ),
        name="columns_step",
    )(rep, in_hbm(whole))


def cotangent_body(token_scale, rep, values, rates, out_raw, out):
    heads = rates.shape[0] // 2
    rows, columns = out.shape
    width = columns // heads
    for h in range(heads):
        rate = -(rates[pl.ds(rep[0] * heads + h, 1), :] * token_scale)
        rate = jnp.transpose(jnp.broadcast_to(rate, (rows, rows)))[:, :1]
        part = values[:, h * width : (h + 1) * width]
        out_raw[:, h * width : (h + 1) * width] = part
        out[:, h * width : (h + 1) * width] = (rate * part.astype(jnp.float32)).astype(jnp.bfloat16)


def cotangent_step(token_scale, rep, values, rates):
    rows, columns = values.shape[0], values.shape[1] // 2
    made = jax.ShapeDtypeStruct((rows, columns), jnp.bfloat16)
    whole = pl.BlockSpec((rows, columns), lambda i, rep: (0, 0))
    return pl.pallas_call(
        functools.partial(cotangent_body, token_scale),
        out_shape=(made, made),
        grid_spec=pltpu.PrefetchScalarGridSpec(
            num_scalar_prefetch=1,
            grid=(1,),
            in_specs=[
                pl.BlockSpec((rows, columns), lambda i, rep: (0, rep[0])),
                pl.BlockSpec(rates.shape, lambda i, rep: (0, 0)),
            ],
            out_specs=(whole, whole),
        ),
        compiler_params=pltpu.CompilerParams(vmem_limit_bytes=8 << 20),
        cost_estimate=pl.CostEstimate(
            flops=2 * rows * columns, bytes_accessed=6 * rows * columns, transcendentals=0
        ),
        name="cotangent_step",
    )(rep, in_hbm(values), in_hbm(rates))


def other_body(rep, weights, momentum, low, base):
    current = weights[...]
    low[...] = current.astype(jnp.bfloat16)
    base[...] = current - momentum_decay * momentum[...]


def other_step(rep, weights, momentum):
    heads = weights.shape[0] // 2
    block = (1,) + weights.shape[1:]
    made = (heads,) + weights.shape[1:]
    taken = pl.BlockSpec(block, lambda h, rep: ((1 - rep[0]) * heads + h, 0, 0, 0))
    given = pl.BlockSpec(block, lambda h, rep: (h, 0, 0, 0))
    return pl.pallas_call(
        other_body,
        out_shape=(pltpu.HBM(made, jnp.bfloat16), pltpu.HBM(made, jnp.float32)),
        grid_spec=pltpu.PrefetchScalarGridSpec(
            num_scalar_prefetch=1,
            grid=(heads,),
            in_specs=[taken, taken],
            out_specs=(given, given),
        ),
        compiler_params=pltpu.CompilerParams(vmem_limit_bytes=12 << 20),
        cost_estimate=pl.CostEstimate(
            flops=weights.size, bytes_accessed=7 * weights.size, transcendentals=0
        ),
        name="other_step",
    )(rep, in_hbm(weights), in_hbm(momentum))


def gradient_products(unit, cot, low, hid):
    fed = lax.dot_general(low[: 4 * hid, :], unit[...], NT, preferred_element_type=jnp.float32)
    gate, upward = fed[: 2 * hid], fed[2 * hid :]
    back = lax.dot_general(low[4 * hid :, :], cot[...], NT, preferred_element_type=jnp.float32)
    sigma = jax.nn.sigmoid(gate)
    activated = gate * sigma
    hidden = (activated * upward).astype(jnp.bfloat16)
    gate_back = (back * upward * sigma * (1.0 + gate * (1.0 - sigma))).astype(jnp.bfloat16)
    up_back = (back * activated).astype(jnp.bfloat16)
    pairs = ((gate_back, unit), (up_back, unit), (hidden, cot))
    return [jnp.dot(left, right[...], preferred_element_type=jnp.float32) for left, right in pairs]


def early_body(slots, rep, *refs):
    keys, cots = refs[:slots], refs[slots : 2 * slots]
    weights, momentum, low_par, base_par, so_far, low, unit, cot = refs[2 * slots :]
    rows = keys[0].shape[0]
    hid = weights.shape[2]
    for s in range(slots):
        here = pl.ds(s * rows, rows)
        unit[here, :] = unit_rows(keys[s][...])
        cot[here, :] = cots[s][...]
    for m in range(3):
        low[pl.ds(2 * m * hid, hid), :] = weights[0, m].astype(jnp.bfloat16)
        low[pl.ds((2 * m + 1) * hid, hid), :] = low_par[0, m]
    for m, grad in enumerate(gradient_products(unit, cot, low, hid)):
        own, par = pl.ds(2 * m * hid, hid), pl.ds((2 * m + 1) * hid, hid)
        so_far[own, :] = weights[0, m] - (momentum_decay * momentum[0, m] + grad[:hid])
        so_far[par, :] = base_par[0, m] - grad[hid:]


def early_step(head, rep, keys, cots, weights, momentum, low_par, base_par):
    slots = len(keys)
    rows = keys[0].shape[0]
    heads, _, hid, width = low_par.shape
    block = (1, 3, hid, width)
    token_spec = pl.BlockSpec((rows, width), lambda i, rep: (0, head))
    own_spec = pl.BlockSpec(block, lambda i, rep: (rep[0] * heads + head, 0, 0, 0))
    par_spec = pl.BlockSpec(block, lambda i, rep: (head, 0, 0, 0))
    made_spec = pl.BlockSpec((6 * hid, width), lambda i, rep: (0, 0))
    return pl.pallas_call(
        functools.partial(early_body, slots),
        out_shape=(
            (pltpu.HBM if head else jax.ShapeDtypeStruct)((6 * hid, width), jnp.float32),
            jax.ShapeDtypeStruct((6 * hid, width), jnp.bfloat16),
        ),
        grid_spec=pltpu.PrefetchScalarGridSpec(
            num_scalar_prefetch=1,
            grid=(1,),
            in_specs=[token_spec] * (2 * slots) + [own_spec] * 2 + [par_spec] * 2,
            out_specs=(made_spec, made_spec),
            scratch_shapes=[
                pltpu.VMEM((slots * rows, width), jnp.bfloat16),
                pltpu.VMEM((slots * rows, width), jnp.bfloat16),
            ],
        ),
        compiler_params=pltpu.CompilerParams(vmem_limit_bytes=20 << 20),
        cost_estimate=pl.CostEstimate(
            flops=24 * slots * rows * hid * width,
            bytes_accessed=60 * hid * width,
            transcendentals=0,
        ),
        name="early_step",
    )(rep, *map(in_hbm, (*keys, *cots, weights, momentum)), low_par, base_par)


def last_body(key, cotangent, so_far, low, new_own, new_par, new_low, unit):
    hid = so_far.shape[0] // 6
    unit[...] = unit_rows(key[...])
    for m, grad in enumerate(gradient_products(unit, cotangent, low, hid)):
        fresh_own = so_far[pl.ds(2 * m * hid, hid), :] - grad[:hid]
        fresh_par = so_far[pl.ds((2 * m + 1) * hid, hid), :] - grad[hid:]
        new_own[0, m] = fresh_own
        new_par[0, m] = fresh_par
        new_low[pl.ds(2 * m * hid, hid), :] = fresh_own.astype(jnp.bfloat16)
        new_low[pl.ds((2 * m + 1) * hid, hid), :] = fresh_par.astype(jnp.bfloat16)


def last_step(head, key, cotangent, so_far, low):
    rows = key.shape[0]
    total, width = low.shape
    hid = total // 6
    token_spec = pl.BlockSpec((rows, width), lambda i: (0, head))
    made_spec = pl.BlockSpec((total, width), lambda i: (0, 0))
    block = (1, 3, hid, width)
    new_spec = pl.BlockSpec(block, lambda i: (0, 0, 0, 0))
    fresh = pltpu.HBM(block, jnp.float32)
    return pl.pallas_call(
        last_body,
        out_shape=(fresh, fresh, jax.ShapeDtypeStruct((total, width), jnp.bfloat16)),
        grid=(1,),
        in_specs=[token_spec, token_spec, made_spec, made_spec],
        out_specs=(new_spec, new_spec, made_spec),
        scratch_shapes=[pltpu.VMEM((rows, width), jnp.bfloat16)],
        compiler_params=pltpu.CompilerParams(vmem_limit_bytes=16 << 20),
        cost_estimate=pl.CostEstimate(
            flops=4 * rows * total * width, bytes_accessed=12 * total * width, transcendentals=0
        ),
        name="last_step",
    )(key, cotangent, in_hbm(so_far) if head else so_far, low)


def apply_body(query, low, out):
    hid = low.shape[0] // 6
    unit = unit_rows(query[...])
    gate = lax.dot_general(unit, low[: 2 * hid, :], NT, preferred_element_type=jnp.float32)
    upward = lax.dot_general(
        unit, low[2 * hid : 4 * hid, :], NT, preferred_element_type=jnp.float32
    )
    hidden = (gate * jax.nn.sigmoid(gate) * upward).astype(jnp.bfloat16)
    made = jnp.dot(hidden, low[4 * hid :, :], preferred_element_type=jnp.float32)
    out[...] = made.astype(out.dtype)


def apply_step(query, low, dtype):
    rows, width = query.shape
    total = low.shape[0]
    whole = pl.BlockSpec((rows, width), lambda i: (0, 0))
    return pl.pallas_call(
        apply_body,
        out_shape=jax.ShapeDtypeStruct((rows, width), dtype),
        grid=(1,),
        in_specs=[whole, pl.BlockSpec((total, width), lambda i: (0, 0))],
        out_specs=whole,
        compiler_params=pltpu.CompilerParams(vmem_limit_bytes=8 << 20),
        cost_estimate=pl.CostEstimate(
            flops=2 * rows * total * width, bytes_accessed=2 * total * width, transcendentals=0
        ),
        name="apply_step",
    )(query, low)


def output_body(kept, attended, moved, *refs):
    total = attended[...] + (kept[...] + moved[...].astype(jnp.float32))
    refs[-1][...] = total.astype(jnp.bfloat16)


def output_step(head, heads, kept, attended, moved, before):
    rows, width = kept.shape
    more = () if before is None else (before,)
    return pl.pallas_call(
        output_body,
        out_shape=pltpu.HBM((rows, heads * width), jnp.bfloat16),
        grid=(1,),
        in_specs=[pl.BlockSpec(memory_space=pltpu.VMEM)] * 3
        + [pl.BlockSpec(memory_space=pl.ANY)] * len(more),
        out_specs=pl.BlockSpec((rows, width), lambda i: (0, head)),
        input_output_aliases={3: 0} if more else {},
        compiler_params=pltpu.CompilerParams(vmem_limit_bytes=4 << 20),
        cost_estimate=pl.CostEstimate(
            flops=rows * width, bytes_accessed=8 * rows * width, transcendentals=0
        ),
        name="output_step",
    )(kept, attended, moved, *more)


def attend_body(token_scale, block_index, *refs):
    key_own, value_own, rate_prior = refs[:3]
    key_slots, cot_slots = refs[3:6], refs[6:9]
    heads = (len(refs) - 9) // 2
    asked, outs = refs[9 : 9 + heads], refs[9 + heads :]
    width = asked[0].shape[1]
    index = block_index[0]
    allowed = jnp.where(index == 0, -jnp.inf, 0.0).astype(jnp.float32)
    for h in range(heads):
        columns = slice(h * width, (h + 1) * width)
        key_prior, cot_prior = (
            jnp.where(
                index == 3,
                one[:, columns],
                jnp.where(index == 2, two[:, columns], three[:, columns]),
            )
            for one, two, three in (key_slots, cot_slots)
        )
        part = asked[h][...]
        near = lax.dot_general(part, key_own[:, columns], NT, preferred_element_type=jnp.float32)
        far = lax.dot_general(part, key_prior, NT, preferred_element_type=jnp.float32)
        near = near * width ** (-0.5)
        far = far * width ** (-0.5) + allowed
        peak = jnp.maximum(
            jnp.max(near, axis=-1, keepdims=True), jnp.max(far, axis=-1, keepdims=True)
        )
        near = jnp.exp(near - peak)
        far = jnp.exp(far - peak)
        total = jnp.sum(near, axis=-1, keepdims=True) + jnp.sum(far, axis=-1, keepdims=True)
        rate = -(rate_prior[h] * token_scale)
        near = (near / total).astype(jnp.bfloat16)
        far = (far / total / rate).astype(jnp.bfloat16)
        outs[h][...] = jnp.dot(
            near, value_own[:, columns], preferred_element_type=jnp.float32
        ) + jnp.dot(far, cot_prior, preferred_element_type=jnp.float32)


def attend_step(token_scale, block_index, keys, value_own, cots, rate_prior, asked):
    rows, columns = value_own.shape
    made = tuple(jax.ShapeDtypeStruct(query.shape, jnp.float32) for query in asked)
    return pl.pallas_call(
        functools.partial(attend_body, token_scale),
        out_shape=made,
        in_specs=[pl.BlockSpec(memory_space=pltpu.SMEM)] + [pl.BlockSpec()] * (9 + len(asked)),
        compiler_params=pltpu.CompilerParams(vmem_limit_bytes=10 << 20),
        cost_estimate=pl.CostEstimate(
            flops=8 * rows * rows * columns, bytes_accessed=20 * rows * columns, transcendentals=0
        ),
        name="attend_step",
    )(
        block_index,
        in_hbm(keys[0]),
        in_hbm(value_own),
        rate_prior,
        *map(in_hbm, (*keys[1:], *cots)),
        *asked,
    )


def tokens_travel(queries, key_vectors, values, learn_rates, fast_weights, momentum):
    width = fast_weights.shape[3]
    slots = lax.axis_size("ctx")
    per_rep = fast_weights.shape[0] // 2
    rep_index = lax.axis_index("rep")
    start = rep_index * per_rep
    token_scale = float(slots * queries.shape[0]) ** (-0.5)

    cycle = (0, 2, 3, 1)

    def hop(value, axis="ctx", order=cycle):
        return ring(value, axis, order if axis == "ctx" else None)

    rep = rep_index.reshape(1)
    value_own, cot = cotangent_step(token_scale, rep, values, learn_rates)
    heads = range(per_rep)
    keys, cots = [columns_step(rep, key_vectors)], [cot]
    asked = [[lax.dynamic_slice_in_dim(queries, (start + h) * width, width, 1) for h in heads]]
    for _ in range(1, slots):
        keys.append(hop(keys[-1]))
        cots.append(hop(cots[-1]))
    rate_prior = hop(
        lax.dynamic_slice_in_dim(learn_rates, start, per_rep, 0)[:, None, :], order=None
    )
    low_other, base_other = other_step(rep, fast_weights, momentum)
    low_par = hop(low_other, "rep")
    base_par = hop(base_other, "rep")
    for _ in range(1, slots):
        asked.append([hop(asked[-1][h]) for h in heads])
    block_index = lax.axis_index("ctx").reshape(1)
    attended = attend_step(
        token_scale, block_index, keys, value_own, cots[1:], rate_prior, asked[0]
    )
    early = []
    for h in heads:
        early.append(
            early_step(
                h, rep, keys[:-1], cots[:-1], fast_weights, momentum, low_par, base_par
            )
        )
    fresh = []
    for h in heads:
        fresh.append(last_step(h, keys[-1], cots[-1], *early[h]))
    lows = [new[2] for new in fresh]
    moving = []
    for step in range(1, slots):
        made = []
        for h in heads:
            kind = jnp.bfloat16 if step == 1 else jnp.float32
            made.append(apply_step(asked[step][h], lows[h], kind))
        if step > 1:
            made = [
                (made[h] + moving[h].astype(jnp.float32)).astype(jnp.bfloat16) for h in heads
            ]
        moving = [hop(made[h]) for h in heads]
    layer_output = None
    for h in heads:
        kept = apply_step(asked[0][h], lows[h], jnp.float32)
        layer_output = output_step(h, per_rep, kept, attended[h], moving[h], layer_output)
    returned = [hop(fresh[h][1], "rep") for h in heads]
    owned = [new[0] for new in fresh]
    fast_updated = jnp.where(
        rep_index == 0,
        jnp.concatenate([*owned, *returned], axis=0),
        jnp.concatenate([*returned, *owned], axis=0),
    )
    return (layer_output, fast_updated)


def on_device(queries, key_vectors, values, learn_rates, fast_weights, momentum):
    slots = lax.axis_size("ctx")
    fits = (
        lax.axis_size("rep") == 2
        and slots == 4
        and fast_weights.shape[0] == 4
        and fast_weights.shape[2] % 16 == 0
        and queries.shape[0] == 128
    )
    program = tokens_travel if fits else weights_travel
    return program(queries, key_vectors, values, learn_rates, fast_weights, momentum)


def solution(mesh):
    return jax.shard_map(
        on_device,
        mesh=mesh,
        in_specs=(
            P(("groups", "ctx"), "head"),
            P(("groups", "ctx"), "head"),
            P(("groups", "ctx"), "head"),
            P("head", ("groups", "ctx")),
            P(("groups", "head"), None, ("ctx", "rep"), None),
            P(("groups", "head"), None, ("ctx", "rep"), None),
        ),
        out_specs=(
            P(("groups", "ctx"), ("head", "rep")),
            P(("groups", "head"), None, ("ctx", "rep"), None),
        ),
        check_vma=False,
    )
```

```python
import functools

import jax
import jax.numpy as jnp
from jax import lax
from jax.experimental import pallas as pl
from jax.experimental.pallas import tpu as pltpu
from jax.sharding import PartitionSpec as P


epsilon = 1e-06
momentum_decay = 0.9
NT = (((1,), (1,)), ((), ()))


def passed_along(value, axis, steps):
    count = lax.axis_size(axis)
    initial, last = (max(0, -steps), min(count, count - steps))
    return lax.ppermute(value, axis, [(source, source + steps) for source in range(initial, last)])


def ring(value, axis, order=None):
    order = order or range(lax.axis_size(axis))
    return lax.ppermute(value, axis, list(zip(order, (*order[1:], order[0]))))


def unit_rows(tensor):
    widened = tensor.astype(jnp.float32)
    factor = lax.rsqrt(jnp.mean(widened * widened, axis=-1, keepdims=True) + epsilon)
    return (widened * factor).astype(jnp.bfloat16)


def swiglu_apply(inputs, weights):
    gate = jnp.einsum("thd,hrd->htr", inputs, weights[:, 0], preferred_element_type=jnp.float32)
    upward = jnp.einsum("thd,hrd->htr", inputs, weights[:, 1], preferred_element_type=jnp.float32)
    hidden = (jax.nn.silu(gate) * upward).astype(jnp.bfloat16)
    return jnp.einsum("htr,hrd->htd", hidden, weights[:, 2], preferred_element_type=jnp.float32)


def window_attention(query_own, key_own, value_own, key_prior, value_prior, first_block):
    tok_rows = query_own.shape[0]
    per_rep = query_own.shape[1]
    width = query_own.shape[2]
    block_rows = min(tok_rows, 512)
    block_count = tok_rows // block_rows
    key_window = jnp.concatenate([key_prior, key_own], axis=0)
    value_window = jnp.concatenate([value_prior, value_own], axis=0)
    score_scale = width ** (-0.5)
    position = jnp.arange(2 * tok_rows)
    valid = jnp.logical_or(position >= tok_rows, jnp.logical_not(first_block))
    query_blocks = query_own.reshape(block_count, block_rows, per_rep, width)

    def one_block(query_block):
        scores = (
            jnp.einsum("tad,sad->ats", query_block, key_window, preferred_element_type=jnp.float32)
            * score_scale
        )
        scores = jnp.where(valid[None, None, :], scores, -jnp.inf)
        peak = jnp.max(scores, axis=-1, keepdims=True)
        weights = jnp.exp(scores - peak)
        probs = (weights / jnp.sum(weights, axis=-1, keepdims=True)).astype(jnp.bfloat16)
        return jnp.einsum("ats,sad->tad", probs, value_window, preferred_element_type=jnp.float32)

    return lax.map(one_block, query_blocks).reshape(tok_rows, per_rep, width)


def weights_travel(queries, key_vectors, values, learn_rates, fast_weights, momentum):
    tok_rows = queries.shape[0]
    head_count = fast_weights.shape[0]
    width = fast_weights.shape[3]
    rep_count = lax.axis_size("rep")
    per_rep = head_count // rep_count
    rep_index = lax.axis_index("rep")
    ctx_index = lax.axis_index("ctx")
    total_tokens = tok_rows * lax.axis_size("ctx")
    query_heads = queries.reshape(tok_rows, head_count, width)
    key_heads = key_vectors.reshape(tok_rows, head_count, width)
    value_heads = values.reshape(tok_rows, head_count, width)
    query_unit = unit_rows(query_heads)
    key_unit = unit_rows(key_heads)
    token_scale = float(total_tokens) ** (-0.5)
    cotangent = (
        -(learn_rates.T[:, :, None] * token_scale) * value_heads.astype(jnp.float32)
    ).astype(jnp.bfloat16)
    weight_rows = lax.all_gather(fast_weights.astype(jnp.bfloat16), "ctx", axis=2, tiled=True)
    gate = jnp.einsum(
        "thd,hrd->htr", key_unit, weight_rows[:, 0], preferred_element_type=jnp.float32
    )
    upward = jnp.einsum(
        "thd,hrd->htr", key_unit, weight_rows[:, 1], preferred_element_type=jnp.float32
    )
    back = jnp.einsum(
        "thd,hrd->htr", cotangent, weight_rows[:, 2], preferred_element_type=jnp.float32
    )
    sigma = jax.nn.sigmoid(gate)
    activated = jax.nn.silu(gate)
    hidden = (activated * upward).astype(jnp.bfloat16)
    gate_back = (back * upward * sigma * (1.0 + gate * (1.0 - sigma))).astype(jnp.bfloat16)
    up_back = (back * activated).astype(jnp.bfloat16)
    grad_gate = jnp.einsum("htr,thd->hrd", gate_back, key_unit, preferred_element_type=jnp.float32)
    grad_up = jnp.einsum("htr,thd->hrd", up_back, key_unit, preferred_element_type=jnp.float32)
    grad_down = jnp.einsum("htr,thd->hrd", hidden, cotangent, preferred_element_type=jnp.float32)
    gradient = jnp.stack([grad_gate, grad_up, grad_down], axis=1)
    share = lax.psum_scatter(
        gradient.astype(jnp.bfloat16), "ctx", scatter_dimension=2, tiled=True
    ).astype(jnp.float32)
    fast_updated = fast_weights - (momentum_decay * momentum + share)
    new_rows = lax.all_gather(fast_updated.astype(jnp.bfloat16), "ctx", axis=2, tiled=True)
    own_start = rep_index * per_rep
    partial_out = swiglu_apply(query_unit, new_rows)
    traded = lax.all_to_all(
        partial_out.astype(jnp.bfloat16), "rep", split_axis=0, concat_axis=0, tiled=True
    ).astype(partial_out.dtype)
    fast_out = jnp.sum(traded.reshape(rep_count, per_rep, tok_rows, width), axis=0)
    attend_query = lax.dynamic_slice_in_dim(query_heads, own_start, per_rep, 1)
    attend_key = lax.dynamic_slice_in_dim(key_heads, own_start, per_rep, 1)
    attend_value = lax.dynamic_slice_in_dim(value_heads, own_start, per_rep, 1)
    key_prior, value_prior = passed_along((attend_key, attend_value), "ctx", 1)
    attended = window_attention(
        attend_query, attend_key, attend_value, key_prior, value_prior, ctx_index == 0
    )
    combined = attended + jnp.transpose(fast_out, (1, 0, 2))
    layer_output = combined.astype(jnp.bfloat16).reshape(tok_rows, per_rep * width)
    return (layer_output, fast_updated)


def in_hbm(value):
    return pltpu.with_memory_space_constraint(value, pltpu.HBM)


def columns_body(rep, whole, out, semaphore):
    columns = out.shape[1]
    taken = whole.at[:, pl.ds(pl.multiple_of(rep[0] * columns, columns), columns)]
    copy = pltpu.make_async_copy(taken, out, semaphore)
    copy.start()
    copy.wait()


def columns_step(rep, whole):
    rows, columns = whole.shape[0], whole.shape[1] // 2
    return pl.pallas_call(
        columns_body,
        out_shape=jax.ShapeDtypeStruct((rows, columns), whole.dtype),
        in_specs=[pl.BlockSpec(memory_space=pltpu.SMEM), pl.BlockSpec(memory_space=pl.ANY)],
        out_specs=pl.BlockSpec(memory_space=pltpu.VMEM),
        scratch_shapes=[pltpu.SemaphoreType.DMA],
        compiler_params=pltpu.CompilerParams(vmem_limit_bytes=4 << 20),
        cost_estimate=pl.CostEstimate(
            flops=0, bytes_accessed=4 * rows * columns, transcendentals=0
        ),
        name="columns_step",
    )(rep, in_hbm(whole))


def cotangent_body(token_scale, rep, values, rates, out_raw, out):
    heads = rates.shape[0] // 2
    rows, columns = out.shape
    width = columns // heads
    for h in range(heads):
        rate = -(rates[pl.ds(rep[0] * heads + h, 1), :] * token_scale)
        rate = jnp.transpose(jnp.broadcast_to(rate, (rows, rows)))[:, :1]
        part = values[:, h * width : (h + 1) * width]
        out_raw[:, h * width : (h + 1) * width] = part
        out[:, h * width : (h + 1) * width] = (rate * part.astype(jnp.float32)).astype(jnp.bfloat16)


def cotangent_step(token_scale, rep, values, rates):
    rows, columns = values.shape[0], values.shape[1] // 2
    made = jax.ShapeDtypeStruct((rows, columns), jnp.bfloat16)
    whole = pl.BlockSpec((rows, columns), lambda i, rep: (0, 0))
    return pl.pallas_call(
        functools.partial(cotangent_body, token_scale),
        out_shape=(made, made),
        grid_spec=pltpu.PrefetchScalarGridSpec(
            num_scalar_prefetch=1,
            grid=(1,),
            in_specs=[
                pl.BlockSpec((rows, columns), lambda i, rep: (0, rep[0])),
                pl.BlockSpec(rates.shape, lambda i, rep: (0, 0)),
            ],
            out_specs=(whole, whole),
        ),
        compiler_params=pltpu.CompilerParams(vmem_limit_bytes=8 << 20),
        cost_estimate=pl.CostEstimate(
            flops=2 * rows * columns, bytes_accessed=6 * rows * columns, transcendentals=0
        ),
        name="cotangent_step",
    )(rep, in_hbm(values), in_hbm(rates))


def other_body(rep, weights, momentum, low, base):
    current = weights[...]
    low[...] = current.astype(jnp.bfloat16)
    base[...] = current - momentum_decay * momentum[...]


def other_step(rep, weights, momentum):
    heads = weights.shape[0] // 2
    block = (1,) + weights.shape[1:]
    made = (heads,) + weights.shape[1:]
    taken = pl.BlockSpec(block, lambda h, rep: ((1 - rep[0]) * heads + h, 0, 0, 0))
    given = pl.BlockSpec(block, lambda h, rep: (h, 0, 0, 0))
    return pl.pallas_call(
        other_body,
        out_shape=(pltpu.HBM(made, jnp.bfloat16), pltpu.HBM(made, jnp.float32)),
        grid_spec=pltpu.PrefetchScalarGridSpec(
            num_scalar_prefetch=1,
            grid=(heads,),
            in_specs=[taken, taken],
            out_specs=(given, given),
        ),
        compiler_params=pltpu.CompilerParams(vmem_limit_bytes=12 << 20),
        cost_estimate=pl.CostEstimate(
            flops=weights.size, bytes_accessed=7 * weights.size, transcendentals=0
        ),
        name="other_step",
    )(rep, in_hbm(weights), in_hbm(momentum))


def gradient_products(unit, cot, low, hid):
    fed = lax.dot_general(low[: 4 * hid, :], unit[...], NT, preferred_element_type=jnp.float32)
    gate, upward = fed[: 2 * hid], fed[2 * hid :]
    back = lax.dot_general(low[4 * hid :, :], cot[...], NT, preferred_element_type=jnp.float32)
    sigma = jax.nn.sigmoid(gate)
    activated = gate * sigma
    hidden = (activated * upward).astype(jnp.bfloat16)
    gate_back = (back * upward * sigma * (1.0 + gate * (1.0 - sigma))).astype(jnp.bfloat16)
    up_back = (back * activated).astype(jnp.bfloat16)
    pairs = ((gate_back, unit), (up_back, unit), (hidden, cot))
    return [jnp.dot(left, right[...], preferred_element_type=jnp.float32) for left, right in pairs]


def early_body(slots, rep, *refs):
    keys, cots = refs[:slots], refs[slots : 2 * slots]
    weights, momentum, low_par, base_par, so_far, low, unit, cot = refs[2 * slots :]
    rows = keys[0].shape[0]
    hid = weights.shape[2]
    for s in range(slots):
        here = pl.ds(s * rows, rows)
        unit[here, :] = unit_rows(keys[s][...])
        cot[here, :] = cots[s][...]
    for m in range(3):
        low[pl.ds(2 * m * hid, hid), :] = weights[0, m].astype(jnp.bfloat16)
        low[pl.ds((2 * m + 1) * hid, hid), :] = low_par[0, m]
    for m, grad in enumerate(gradient_products(unit, cot, low, hid)):
        own, par = pl.ds(2 * m * hid, hid), pl.ds((2 * m + 1) * hid, hid)
        so_far[own, :] = weights[0, m] - (momentum_decay * momentum[0, m] + grad[:hid])
        so_far[par, :] = base_par[0, m] - grad[hid:]


def early_step(head, rep, keys, cots, weights, momentum, low_par, base_par):
    slots = len(keys)
    rows = keys[0].shape[0]
    heads, _, hid, width = low_par.shape
    block = (1, 3, hid, width)
    token_spec = pl.BlockSpec((rows, width), lambda i, rep: (0, head))
    own_spec = pl.BlockSpec(block, lambda i, rep: (rep[0] * heads + head, 0, 0, 0))
    par_spec = pl.BlockSpec(block, lambda i, rep: (head, 0, 0, 0))
    made_spec = pl.BlockSpec((6 * hid, width), lambda i, rep: (0, 0))
    return pl.pallas_call(
        functools.partial(early_body, slots),
        out_shape=(
            (pltpu.HBM if head else jax.ShapeDtypeStruct)((6 * hid, width), jnp.float32),
            jax.ShapeDtypeStruct((6 * hid, width), jnp.bfloat16),
        ),
        grid_spec=pltpu.PrefetchScalarGridSpec(
            num_scalar_prefetch=1,
            grid=(1,),
            in_specs=[token_spec] * (2 * slots) + [own_spec] * 2 + [par_spec] * 2,
            out_specs=(made_spec, made_spec),
            scratch_shapes=[
                pltpu.VMEM((slots * rows, width), jnp.bfloat16),
                pltpu.VMEM((slots * rows, width), jnp.bfloat16),
            ],
        ),
        compiler_params=pltpu.CompilerParams(vmem_limit_bytes=20 << 20),
        cost_estimate=pl.CostEstimate(
            flops=24 * slots * rows * hid * width,
            bytes_accessed=60 * hid * width,
            transcendentals=0,
        ),
        name="early_step",
    )(rep, *map(in_hbm, (*keys, *cots, weights, momentum)), low_par, base_par)


def last_body(rep, key, cotangent, so_far, low, *refs):
    new_own, new_par, new_low, unit = refs[-4:]
    hid = so_far.shape[0] // 6
    unit[...] = unit_rows(key[...])
    for m, grad in enumerate(gradient_products(unit, cotangent, low, hid)):
        fresh_own = so_far[pl.ds(2 * m * hid, hid), :] - grad[:hid]
        fresh_par = so_far[pl.ds((2 * m + 1) * hid, hid), :] - grad[hid:]
        new_own[0, m] = fresh_own
        new_par[0, m] = fresh_par
        new_low[pl.ds(2 * m * hid, hid), :] = fresh_own.astype(jnp.bfloat16)
        new_low[pl.ds((2 * m + 1) * hid, hid), :] = fresh_par.astype(jnp.bfloat16)


def last_step(head, heads, rep, key, cotangent, so_far, low, before):
    rows = key.shape[0]
    total, width = low.shape
    hid = total // 6
    token_spec = pl.BlockSpec((rows, width), lambda i, rep: (0, head))
    made_spec = pl.BlockSpec((total, width), lambda i, rep: (0, 0))
    block = (1, 3, hid, width)
    own_spec = pl.BlockSpec(block, lambda i, rep: (rep[0] * heads + head, 0, 0, 0))
    par_spec = pl.BlockSpec(block, lambda i, rep: (0, 0, 0, 0))
    more = () if before is None else (before,)
    return pl.pallas_call(
        last_body,
        out_shape=(
            pltpu.HBM((2 * heads, 3, hid, width), jnp.float32),
            pltpu.HBM(block, jnp.float32),
            jax.ShapeDtypeStruct((total, width), jnp.bfloat16),
        ),
        grid_spec=pltpu.PrefetchScalarGridSpec(
            num_scalar_prefetch=1,
            grid=(1,),
            in_specs=[token_spec, token_spec, made_spec, made_spec]
            + [pl.BlockSpec(memory_space=pl.ANY)] * len(more),
            out_specs=(own_spec, par_spec, made_spec),
            scratch_shapes=[pltpu.VMEM((rows, width), jnp.bfloat16)],
        ),
        input_output_aliases={5: 0} if more else {},
        compiler_params=pltpu.CompilerParams(vmem_limit_bytes=16 << 20),
        cost_estimate=pl.CostEstimate(
            flops=4 * rows * total * width, bytes_accessed=12 * total * width, transcendentals=0
        ),
        name="last_step",
    )(rep, key, cotangent, in_hbm(so_far) if head else so_far, low, *more)


def place_body(rep, block, before, out):
    out[...] = block[...]


def place_step(head, heads, rep, block, before):
    given = pl.BlockSpec(block.shape, lambda i, rep: (0, 0, 0, 0))
    taken = pl.BlockSpec(block.shape, lambda i, rep: ((1 - rep[0]) * heads + head, 0, 0, 0))
    return pl.pallas_call(
        place_body,
        out_shape=pltpu.HBM(before.shape, before.dtype),
        grid_spec=pltpu.PrefetchScalarGridSpec(
            num_scalar_prefetch=1,
            grid=(1,),
            in_specs=[given, pl.BlockSpec(memory_space=pl.ANY)],
            out_specs=taken,
        ),
        input_output_aliases={2: 0},
        compiler_params=pltpu.CompilerParams(vmem_limit_bytes=6 << 20),
        cost_estimate=pl.CostEstimate(
            flops=0, bytes_accessed=8 * block.size, transcendentals=0
        ),
        name="place_step",
    )(rep, block, before)


def join_body(made, moved, out):
    out[...] = (made[...] + moved[...].astype(jnp.float32)).astype(jnp.bfloat16)


def join_step(made, moved):
    in_vmem = pl.BlockSpec(memory_space=pltpu.VMEM)
    return pl.pallas_call(
        join_body,
        out_shape=jax.ShapeDtypeStruct(made.shape, jnp.bfloat16),
        in_specs=[in_vmem, in_vmem],
        out_specs=in_vmem,
        compiler_params=pltpu.CompilerParams(vmem_limit_bytes=2 << 20),
        cost_estimate=pl.CostEstimate(
            flops=made.size, bytes_accessed=8 * made.size, transcendentals=0
        ),
        name="join_step",
    )(made, moved)


def apply_body(query, low, out):
    hid = low.shape[0] // 6
    unit = unit_rows(query[...])
    gate = lax.dot_general(unit, low[: 2 * hid, :], NT, preferred_element_type=jnp.float32)
    upward = lax.dot_general(
        unit, low[2 * hid : 4 * hid, :], NT, preferred_element_type=jnp.float32
    )
    hidden = (gate * jax.nn.sigmoid(gate) * upward).astype(jnp.bfloat16)
    made = jnp.dot(hidden, low[4 * hid :, :], preferred_element_type=jnp.float32)
    out[...] = made.astype(out.dtype)


def apply_step(query, low, dtype):
    rows, width = query.shape
    total = low.shape[0]
    whole = pl.BlockSpec((rows, width), lambda i: (0, 0))
    return pl.pallas_call(
        apply_body,
        out_shape=jax.ShapeDtypeStruct((rows, width), dtype),
        grid=(1,),
        in_specs=[whole, pl.BlockSpec((total, width), lambda i: (0, 0))],
        out_specs=whole,
        compiler_params=pltpu.CompilerParams(vmem_limit_bytes=8 << 20),
        cost_estimate=pl.CostEstimate(
            flops=2 * rows * total * width, bytes_accessed=2 * total * width, transcendentals=0
        ),
        name="apply_step",
    )(query, low)


def output_body(kept, attended, moved, *refs):
    total = attended[...] + (kept[...] + moved[...].astype(jnp.float32))
    refs[-1][...] = total.astype(jnp.bfloat16)


def output_step(head, heads, kept, attended, moved, before):
    rows, width = kept.shape
    more = () if before is None else (before,)
    return pl.pallas_call(
        output_body,
        out_shape=pltpu.HBM((rows, heads * width), jnp.bfloat16),
        grid=(1,),
        in_specs=[pl.BlockSpec(memory_space=pltpu.VMEM)] * 3
        + [pl.BlockSpec(memory_space=pl.ANY)] * len(more),
        out_specs=pl.BlockSpec((rows, width), lambda i: (0, head)),
        input_output_aliases={3: 0} if more else {},
        compiler_params=pltpu.CompilerParams(vmem_limit_bytes=4 << 20),
        cost_estimate=pl.CostEstimate(
            flops=rows * width, bytes_accessed=8 * rows * width, transcendentals=0
        ),
        name="output_step",
    )(kept, attended, moved, *more)


def attend_body(token_scale, block_index, *refs):
    key_own, value_own, rate_prior = refs[:3]
    key_slots, cot_slots = refs[3:6], refs[6:9]
    heads = (len(refs) - 9) // 2
    asked, outs = refs[9 : 9 + heads], refs[9 + heads :]
    width = asked[0].shape[1]
    index = block_index[0]
    allowed = jnp.where(index == 0, -jnp.inf, 0.0).astype(jnp.float32)
    for h in range(heads):
        columns = slice(h * width, (h + 1) * width)
        key_prior, cot_prior = (
            jnp.where(
                index == 3,
                one[:, columns],
                jnp.where(index == 2, two[:, columns], three[:, columns]),
            )
            for one, two, three in (key_slots, cot_slots)
        )
        part = asked[h][...]
        near = lax.dot_general(part, key_own[:, columns], NT, preferred_element_type=jnp.float32)
        far = lax.dot_general(part, key_prior, NT, preferred_element_type=jnp.float32)
        near = near * width ** (-0.5)
        far = far * width ** (-0.5) + allowed
        peak = jnp.maximum(
            jnp.max(near, axis=-1, keepdims=True), jnp.max(far, axis=-1, keepdims=True)
        )
        near = jnp.exp(near - peak)
        far = jnp.exp(far - peak)
        total = jnp.sum(near, axis=-1, keepdims=True) + jnp.sum(far, axis=-1, keepdims=True)
        rate = -(rate_prior[h] * token_scale)
        near = (near / total).astype(jnp.bfloat16)
        far = (far / total / rate).astype(jnp.bfloat16)
        outs[h][...] = jnp.dot(
            near, value_own[:, columns], preferred_element_type=jnp.float32
        ) + jnp.dot(far, cot_prior, preferred_element_type=jnp.float32)


def attend_step(token_scale, block_index, keys, value_own, cots, rate_prior, asked):
    rows, columns = value_own.shape
    made = tuple(jax.ShapeDtypeStruct(query.shape, jnp.float32) for query in asked)
    return pl.pallas_call(
        functools.partial(attend_body, token_scale),
        out_shape=made,
        in_specs=[pl.BlockSpec(memory_space=pltpu.SMEM)] + [pl.BlockSpec()] * (9 + len(asked)),
        compiler_params=pltpu.CompilerParams(vmem_limit_bytes=10 << 20),
        cost_estimate=pl.CostEstimate(
            flops=8 * rows * rows * columns, bytes_accessed=20 * rows * columns, transcendentals=0
        ),
        name="attend_step",
    )(
        block_index,
        in_hbm(keys[0]),
        in_hbm(value_own),
        rate_prior,
        *map(in_hbm, (*keys[1:], *cots)),
        *asked,
    )


def tokens_travel(queries, key_vectors, values, learn_rates, fast_weights, momentum):
    width = fast_weights.shape[3]
    slots = lax.axis_size("ctx")
    per_rep = fast_weights.shape[0] // 2
    rep_index = lax.axis_index("rep")
    start = rep_index * per_rep
    token_scale = float(slots * queries.shape[0]) ** (-0.5)

    cycle = (0, 2, 3, 1)

    def hop(value, axis="ctx", order=cycle):
        return ring(value, axis, order if axis == "ctx" else None)

    rep = rep_index.reshape(1)
    value_own, cot = cotangent_step(token_scale, rep, values, learn_rates)
    heads = range(per_rep)
    keys, cots = [columns_step(rep, key_vectors)], [cot]
    asked = [[lax.dynamic_slice_in_dim(queries, (start + h) * width, width, 1) for h in heads]]
    for _ in range(1, slots):
        keys.append(hop(keys[-1]))
        cots.append(hop(cots[-1]))
    rate_prior = hop(
        lax.dynamic_slice_in_dim(learn_rates, start, per_rep, 0)[:, None, :], order=None
    )
    low_other, base_other = other_step(rep, fast_weights, momentum)
    low_par = hop(low_other, "rep")
    base_par = hop(base_other, "rep")
    for _ in range(1, slots):
        asked.append([hop(asked[-1][h]) for h in heads])
    block_index = lax.axis_index("ctx").reshape(1)
    attended = attend_step(
        token_scale, block_index, keys, value_own, cots[1:], rate_prior, asked[0]
    )
    early = []
    for h in heads:
        early.append(
            early_step(
                h, rep, keys[:-1], cots[:-1], fast_weights, momentum, low_par, base_par
            )
        )
    fast_updated, sent_back, lows = None, [], []
    for h in heads:
        fast_updated, for_other, low = last_step(
            h, per_rep, rep, keys[-1], cots[-1], *early[h], fast_updated
        )
        sent_back.append(for_other)
        lows.append(low)
    moving = []
    for step in range(1, slots):
        made = []
        for h in heads:
            kind = jnp.bfloat16 if step == 1 else jnp.float32
            made.append(apply_step(asked[step][h], lows[h], kind))
        if step > 1:
            made = [join_step(made[h], moving[h]) for h in heads]
        moving = [hop(made[h]) for h in heads]
    layer_output = None
    for h in heads:
        kept = apply_step(asked[0][h], lows[h], jnp.float32)
        layer_output = output_step(h, per_rep, kept, attended[h], moving[h], layer_output)
    for h in heads:
        returned = hop(sent_back[h], "rep")
        fast_updated = place_step(h, per_rep, rep, returned, fast_updated)
    return (layer_output, fast_updated)


def on_device(queries, key_vectors, values, learn_rates, fast_weights, momentum):
    slots = lax.axis_size("ctx")
    fits = (
        lax.axis_size("rep") == 2
        and slots == 4
        and fast_weights.shape[0] == 4
        and fast_weights.shape[2] % 16 == 0
        and queries.shape[0] == 128
    )
    program = tokens_travel if fits else weights_travel
    return program(queries, key_vectors, values, learn_rates, fast_weights, momentum)


def solution(mesh):
    return jax.shard_map(
        on_device,
        mesh=mesh,
        in_specs=(
            P(("groups", "ctx"), "head"),
            P(("groups", "ctx"), "head"),
            P(("groups", "ctx"), "head"),
            P("head", ("groups", "ctx")),
            P(("groups", "head"), None, ("ctx", "rep"), None),
            P(("groups", "head"), None, ("ctx", "rep"), None),
        ),
        out_specs=(
            P(("groups", "ctx"), ("head", "rep")),
            P(("groups", "head"), None, ("ctx", "rep"), None),
        ),
        check_vma=False,
    )
```

```python
import functools

import jax
import jax.numpy as jnp
from jax import lax
from jax.experimental import pallas as pl
from jax.experimental.pallas import tpu as pltpu
from jax.sharding import PartitionSpec as P


epsilon = 1e-06
momentum_decay = 0.9
NT = (((1,), (1,)), ((), ()))


def passed_along(value, axis, steps):
    count = lax.axis_size(axis)
    initial, last = (max(0, -steps), min(count, count - steps))
    return lax.ppermute(value, axis, [(source, source + steps) for source in range(initial, last)])


def ring(value, axis, order=None):
    order = order or range(lax.axis_size(axis))
    return lax.ppermute(value, axis, list(zip(order, (*order[1:], order[0]))))


def unit_rows(tensor):
    widened = tensor.astype(jnp.float32)
    factor = lax.rsqrt(jnp.mean(widened * widened, axis=-1, keepdims=True) + epsilon)
    return (widened * factor).astype(jnp.bfloat16)


def swiglu_apply(inputs, weights):
    gate = jnp.einsum("thd,hrd->htr", inputs, weights[:, 0], preferred_element_type=jnp.float32)
    upward = jnp.einsum("thd,hrd->htr", inputs, weights[:, 1], preferred_element_type=jnp.float32)
    hidden = (jax.nn.silu(gate) * upward).astype(jnp.bfloat16)
    return jnp.einsum("htr,hrd->htd", hidden, weights[:, 2], preferred_element_type=jnp.float32)


def window_attention(query_own, key_own, value_own, key_prior, value_prior, first_block):
    tok_rows = query_own.shape[0]
    per_rep = query_own.shape[1]
    width = query_own.shape[2]
    block_rows = min(tok_rows, 512)
    block_count = tok_rows // block_rows
    key_window = jnp.concatenate([key_prior, key_own], axis=0)
    value_window = jnp.concatenate([value_prior, value_own], axis=0)
    score_scale = width ** (-0.5)
    position = jnp.arange(2 * tok_rows)
    valid = jnp.logical_or(position >= tok_rows, jnp.logical_not(first_block))
    query_blocks = query_own.reshape(block_count, block_rows, per_rep, width)

    def one_block(query_block):
        scores = (
            jnp.einsum("tad,sad->ats", query_block, key_window, preferred_element_type=jnp.float32)
            * score_scale
        )
        scores = jnp.where(valid[None, None, :], scores, -jnp.inf)
        peak = jnp.max(scores, axis=-1, keepdims=True)
        weights = jnp.exp(scores - peak)
        probs = (weights / jnp.sum(weights, axis=-1, keepdims=True)).astype(jnp.bfloat16)
        return jnp.einsum("ats,sad->tad", probs, value_window, preferred_element_type=jnp.float32)

    return lax.map(one_block, query_blocks).reshape(tok_rows, per_rep, width)


def weights_travel(queries, key_vectors, values, learn_rates, fast_weights, momentum):
    tok_rows = queries.shape[0]
    head_count = fast_weights.shape[0]
    width = fast_weights.shape[3]
    rep_count = lax.axis_size("rep")
    per_rep = head_count // rep_count
    rep_index = lax.axis_index("rep")
    ctx_index = lax.axis_index("ctx")
    total_tokens = tok_rows * lax.axis_size("ctx")
    query_heads = queries.reshape(tok_rows, head_count, width)
    key_heads = key_vectors.reshape(tok_rows, head_count, width)
    value_heads = values.reshape(tok_rows, head_count, width)
    query_unit = unit_rows(query_heads)
    key_unit = unit_rows(key_heads)
    token_scale = float(total_tokens) ** (-0.5)
    cotangent = (
        -(learn_rates.T[:, :, None] * token_scale) * value_heads.astype(jnp.float32)
    ).astype(jnp.bfloat16)
    weight_rows = lax.all_gather(fast_weights.astype(jnp.bfloat16), "ctx", axis=2, tiled=True)
    gate = jnp.einsum(
        "thd,hrd->htr", key_unit, weight_rows[:, 0], preferred_element_type=jnp.float32
    )
    upward = jnp.einsum(
        "thd,hrd->htr", key_unit, weight_rows[:, 1], preferred_element_type=jnp.float32
    )
    back = jnp.einsum(
        "thd,hrd->htr", cotangent, weight_rows[:, 2], preferred_element_type=jnp.float32
    )
    sigma = jax.nn.sigmoid(gate)
    activated = jax.nn.silu(gate)
    hidden = (activated * upward).astype(jnp.bfloat16)
    gate_back = (back * upward * sigma * (1.0 + gate * (1.0 - sigma))).astype(jnp.bfloat16)
    up_back = (back * activated).astype(jnp.bfloat16)
    grad_gate = jnp.einsum("htr,thd->hrd", gate_back, key_unit, preferred_element_type=jnp.float32)
    grad_up = jnp.einsum("htr,thd->hrd", up_back, key_unit, preferred_element_type=jnp.float32)
    grad_down = jnp.einsum("htr,thd->hrd", hidden, cotangent, preferred_element_type=jnp.float32)
    gradient = jnp.stack([grad_gate, grad_up, grad_down], axis=1)
    share = lax.psum_scatter(
        gradient.astype(jnp.bfloat16), "ctx", scatter_dimension=2, tiled=True
    ).astype(jnp.float32)
    fast_updated = fast_weights - (momentum_decay * momentum + share)
    new_rows = lax.all_gather(fast_updated.astype(jnp.bfloat16), "ctx", axis=2, tiled=True)
    own_start = rep_index * per_rep
    partial_out = swiglu_apply(query_unit, new_rows)
    traded = lax.all_to_all(
        partial_out.astype(jnp.bfloat16), "rep", split_axis=0, concat_axis=0, tiled=True
    ).astype(partial_out.dtype)
    fast_out = jnp.sum(traded.reshape(rep_count, per_rep, tok_rows, width), axis=0)
    attend_query = lax.dynamic_slice_in_dim(query_heads, own_start, per_rep, 1)
    attend_key = lax.dynamic_slice_in_dim(key_heads, own_start, per_rep, 1)
    attend_value = lax.dynamic_slice_in_dim(value_heads, own_start, per_rep, 1)
    key_prior, value_prior = passed_along((attend_key, attend_value), "ctx", 1)
    attended = window_attention(
        attend_query, attend_key, attend_value, key_prior, value_prior, ctx_index == 0
    )
    combined = attended + jnp.transpose(fast_out, (1, 0, 2))
    layer_output = combined.astype(jnp.bfloat16).reshape(tok_rows, per_rep * width)
    return (layer_output, fast_updated)


def in_hbm(value):
    return pltpu.with_memory_space_constraint(value, pltpu.HBM)


def columns_body(whole, out, semaphore):
    columns = out.shape[1]
    first = pl.multiple_of(lax.axis_index("rep") * columns, columns)
    taken = whole.at[:, pl.ds(first, columns)]
    copy = pltpu.make_async_copy(taken, out, semaphore)
    copy.start()
    copy.wait()


def columns_step(whole):
    rows, columns = whole.shape[0], whole.shape[1] // 2
    return pl.pallas_call(
        columns_body,
        out_shape=jax.ShapeDtypeStruct((rows, columns), whole.dtype),
        in_specs=[pl.BlockSpec(memory_space=pl.ANY)],
        out_specs=pl.BlockSpec(memory_space=pltpu.VMEM),
        scratch_shapes=[pltpu.SemaphoreType.DMA],
        compiler_params=pltpu.CompilerParams(vmem_limit_bytes=4 << 20),
        cost_estimate=pl.CostEstimate(
            flops=0, bytes_accessed=4 * rows * columns, transcendentals=0
        ),
        name="columns_step",
    )(in_hbm(whole))


def cotangent_body(token_scale, rep, values, rates, out_raw, out):
    heads = rates.shape[0] // 2
    rows, columns = out.shape
    width = columns // heads
    for h in range(heads):
        rate = -(rates[pl.ds(rep[0] * heads + h, 1), :] * token_scale)
        rate = jnp.transpose(jnp.broadcast_to(rate, (rows, rows)))[:, :1]
        part = values[:, h * width : (h + 1) * width]
        out_raw[:, h * width : (h + 1) * width] = part
        out[:, h * width : (h + 1) * width] = (rate * part.astype(jnp.float32)).astype(jnp.bfloat16)


def cotangent_step(token_scale, rep, values, rates):
    rows, columns = values.shape[0], values.shape[1] // 2
    made = jax.ShapeDtypeStruct((rows, columns), jnp.bfloat16)
    whole = pl.BlockSpec((rows, columns), lambda i, rep: (0, 0))
    return pl.pallas_call(
        functools.partial(cotangent_body, token_scale),
        out_shape=(made, made),
        grid_spec=pltpu.PrefetchScalarGridSpec(
            num_scalar_prefetch=1,
            grid=(1,),
            in_specs=[
                pl.BlockSpec((rows, columns), lambda i, rep: (0, rep[0])),
                pl.BlockSpec(rates.shape, lambda i, rep: (0, 0)),
            ],
            out_specs=(whole, whole),
        ),
        compiler_params=pltpu.CompilerParams(vmem_limit_bytes=8 << 20),
        cost_estimate=pl.CostEstimate(
            flops=2 * rows * columns, bytes_accessed=6 * rows * columns, transcendentals=0
        ),
        name="cotangent_step",
    )(rep, in_hbm(values), in_hbm(rates))


def other_body(rep, weights, momentum, low, base):
    current = weights[...]
    low[...] = current.astype(jnp.bfloat16)
    base[...] = current - momentum_decay * momentum[...]


def other_step(rep, weights, momentum):
    heads = weights.shape[0] // 2
    block = (1,) + weights.shape[1:]
    made = (heads,) + weights.shape[1:]
    taken = pl.BlockSpec(block, lambda h, rep: ((1 - rep[0]) * heads + h, 0, 0, 0))
    given = pl.BlockSpec(block, lambda h, rep: (h, 0, 0, 0))
    return pl.pallas_call(
        other_body,
        out_shape=(pltpu.HBM(made, jnp.bfloat16), pltpu.HBM(made, jnp.float32)),
        grid_spec=pltpu.PrefetchScalarGridSpec(
            num_scalar_prefetch=1,
            grid=(heads,),
            in_specs=[taken, taken],
            out_specs=(given, given),
        ),
        compiler_params=pltpu.CompilerParams(vmem_limit_bytes=12 << 20),
        cost_estimate=pl.CostEstimate(
            flops=weights.size, bytes_accessed=7 * weights.size, transcendentals=0
        ),
        name="other_step",
    )(rep, in_hbm(weights), in_hbm(momentum))


def gradient_products(unit, cot, low, hid):
    fed = lax.dot_general(low[: 4 * hid, :], unit[...], NT, preferred_element_type=jnp.float32)
    gate, upward = fed[: 2 * hid], fed[2 * hid :]
    back = lax.dot_general(low[4 * hid :, :], cot[...], NT, preferred_element_type=jnp.float32)
    sigma = jax.nn.sigmoid(gate)
    activated = gate * sigma
    hidden = (activated * upward).astype(jnp.bfloat16)
    gate_back = (back * upward * sigma * (1.0 + gate * (1.0 - sigma))).astype(jnp.bfloat16)
    up_back = (back * activated).astype(jnp.bfloat16)
    pairs = ((gate_back, unit), (up_back, unit), (hidden, cot))
    return [jnp.dot(left, right[...], preferred_element_type=jnp.float32) for left, right in pairs]


def early_body(slots, rep, *refs):
    keys, cots = refs[:slots], refs[slots : 2 * slots]
    weights, momentum, low_par, base_par, so_far, low, unit, cot = refs[2 * slots :]
    rows = keys[0].shape[0]
    hid = weights.shape[2]
    for s in range(slots):
        here = pl.ds(s * rows, rows)
        unit[here, :] = unit_rows(keys[s][...])
        cot[here, :] = cots[s][...]
    for m in range(3):
        low[pl.ds(2 * m * hid, hid), :] = weights[0, m].astype(jnp.bfloat16)
        low[pl.ds((2 * m + 1) * hid, hid), :] = low_par[0, m]
    for m, grad in enumerate(gradient_products(unit, cot, low, hid)):
        own, par = pl.ds(2 * m * hid, hid), pl.ds((2 * m + 1) * hid, hid)
        so_far[own, :] = weights[0, m] - (momentum_decay * momentum[0, m] + grad[:hid])
        so_far[par, :] = base_par[0, m] - grad[hid:]


def early_step(head, rep, keys, cots, weights, momentum, low_par, base_par):
    slots = len(keys)
    rows = keys[0].shape[0]
    heads, _, hid, width = low_par.shape
    block = (1, 3, hid, width)
    token_spec = pl.BlockSpec((rows, width), lambda i, rep: (0, head))
    own_spec = pl.BlockSpec(block, lambda i, rep: (rep[0] * heads + head, 0, 0, 0))
    par_spec = pl.BlockSpec(block, lambda i, rep: (head, 0, 0, 0))
    made_spec = pl.BlockSpec((6 * hid, width), lambda i, rep: (0, 0))
    return pl.pallas_call(
        functools.partial(early_body, slots),
        out_shape=(
            (pltpu.HBM if head else jax.ShapeDtypeStruct)((6 * hid, width), jnp.float32),
            jax.ShapeDtypeStruct((6 * hid, width), jnp.bfloat16),
        ),
        grid_spec=pltpu.PrefetchScalarGridSpec(
            num_scalar_prefetch=1,
            grid=(1,),
            in_specs=[token_spec] * (2 * slots) + [own_spec] * 2 + [par_spec] * 2,
            out_specs=(made_spec, made_spec),
            scratch_shapes=[
                pltpu.VMEM((slots * rows, width), jnp.bfloat16),
                pltpu.VMEM((slots * rows, width), jnp.bfloat16),
            ],
        ),
        compiler_params=pltpu.CompilerParams(vmem_limit_bytes=20 << 20),
        cost_estimate=pl.CostEstimate(
            flops=24 * slots * rows * hid * width,
            bytes_accessed=60 * hid * width,
            transcendentals=0,
        ),
        name="early_step",
    )(rep, *map(in_hbm, (*keys, *cots, weights, momentum)), low_par, base_par)


def last_body(rep, key, cotangent, so_far, low, *refs):
    new_own, new_par, new_low, unit = refs[-4:]
    hid = so_far.shape[0] // 6
    unit[...] = unit_rows(key[...])
    for m, grad in enumerate(gradient_products(unit, cotangent, low, hid)):
        fresh_own = so_far[pl.ds(2 * m * hid, hid), :] - grad[:hid]
        fresh_par = so_far[pl.ds((2 * m + 1) * hid, hid), :] - grad[hid:]
        new_own[0, m] = fresh_own
        new_par[0, m] = fresh_par
        new_low[pl.ds(2 * m * hid, hid), :] = fresh_own.astype(jnp.bfloat16)
        new_low[pl.ds((2 * m + 1) * hid, hid), :] = fresh_par.astype(jnp.bfloat16)


def last_step(head, heads, rep, key, cotangent, so_far, low, before):
    rows = key.shape[0]
    total, width = low.shape
    hid = total // 6
    token_spec = pl.BlockSpec((rows, width), lambda i, rep: (0, head))
    made_spec = pl.BlockSpec((total, width), lambda i, rep: (0, 0))
    block = (1, 3, hid, width)
    own_spec = pl.BlockSpec(block, lambda i, rep: (rep[0] * heads + head, 0, 0, 0))
    par_spec = pl.BlockSpec(block, lambda i, rep: (0, 0, 0, 0))
    more = () if before is None else (before,)
    return pl.pallas_call(
        last_body,
        out_shape=(
            pltpu.HBM((2 * heads, 3, hid, width), jnp.float32),
            pltpu.HBM(block, jnp.float32),
            jax.ShapeDtypeStruct((total, width), jnp.bfloat16),
        ),
        grid_spec=pltpu.PrefetchScalarGridSpec(
            num_scalar_prefetch=1,
            grid=(1,),
            in_specs=[token_spec, token_spec, made_spec, made_spec]
            + [pl.BlockSpec(memory_space=pl.ANY)] * len(more),
            out_specs=(own_spec, par_spec, made_spec),
            scratch_shapes=[pltpu.VMEM((rows, width), jnp.bfloat16)],
        ),
        input_output_aliases={5: 0} if more else {},
        compiler_params=pltpu.CompilerParams(vmem_limit_bytes=16 << 20),
        cost_estimate=pl.CostEstimate(
            flops=4 * rows * total * width, bytes_accessed=12 * total * width, transcendentals=0
        ),
        name="last_step",
    )(rep, key, cotangent, in_hbm(so_far) if head else so_far, low, *more)


def place_body(rep, block, before, out):
    out[...] = block[...]


def place_step(head, heads, rep, block, before):
    given = pl.BlockSpec(block.shape, lambda i, rep: (0, 0, 0, 0))
    taken = pl.BlockSpec(block.shape, lambda i, rep: ((1 - rep[0]) * heads + head, 0, 0, 0))
    return pl.pallas_call(
        place_body,
        out_shape=pltpu.HBM(before.shape, before.dtype),
        grid_spec=pltpu.PrefetchScalarGridSpec(
            num_scalar_prefetch=1,
            grid=(1,),
            in_specs=[given, pl.BlockSpec(memory_space=pl.ANY)],
            out_specs=taken,
        ),
        input_output_aliases={2: 0},
        compiler_params=pltpu.CompilerParams(vmem_limit_bytes=6 << 20),
        cost_estimate=pl.CostEstimate(
            flops=0, bytes_accessed=8 * block.size, transcendentals=0
        ),
        name="place_step",
    )(rep, block, before)


def join_body(first, made, moved, *outs):
    for out in outs:
        rows = out.shape[0]
        here = moved[...] if moved.shape[0] == rows else moved[first : first + rows, :]
        total = made[first : first + rows, :] + here.astype(jnp.float32)
        out[...] = total.astype(jnp.bfloat16)
        first += rows


def join_step(made, moved, first=0, pieces=1):
    rows, width = moved.shape
    in_vmem = pl.BlockSpec(memory_space=pltpu.VMEM)
    return pl.pallas_call(
        functools.partial(join_body, first),
        out_shape=(jax.ShapeDtypeStruct((rows // pieces, width), jnp.bfloat16),) * pieces,
        in_specs=[in_vmem, in_vmem],
        out_specs=(in_vmem,) * pieces,
        compiler_params=pltpu.CompilerParams(vmem_limit_bytes=2 << 20),
        cost_estimate=pl.CostEstimate(
            flops=made.size, bytes_accessed=8 * made.size, transcendentals=0
        ),
        name="join_step",
    )(made, moved)


def apply_body(query, low, out):
    hid = low.shape[0] // 6
    unit = unit_rows(query[...])
    gate = lax.dot_general(unit, low[: 2 * hid, :], NT, preferred_element_type=jnp.float32)
    upward = lax.dot_general(
        unit, low[2 * hid : 4 * hid, :], NT, preferred_element_type=jnp.float32
    )
    hidden = (gate * jax.nn.sigmoid(gate) * upward).astype(jnp.bfloat16)
    made = jnp.dot(hidden, low[4 * hid :, :], preferred_element_type=jnp.float32)
    out[...] = made.astype(out.dtype)


def apply_step(query, low, dtype):
    rows, width = query.shape
    total = low.shape[0]
    whole = pl.BlockSpec((rows, width), lambda i: (0, 0))
    return pl.pallas_call(
        apply_body,
        out_shape=jax.ShapeDtypeStruct((rows, width), dtype),
        grid=(1,),
        in_specs=[whole, pl.BlockSpec((total, width), lambda i: (0, 0))],
        out_specs=whole,
        compiler_params=pltpu.CompilerParams(vmem_limit_bytes=8 << 20),
        cost_estimate=pl.CostEstimate(
            flops=2 * rows * total * width, bytes_accessed=2 * total * width, transcendentals=0
        ),
        name="apply_step",
    )(query, low)


def output_body(parts, kept, attended, *refs):
    first = 0
    for moved in refs[:parts]:
        here = slice(first, first + moved.shape[0])
        total = attended[here, :] + (kept[here, :] + moved[...].astype(jnp.float32))
        refs[-1][here, :] = total.astype(jnp.bfloat16)
        first += moved.shape[0]


def output_step(head, heads, kept, attended, moved, before):
    rows, width = kept.shape
    more = () if before is None else (before,)
    return pl.pallas_call(
        functools.partial(output_body, len(moved)),
        out_shape=pltpu.HBM((rows, heads * width), jnp.bfloat16),
        grid=(1,),
        in_specs=[pl.BlockSpec(memory_space=pltpu.VMEM)] * (2 + len(moved))
        + [pl.BlockSpec(memory_space=pl.ANY)] * len(more),
        out_specs=pl.BlockSpec((rows, width), lambda i: (0, head)),
        input_output_aliases={2 + len(moved): 0} if more else {},
        compiler_params=pltpu.CompilerParams(vmem_limit_bytes=4 << 20),
        cost_estimate=pl.CostEstimate(
            flops=rows * width, bytes_accessed=8 * rows * width, transcendentals=0
        ),
        name="output_step",
    )(kept, attended, *moved, *more)


def attend_body(token_scale, block_index, *refs):
    key_own, value_own, rate_prior = refs[:3]
    key_slots, cot_slots = refs[3:6], refs[6:9]
    heads = (len(refs) - 9) // 2
    asked, outs = refs[9 : 9 + heads], refs[9 + heads :]
    width = asked[0].shape[1]
    index = block_index[0]
    allowed = jnp.where(index == 0, -jnp.inf, 0.0).astype(jnp.float32)
    for h in range(heads):
        columns = slice(h * width, (h + 1) * width)
        key_prior, cot_prior = (
            jnp.where(
                index == 3,
                one[:, columns],
                jnp.where(index == 2, two[:, columns], three[:, columns]),
            )
            for one, two, three in (key_slots, cot_slots)
        )
        part = asked[h][...]
        near = lax.dot_general(part, key_own[:, columns], NT, preferred_element_type=jnp.float32)
        far = lax.dot_general(part, key_prior, NT, preferred_element_type=jnp.float32)
        near = near * width ** (-0.5)
        far = far * width ** (-0.5) + allowed
        peak = jnp.maximum(
            jnp.max(near, axis=-1, keepdims=True), jnp.max(far, axis=-1, keepdims=True)
        )
        near = jnp.exp(near - peak)
        far = jnp.exp(far - peak)
        total = jnp.sum(near, axis=-1, keepdims=True) + jnp.sum(far, axis=-1, keepdims=True)
        rate = -(rate_prior[h] * token_scale)
        near = (near / total).astype(jnp.bfloat16)
        far = (far / total / rate).astype(jnp.bfloat16)
        outs[h][...] = jnp.dot(
            near, value_own[:, columns], preferred_element_type=jnp.float32
        ) + jnp.dot(far, cot_prior, preferred_element_type=jnp.float32)


def attend_step(token_scale, block_index, keys, value_own, cots, rate_prior, asked):
    rows, columns = value_own.shape
    made = tuple(jax.ShapeDtypeStruct(query.shape, jnp.float32) for query in asked)
    return pl.pallas_call(
        functools.partial(attend_body, token_scale),
        out_shape=made,
        in_specs=[pl.BlockSpec(memory_space=pltpu.SMEM)] + [pl.BlockSpec()] * (9 + len(asked)),
        compiler_params=pltpu.CompilerParams(vmem_limit_bytes=10 << 20),
        cost_estimate=pl.CostEstimate(
            flops=8 * rows * rows * columns, bytes_accessed=20 * rows * columns, transcendentals=0
        ),
        name="attend_step",
    )(
        block_index,
        in_hbm(keys[0]),
        in_hbm(value_own),
        rate_prior,
        *map(in_hbm, (*keys[1:], *cots)),
        *asked,
    )


def tokens_travel(queries, key_vectors, values, learn_rates, fast_weights, momentum):
    width = fast_weights.shape[3]
    slots = lax.axis_size("ctx")
    per_rep = fast_weights.shape[0] // 2
    rep_index = lax.axis_index("rep")
    start = rep_index * per_rep
    token_scale = float(slots * queries.shape[0]) ** (-0.5)

    cycle = (0, 2, 3, 1)

    def hop(value, axis="ctx", order=cycle):
        return ring(value, axis, order if axis == "ctx" else None)

    rep = rep_index.reshape(1)
    value_own, cot = cotangent_step(token_scale, rep, values, learn_rates)
    heads = range(per_rep)
    keys, cots = [columns_step(key_vectors)], [cot]
    asked = [[lax.dynamic_slice_in_dim(queries, (start + h) * width, width, 1) for h in heads]]
    for _ in range(1, slots):
        keys.append(hop(keys[-1]))
        cots.append(hop(cots[-1]))
    rate_prior = hop(
        lax.dynamic_slice_in_dim(learn_rates, start, per_rep, 0)[:, None, :], order=None
    )
    low_other, base_other = other_step(rep, fast_weights, momentum)
    low_par = hop(low_other, "rep")
    base_par = hop(base_other, "rep")
    for _ in range(1, slots):
        asked.append([hop(asked[-1][h]) for h in heads])
    block_index = lax.axis_index("ctx").reshape(1)
    attended = attend_step(
        token_scale, block_index, keys, value_own, cots[1:], rate_prior, asked[0]
    )
    early = []
    for h in heads:
        early.append(
            early_step(
                h, rep, keys[:-1], cots[:-1], fast_weights, momentum, low_par, base_par
            )
        )
    fast_updated, sent_back, lows = None, [], []
    for h in heads:
        fast_updated, for_other, low = last_step(
            h, per_rep, rep, keys[-1], cots[-1], *early[h], fast_updated
        )
        sent_back.append(for_other)
        lows.append(low)
    moving = []
    for step in range(1, slots):
        made = []
        for h in heads:
            kind = jnp.bfloat16 if step == 1 else jnp.float32
            made.append(apply_step(asked[step][h], lows[h], kind))
        if step == 1:
            moving = [[hop(made[h])] for h in heads]
            continue
        sent = []
        for h in heads:
            if step == 2:
                sent.append(join_step(made[h], moving[h][0], 0, 1 + h))
            else:
                rows = made[h].shape[0] // len(moving[h])
                sent.append([])
                for i, part in enumerate(moving[h]):
                    sent[h].append(join_step(made[h], part, i * rows)[0])
        moving = [[hop(part) for part in sent[h]] for h in heads]
    layer_output = None
    for h in heads:
        kept = apply_step(asked[0][h], lows[h], jnp.float32)
        layer_output = output_step(h, per_rep, kept, attended[h], moving[h], layer_output)
    for h in heads:
        returned = hop(sent_back[h], "rep")
        fast_updated = place_step(h, per_rep, rep, returned, fast_updated)
    return (layer_output, fast_updated)


def on_device(queries, key_vectors, values, learn_rates, fast_weights, momentum):
    slots = lax.axis_size("ctx")
    fits = (
        lax.axis_size("rep") == 2
        and slots == 4
        and fast_weights.shape[0] == 4
        and fast_weights.shape[2] % 16 == 0
        and queries.shape[0] == 128
    )
    program = tokens_travel if fits else weights_travel
    return program(queries, key_vectors, values, learn_rates, fast_weights, momentum)


def solution(mesh):
    return jax.shard_map(
        on_device,
        mesh=mesh,
        in_specs=(
            P(("groups", "ctx"), "head"),
            P(("groups", "ctx"), "head"),
            P(("groups", "ctx"), "head"),
            P("head", ("groups", "ctx")),
            P(("groups", "head"), None, ("ctx", "rep"), None),
            P(("groups", "head"), None, ("ctx", "rep"), None),
        ),
        out_specs=(
            P(("groups", "ctx"), ("head", "rep")),
            P(("groups", "head"), None, ("ctx", "rep"), None),
        ),
        check_vma=False,
    )
```

```python
import functools

import jax
import jax.numpy as jnp
from jax import lax
from jax.experimental import pallas as pl
from jax.experimental.pallas import tpu as pltpu
from jax.sharding import PartitionSpec as P


epsilon = 1e-06
momentum_decay = 0.9
NT = (((1,), (1,)), ((), ()))


def passed_along(value, axis, steps):
    count = lax.axis_size(axis)
    initial, last = (max(0, -steps), min(count, count - steps))
    return lax.ppermute(value, axis, [(source, source + steps) for source in range(initial, last)])


def ring(value, axis, order=None):
    order = order or range(lax.axis_size(axis))
    return lax.ppermute(value, axis, list(zip(order, (*order[1:], order[0]))))


def unit_rows(tensor):
    widened = tensor.astype(jnp.float32)
    factor = lax.rsqrt(jnp.mean(widened * widened, axis=-1, keepdims=True) + epsilon)
    return (widened * factor).astype(jnp.bfloat16)


def swiglu_apply(inputs, weights):
    gate = jnp.einsum("thd,hrd->htr", inputs, weights[:, 0], preferred_element_type=jnp.float32)
    upward = jnp.einsum("thd,hrd->htr", inputs, weights[:, 1], preferred_element_type=jnp.float32)
    hidden = (jax.nn.silu(gate) * upward).astype(jnp.bfloat16)
    return jnp.einsum("htr,hrd->htd", hidden, weights[:, 2], preferred_element_type=jnp.float32)


def window_attention(query_own, key_own, value_own, key_prior, value_prior, first_block):
    tok_rows = query_own.shape[0]
    per_rep = query_own.shape[1]
    width = query_own.shape[2]
    block_rows = min(tok_rows, 512)
    block_count = tok_rows // block_rows
    key_window = jnp.concatenate([key_prior, key_own], axis=0)
    value_window = jnp.concatenate([value_prior, value_own], axis=0)
    score_scale = width ** (-0.5)
    position = jnp.arange(2 * tok_rows)
    valid = jnp.logical_or(position >= tok_rows, jnp.logical_not(first_block))
    query_blocks = query_own.reshape(block_count, block_rows, per_rep, width)

    def one_block(query_block):
        scores = (
            jnp.einsum("tad,sad->ats", query_block, key_window, preferred_element_type=jnp.float32)
            * score_scale
        )
        scores = jnp.where(valid[None, None, :], scores, -jnp.inf)
        peak = jnp.max(scores, axis=-1, keepdims=True)
        weights = jnp.exp(scores - peak)
        probs = (weights / jnp.sum(weights, axis=-1, keepdims=True)).astype(jnp.bfloat16)
        return jnp.einsum("ats,sad->tad", probs, value_window, preferred_element_type=jnp.float32)

    return lax.map(one_block, query_blocks).reshape(tok_rows, per_rep, width)


def weights_travel(queries, key_vectors, values, learn_rates, fast_weights, momentum):
    tok_rows = queries.shape[0]
    head_count = fast_weights.shape[0]
    width = fast_weights.shape[3]
    rep_count = lax.axis_size("rep")
    per_rep = head_count // rep_count
    rep_index = lax.axis_index("rep")
    ctx_index = lax.axis_index("ctx")
    total_tokens = tok_rows * lax.axis_size("ctx")
    query_heads = queries.reshape(tok_rows, head_count, width)
    key_heads = key_vectors.reshape(tok_rows, head_count, width)
    value_heads = values.reshape(tok_rows, head_count, width)
    query_unit = unit_rows(query_heads)
    key_unit = unit_rows(key_heads)
    token_scale = float(total_tokens) ** (-0.5)
    cotangent = (
        -(learn_rates.T[:, :, None] * token_scale) * value_heads.astype(jnp.float32)
    ).astype(jnp.bfloat16)
    weight_rows = lax.all_gather(fast_weights.astype(jnp.bfloat16), "ctx", axis=2, tiled=True)
    gate = jnp.einsum(
        "thd,hrd->htr", key_unit, weight_rows[:, 0], preferred_element_type=jnp.float32
    )
    upward = jnp.einsum(
        "thd,hrd->htr", key_unit, weight_rows[:, 1], preferred_element_type=jnp.float32
    )
    back = jnp.einsum(
        "thd,hrd->htr", cotangent, weight_rows[:, 2], preferred_element_type=jnp.float32
    )
    sigma = jax.nn.sigmoid(gate)
    activated = jax.nn.silu(gate)
    hidden = (activated * upward).astype(jnp.bfloat16)
    gate_back = (back * upward * sigma * (1.0 + gate * (1.0 - sigma))).astype(jnp.bfloat16)
    up_back = (back * activated).astype(jnp.bfloat16)
    grad_gate = jnp.einsum("htr,thd->hrd", gate_back, key_unit, preferred_element_type=jnp.float32)
    grad_up = jnp.einsum("htr,thd->hrd", up_back, key_unit, preferred_element_type=jnp.float32)
    grad_down = jnp.einsum("htr,thd->hrd", hidden, cotangent, preferred_element_type=jnp.float32)
    gradient = jnp.stack([grad_gate, grad_up, grad_down], axis=1)
    share = lax.psum_scatter(
        gradient.astype(jnp.bfloat16), "ctx", scatter_dimension=2, tiled=True
    ).astype(jnp.float32)
    fast_updated = fast_weights - (momentum_decay * momentum + share)
    new_rows = lax.all_gather(fast_updated.astype(jnp.bfloat16), "ctx", axis=2, tiled=True)
    own_start = rep_index * per_rep
    partial_out = swiglu_apply(query_unit, new_rows)
    traded = lax.all_to_all(
        partial_out.astype(jnp.bfloat16), "rep", split_axis=0, concat_axis=0, tiled=True
    ).astype(partial_out.dtype)
    fast_out = jnp.sum(traded.reshape(rep_count, per_rep, tok_rows, width), axis=0)
    attend_query = lax.dynamic_slice_in_dim(query_heads, own_start, per_rep, 1)
    attend_key = lax.dynamic_slice_in_dim(key_heads, own_start, per_rep, 1)
    attend_value = lax.dynamic_slice_in_dim(value_heads, own_start, per_rep, 1)
    key_prior, value_prior = passed_along((attend_key, attend_value), "ctx", 1)
    attended = window_attention(
        attend_query, attend_key, attend_value, key_prior, value_prior, ctx_index == 0
    )
    combined = attended + jnp.transpose(fast_out, (1, 0, 2))
    layer_output = combined.astype(jnp.bfloat16).reshape(tok_rows, per_rep * width)
    return (layer_output, fast_updated)


def in_hbm(value):
    return pltpu.with_memory_space_constraint(value, pltpu.HBM)


def columns_body(whole, out, semaphore):
    columns = out.shape[1]
    first = pl.multiple_of(lax.axis_index("rep") * columns, columns)
    taken = whole.at[:, pl.ds(first, columns)]
    copy = pltpu.make_async_copy(taken, out, semaphore)
    copy.start()
    copy.wait()


def columns_step(whole):
    rows, columns = whole.shape[0], whole.shape[1] // 2
    return pl.pallas_call(
        columns_body,
        out_shape=jax.ShapeDtypeStruct((rows, columns), whole.dtype),
        in_specs=[pl.BlockSpec(memory_space=pl.ANY)],
        out_specs=pl.BlockSpec(memory_space=pltpu.VMEM),
        scratch_shapes=[pltpu.SemaphoreType.DMA],
        compiler_params=pltpu.CompilerParams(vmem_limit_bytes=4 << 20),
        cost_estimate=pl.CostEstimate(
            flops=0, bytes_accessed=4 * rows * columns, transcendentals=0
        ),
        name="columns_step",
    )(in_hbm(whole))


def cotangent_body(token_scale, rep, values, rates, out_raw, out):
    heads = rates.shape[0] // 2
    rows, columns = out.shape
    width = columns // heads
    for h in range(heads):
        rate = -(rates[pl.ds(rep[0] * heads + h, 1), :] * token_scale)
        rate = jnp.transpose(jnp.broadcast_to(rate, (rows, rows)))[:, :1]
        part = values[:, h * width : (h + 1) * width]
        out_raw[:, h * width : (h + 1) * width] = part
        out[:, h * width : (h + 1) * width] = (rate * part.astype(jnp.float32)).astype(jnp.bfloat16)


def cotangent_step(token_scale, rep, values, rates):
    rows, columns = values.shape[0], values.shape[1] // 2
    made = jax.ShapeDtypeStruct((rows, columns), jnp.bfloat16)
    whole = pl.BlockSpec((rows, columns), lambda i, rep: (0, 0))
    return pl.pallas_call(
        functools.partial(cotangent_body, token_scale),
        out_shape=(made, made),
        grid_spec=pltpu.PrefetchScalarGridSpec(
            num_scalar_prefetch=1,
            grid=(1,),
            in_specs=[
                pl.BlockSpec((rows, columns), lambda i, rep: (0, rep[0])),
                pl.BlockSpec(rates.shape, lambda i, rep: (0, 0)),
            ],
            out_specs=(whole, whole),
        ),
        compiler_params=pltpu.CompilerParams(vmem_limit_bytes=8 << 20),
        cost_estimate=pl.CostEstimate(
            flops=2 * rows * columns, bytes_accessed=6 * rows * columns, transcendentals=0
        ),
        name="cotangent_step",
    )(rep, in_hbm(values), in_hbm(rates))


def other_body(rep, weights, momentum, low, base):
    current = weights[...]
    low[...] = current.astype(jnp.bfloat16)
    base[...] = current - momentum_decay * momentum[...]


def other_step(rep, weights, momentum):
    heads = weights.shape[0] // 2
    block = (1,) + weights.shape[1:]
    made = (heads,) + weights.shape[1:]
    taken = pl.BlockSpec(block, lambda h, rep: ((1 - rep[0]) * heads + h, 0, 0, 0))
    given = pl.BlockSpec(block, lambda h, rep: (h, 0, 0, 0))
    return pl.pallas_call(
        other_body,
        out_shape=(pltpu.HBM(made, jnp.bfloat16), pltpu.HBM(made, jnp.float32)),
        grid_spec=pltpu.PrefetchScalarGridSpec(
            num_scalar_prefetch=1,
            grid=(heads,),
            in_specs=[taken, taken],
            out_specs=(given, given),
        ),
        compiler_params=pltpu.CompilerParams(vmem_limit_bytes=12 << 20),
        cost_estimate=pl.CostEstimate(
            flops=weights.size, bytes_accessed=7 * weights.size, transcendentals=0
        ),
        name="other_step",
    )(rep, in_hbm(weights), in_hbm(momentum))


def gradient_products(unit, cot, low, hid):
    fed = lax.dot_general(low[: 4 * hid, :], unit[...], NT, preferred_element_type=jnp.float32)
    gate, upward = fed[: 2 * hid], fed[2 * hid :]
    back = lax.dot_general(low[4 * hid :, :], cot[...], NT, preferred_element_type=jnp.float32)
    sigma = jax.nn.sigmoid(gate)
    activated = gate * sigma
    hidden = (activated * upward).astype(jnp.bfloat16)
    gate_back = (back * upward * sigma * (1.0 + gate * (1.0 - sigma))).astype(jnp.bfloat16)
    up_back = (back * activated).astype(jnp.bfloat16)
    pairs = ((gate_back, unit), (up_back, unit), (hidden, cot))
    return [jnp.dot(left, right[...], preferred_element_type=jnp.float32) for left, right in pairs]


def early_body(slots, rep, *refs):
    keys, cots = refs[:slots], refs[slots : 2 * slots]
    weights, momentum, low_par, base_par, so_far, low, unit, cot = refs[2 * slots :]
    rows = keys[0].shape[0]
    hid = weights.shape[2]
    for s in range(slots):
        here = pl.ds(s * rows, rows)
        unit[here, :] = unit_rows(keys[s][...])
        cot[here, :] = cots[s][...]
    for m in range(3):
        low[pl.ds(2 * m * hid, hid), :] = weights[0, m].astype(jnp.bfloat16)
        low[pl.ds((2 * m + 1) * hid, hid), :] = low_par[0, m]
    for m, grad in enumerate(gradient_products(unit, cot, low, hid)):
        own, par = pl.ds(2 * m * hid, hid), pl.ds((2 * m + 1) * hid, hid)
        so_far[own, :] = weights[0, m] - (momentum_decay * momentum[0, m] + grad[:hid])
        so_far[par, :] = base_par[0, m] - grad[hid:]


def early_step(head, rep, keys, cots, weights, momentum, low_par, base_par):
    slots = len(keys)
    rows = keys[0].shape[0]
    heads, _, hid, width = low_par.shape
    block = (1, 3, hid, width)
    token_spec = pl.BlockSpec((rows, width), lambda i, rep: (0, head))
    own_spec = pl.BlockSpec(block, lambda i, rep: (rep[0] * heads + head, 0, 0, 0))
    par_spec = pl.BlockSpec(block, lambda i, rep: (head, 0, 0, 0))
    made_spec = pl.BlockSpec((6 * hid, width), lambda i, rep: (0, 0))
    return pl.pallas_call(
        functools.partial(early_body, slots),
        out_shape=(
            (pltpu.HBM if head else jax.ShapeDtypeStruct)((6 * hid, width), jnp.float32),
            jax.ShapeDtypeStruct((6 * hid, width), jnp.bfloat16),
        ),
        grid_spec=pltpu.PrefetchScalarGridSpec(
            num_scalar_prefetch=1,
            grid=(1,),
            in_specs=[token_spec] * (2 * slots) + [own_spec] * 2 + [par_spec] * 2,
            out_specs=(made_spec, made_spec),
            scratch_shapes=[
                pltpu.VMEM((slots * rows, width), jnp.bfloat16),
                pltpu.VMEM((slots * rows, width), jnp.bfloat16),
            ],
        ),
        compiler_params=pltpu.CompilerParams(vmem_limit_bytes=20 << 20),
        cost_estimate=pl.CostEstimate(
            flops=24 * slots * rows * hid * width,
            bytes_accessed=60 * hid * width,
            transcendentals=0,
        ),
        name="early_step",
    )(rep, *map(in_hbm, (*keys, *cots, weights, momentum)), low_par, base_par)


def last_body(rep, key, cotangent, so_far, low, *refs):
    new_own, new_par, new_low, unit = refs[-4:]
    hid = so_far.shape[0] // 6
    unit[...] = unit_rows(key[...])
    for m, grad in enumerate(gradient_products(unit, cotangent, low, hid)):
        fresh_own = so_far[pl.ds(2 * m * hid, hid), :] - grad[:hid]
        fresh_par = so_far[pl.ds((2 * m + 1) * hid, hid), :] - grad[hid:]
        new_own[0, m] = fresh_own
        new_par[0, m] = fresh_par
        new_low[pl.ds(2 * m * hid, hid), :] = fresh_own.astype(jnp.bfloat16)
        new_low[pl.ds((2 * m + 1) * hid, hid), :] = fresh_par.astype(jnp.bfloat16)


def last_step(head, heads, rep, key, cotangent, so_far, low, before):
    rows = key.shape[0]
    total, width = low.shape
    hid = total // 6
    token_spec = pl.BlockSpec((rows, width), lambda i, rep: (0, head))
    made_spec = pl.BlockSpec((total, width), lambda i, rep: (0, 0))
    block = (1, 3, hid, width)
    own_spec = pl.BlockSpec(block, lambda i, rep: (rep[0] * heads + head, 0, 0, 0))
    par_spec = pl.BlockSpec(block, lambda i, rep: (0, 0, 0, 0))
    more = () if before is None else (before,)
    return pl.pallas_call(
        last_body,
        out_shape=(
            pltpu.HBM((2 * heads, 3, hid, width), jnp.float32),
            pltpu.HBM(block, jnp.float32),
            jax.ShapeDtypeStruct((total, width), jnp.bfloat16),
        ),
        grid_spec=pltpu.PrefetchScalarGridSpec(
            num_scalar_prefetch=1,
            grid=(1,),
            in_specs=[token_spec, token_spec, made_spec, made_spec]
            + [pl.BlockSpec(memory_space=pl.ANY)] * len(more),
            out_specs=(own_spec, par_spec, made_spec),
            scratch_shapes=[pltpu.VMEM((rows, width), jnp.bfloat16)],
        ),
        input_output_aliases={5: 0} if more else {},
        compiler_params=pltpu.CompilerParams(vmem_limit_bytes=16 << 20),
        cost_estimate=pl.CostEstimate(
            flops=4 * rows * total * width, bytes_accessed=12 * total * width, transcendentals=0
        ),
        name="last_step",
    )(rep, key, cotangent, in_hbm(so_far) if head else so_far, low, *more)


def place_body(rep, block, before, out):
    out[...] = block[...]


def place_step(head, heads, rep, block, before):
    given = pl.BlockSpec(block.shape, lambda i, rep: (0, 0, 0, 0))
    taken = pl.BlockSpec(block.shape, lambda i, rep: ((1 - rep[0]) * heads + head, 0, 0, 0))
    return pl.pallas_call(
        place_body,
        out_shape=pltpu.HBM(before.shape, before.dtype),
        grid_spec=pltpu.PrefetchScalarGridSpec(
            num_scalar_prefetch=1,
            grid=(1,),
            in_specs=[given, pl.BlockSpec(memory_space=pl.ANY)],
            out_specs=taken,
        ),
        input_output_aliases={2: 0},
        compiler_params=pltpu.CompilerParams(vmem_limit_bytes=6 << 20),
        cost_estimate=pl.CostEstimate(
            flops=0, bytes_accessed=8 * block.size, transcendentals=0
        ),
        name="place_step",
    )(rep, block, before)


def join_body(made, moved, out):
    out[...] = (made[...] + moved[...].astype(jnp.float32)).astype(jnp.bfloat16)


def join_step(made, moved):
    in_vmem = pl.BlockSpec(memory_space=pltpu.VMEM)
    return pl.pallas_call(
        join_body,
        out_shape=jax.ShapeDtypeStruct(made.shape, jnp.bfloat16),
        in_specs=[in_vmem, in_vmem],
        out_specs=in_vmem,
        compiler_params=pltpu.CompilerParams(vmem_limit_bytes=2 << 20),
        cost_estimate=pl.CostEstimate(
            flops=made.size, bytes_accessed=8 * made.size, transcendentals=0
        ),
        name="join_step",
    )(made, moved)


def apply_body(query, low, out):
    hid = low.shape[0] // 6
    unit = unit_rows(query[...])
    gate = lax.dot_general(unit, low[: 2 * hid, :], NT, preferred_element_type=jnp.float32)
    upward = lax.dot_general(
        unit, low[2 * hid : 4 * hid, :], NT, preferred_element_type=jnp.float32
    )
    hidden = (gate * jax.nn.sigmoid(gate) * upward).astype(jnp.bfloat16)
    made = jnp.dot(hidden, low[4 * hid :, :], preferred_element_type=jnp.float32)
    out[...] = made.astype(out.dtype)


def apply_step(query, low, dtype):
    rows, width = query.shape
    total = low.shape[0]
    whole = pl.BlockSpec((rows, width), lambda i: (0, 0))
    return pl.pallas_call(
        apply_body,
        out_shape=jax.ShapeDtypeStruct((rows, width), dtype),
        grid=(1,),
        in_specs=[whole, pl.BlockSpec((total, width), lambda i: (0, 0))],
        out_specs=whole,
        compiler_params=pltpu.CompilerParams(vmem_limit_bytes=8 << 20),
        cost_estimate=pl.CostEstimate(
            flops=2 * rows * total * width, bytes_accessed=2 * total * width, transcendentals=0
        ),
        name="apply_step",
    )(query, low)


def output_body(kept, attended, moved, *refs):
    total = attended[...] + (kept[...] + moved[...].astype(jnp.float32))
    refs[-1][...] = total.astype(jnp.bfloat16)


def output_step(head, heads, kept, attended, moved, before):
    rows, width = kept.shape
    more = () if before is None else (before,)
    return pl.pallas_call(
        output_body,
        out_shape=pltpu.HBM((rows, heads * width), jnp.bfloat16),
        grid=(1,),
        in_specs=[pl.BlockSpec(memory_space=pltpu.VMEM)] * 3
        + [pl.BlockSpec(memory_space=pl.ANY)] * len(more),
        out_specs=pl.BlockSpec((rows, width), lambda i: (0, head)),
        input_output_aliases={3: 0} if more else {},
        compiler_params=pltpu.CompilerParams(vmem_limit_bytes=4 << 20),
        cost_estimate=pl.CostEstimate(
            flops=rows * width, bytes_accessed=8 * rows * width, transcendentals=0
        ),
        name="output_step",
    )(kept, attended, moved, *more)


def attend_body(token_scale, block_index, *refs):
    key_own, value_own, rate_prior = refs[:3]
    key_slots, cot_slots = refs[3:6], refs[6:9]
    heads = (len(refs) - 9) // 2
    asked, outs = refs[9 : 9 + heads], refs[9 + heads :]
    width = asked[0].shape[1]
    index = block_index[0]
    allowed = jnp.where(index == 0, -jnp.inf, 0.0).astype(jnp.float32)
    for h in range(heads):
        columns = slice(h * width, (h + 1) * width)
        key_prior, cot_prior = (
            jnp.where(
                index == 3,
                one[:, columns],
                jnp.where(index == 2, two[:, columns], three[:, columns]),
            )
            for one, two, three in (key_slots, cot_slots)
        )
        part = asked[h][...]
        near = lax.dot_general(part, key_own[:, columns], NT, preferred_element_type=jnp.float32)
        far = lax.dot_general(part, key_prior, NT, preferred_element_type=jnp.float32)
        near = near * width ** (-0.5)
        far = far * width ** (-0.5) + allowed
        peak = jnp.maximum(
            jnp.max(near, axis=-1, keepdims=True), jnp.max(far, axis=-1, keepdims=True)
        )
        near = jnp.exp(near - peak)
        far = jnp.exp(far - peak)
        total = jnp.sum(near, axis=-1, keepdims=True) + jnp.sum(far, axis=-1, keepdims=True)
        rate = -(rate_prior[h] * token_scale)
        near = (near / total).astype(jnp.bfloat16)
        far = (far / total / rate).astype(jnp.bfloat16)
        outs[h][...] = jnp.dot(
            near, value_own[:, columns], preferred_element_type=jnp.float32
        ) + jnp.dot(far, cot_prior, preferred_element_type=jnp.float32)


def attend_step(token_scale, block_index, keys, value_own, cots, rate_prior, asked):
    rows, columns = value_own.shape
    made = tuple(jax.ShapeDtypeStruct(query.shape, jnp.float32) for query in asked)
    return pl.pallas_call(
        functools.partial(attend_body, token_scale),
        out_shape=made,
        in_specs=[pl.BlockSpec(memory_space=pltpu.SMEM)] + [pl.BlockSpec()] * (9 + len(asked)),
        compiler_params=pltpu.CompilerParams(vmem_limit_bytes=10 << 20),
        cost_estimate=pl.CostEstimate(
            flops=8 * rows * rows * columns, bytes_accessed=20 * rows * columns, transcendentals=0
        ),
        name="attend_step",
    )(
        block_index,
        in_hbm(keys[0]),
        in_hbm(value_own),
        rate_prior,
        *map(in_hbm, (*keys[1:], *cots)),
        *asked,
    )


def tokens_travel(queries, key_vectors, values, learn_rates, fast_weights, momentum):
    width = fast_weights.shape[3]
    slots = lax.axis_size("ctx")
    per_rep = fast_weights.shape[0] // 2
    rep_index = lax.axis_index("rep")
    start = rep_index * per_rep
    token_scale = float(slots * queries.shape[0]) ** (-0.5)

    cycle = (0, 2, 3, 1)

    def hop(value, axis="ctx", order=cycle):
        if order is None or axis != "ctx":
            return ring(value, axis)
        ahead = list(zip(order, (*order[1:], order[0])))
        pairs = [(2 * source, 2 * target) for source, target in ahead]
        pairs += [(2 * target + 1, 2 * source + 1) for source, target in ahead]
        return lax.ppermute(value, ("ctx", "rep"), pairs)

    rep = rep_index.reshape(1)
    value_own, cot = cotangent_step(token_scale, rep, values, learn_rates)
    heads = range(per_rep)
    keys, cots = [columns_step(key_vectors)], [cot]
    asked = [[lax.dynamic_slice_in_dim(queries, (start + h) * width, width, 1) for h in heads]]
    for _ in range(1, slots):
        keys.append(hop(keys[-1]))
        cots.append(hop(cots[-1]))
    rate_prior = hop(
        lax.dynamic_slice_in_dim(learn_rates, start, per_rep, 0)[:, None, :], order=None
    )
    low_other, base_other = other_step(rep, fast_weights, momentum)
    low_par = hop(low_other, "rep")
    base_par = hop(base_other, "rep")
    for _ in range(1, slots):
        asked.append([hop(asked[-1][h]) for h in heads])
    block_index = lax.axis_index("ctx")
    block_index = jnp.where(rep_index == 0, block_index, (slots - block_index) % slots).reshape(1)
    attended = attend_step(
        token_scale, block_index, keys, value_own, cots[1:], rate_prior, asked[0]
    )
    early = []
    for h in heads:
        early.append(
            early_step(
                h, rep, keys[:-1], cots[:-1], fast_weights, momentum, low_par, base_par
            )
        )
    fast_updated, sent_back, lows = None, [], []
    for h in heads:
        fast_updated, for_other, low = last_step(
            h, per_rep, rep, keys[-1], cots[-1], *early[h], fast_updated
        )
        sent_back.append(for_other)
        lows.append(low)
    moving = []
    for step in range(1, slots):
        made = []
        for h in heads:
            kind = jnp.bfloat16 if step == 1 else jnp.float32
            made.append(apply_step(asked[step][h], lows[h], kind))
        if step > 1:
            made = [join_step(made[h], moving[h]) for h in heads]
        moving = [hop(made[h]) for h in heads]
    layer_output = None
    for h in heads:
        kept = apply_step(asked[0][h], lows[h], jnp.float32)
        layer_output = output_step(h, per_rep, kept, attended[h], moving[h], layer_output)
    for h in heads:
        returned = hop(sent_back[h], "rep")
        fast_updated = place_step(h, per_rep, rep, returned, fast_updated)
    return (layer_output, fast_updated)


def on_device(queries, key_vectors, values, learn_rates, fast_weights, momentum):
    slots = lax.axis_size("ctx")
    fits = (
        lax.axis_size("rep") == 2
        and slots == 4
        and fast_weights.shape[0] == 4
        and fast_weights.shape[2] % 16 == 0
        and queries.shape[0] == 128
    )
    program = tokens_travel if fits else weights_travel
    return program(queries, key_vectors, values, learn_rates, fast_weights, momentum)


def solution(mesh):
    return jax.shard_map(
        on_device,
        mesh=mesh,
        in_specs=(
            P(("groups", "ctx"), "head"),
            P(("groups", "ctx"), "head"),
            P(("groups", "ctx"), "head"),
            P("head", ("groups", "ctx")),
            P(("groups", "head"), None, ("ctx", "rep"), None),
            P(("groups", "head"), None, ("ctx", "rep"), None),
        ),
        out_specs=(
            P(("groups", "ctx"), ("head", "rep")),
            P(("groups", "head"), None, ("ctx", "rep"), None),
        ),
        check_vma=False,
    )
```
